32 devices in a mesh: grp: 2 (over y), dp: 4 (over x, core), slab: 4 (over z).
Axes of the slice: x: 2, y: 2, z: 4, core: 2. Of those that a mesh axis runs over, the one named last changes fastest.
Arguments:
- feats: bfloat16 [8, 32, 32, 128, 128], P(('grp', 'dp'), None, 'slab'), parts along dimension 0, may hold values from -6 to 6
- grains: int32 [8, 32, 128, 128], P(('grp', 'dp'), 'slab'), parts along dimension 0, may hold values from 0 to 4095
- spec_weight: bfloat16 [256, 16, 2048], P('slab'), may hold values from -0.75 to 0.75
- taps: float32 [27, 32], replicated, may hold values from -1.25 to 1.25
- point_weight: bfloat16 [32, 32], replicated, may hold values from -1 to 1
- bias: float32 [32], replicated, may hold values from -4 to 4
- cotangent: bfloat16 [8, 32, 32, 128, 128], P(('grp', 'dp'), None, 'slab'), parts along dimension 0, may hold values from -3 to 3
Outputs:
- grad_feats: bfloat16 [8, 32, 32, 128, 128], P(('grp', 'dp'), None, 'slab'), parts along dimension 0
- grad_spec: float32 [256, 32, 2048], P('slab', 'grp', 'dp'), parts along dimension 1
The draws below stay inside these ranges and needn't reach their ends.
There are 2 independent parts, one for each index of `grp`. The reference program is written for one: setup_inputs(seed, part) draws one part's arguments, and reference() takes and returns one part's arrays. A program takes and returns all parts, laid end to end along the dimension named above; an argument that names none is the same for every part. Nothing has to cross between parts.
All inputs are finite; a program needn't handle non-finite values.
Results may differ from the reference program's by a relative error of at most 0.017.
Values may be sent and summed in bfloat16 or wider, within the bound.
A program may use at most 192 MiB of HBM per device.

```python
import math
import jax
import jax.numpy as jnp
from jax import lax

C = 32
NX = 128
NY = 128
NZ = 32
KX = 16
KY = 16
KZ = 16
GRAINS = 4096
SAMPLES = 4


def draw_grains(key, part):
    key_table, key_shift_x, key_shift_y = jax.random.split(jax.random.fold_in(key, 11), 3)
    blocks_x = NX // 8 + 1
    blocks_y = NY // 8 + 1
    table = jax.random.randint(key_table, (SAMPLES, NZ, blocks_x, blocks_y), 0, GRAINS, dtype=jnp.int32)
    table = table.at[0, 0, 0, 0].set(GRAINS - 1)
    shift_x = jax.random.randint(key_shift_x, (SAMPLES, NZ, 1, NY), 0, 8, dtype=jnp.int32)
    shift_y = jax.random.randint(key_shift_y, (SAMPLES, NZ, NX, 1), 0, 8, dtype=jnp.int32)
    block_x = (jnp.arange(NX, dtype=jnp.int32)[None, None, :, None] + shift_x) // 8
    block_y = (jnp.arange(NY, dtype=jnp.int32)[None, None, None, :] + shift_y) // 8
    sample_index = jnp.arange(SAMPLES, dtype=jnp.int32)[:, None, None, None]
    plane_index = jnp.arange(NZ, dtype=jnp.int32)[None, :, None, None]
    return table[sample_index, plane_index, block_x, block_y]


def level_of(stream_key, extent, cuts, smallest, top_value):
    gain, own = 1.0, jax.random.fold_in(stream_key, 6)
    for dim, shards_of in cuts:
        draws = jnp.exp(jax.random.uniform(jax.random.fold_in(own, dim), (shards_of,), jnp.float32, smallest / len(cuts), top_value / len(cuts)))
        gain = gain * jnp.repeat(draws, extent[dim] // shards_of).reshape([-1 if axis == dim else 1 for axis in range(len(extent))])
    return gain


def centred(stream_key, dims, scale, most, cuts=(), kind=jnp.bfloat16):
    array = jax.random.normal(stream_key, dims, jnp.float32) * scale
    if len(cuts) > 0:
        array = level_of(stream_key, dims, cuts, -0.22, 0.18) * array
    return jnp.clip(array, min=-most, max=most).astype(kind)


def setup_inputs(seed: int = 0, part: int = 0) -> dict:
    seeds = jax.random.split(jax.random.key(seed), 8)
    part_splits = jax.random.split(jax.random.fold_in(seeds[7], part), 8)
    feats = centred(part_splits[0], (SAMPLES, C, NZ, NX, NY), 1.0, 6.0, ((0, 4), (2, 4)))
    grains = draw_grains(jax.random.fold_in(jax.random.fold_in(seeds[7], part), 71), part)
    spec_weight = centred(seeds[2], (KX * KY, KZ, 2 * C * C), (2 * C) ** -0.5, 0.75, ((0, 4),))
    taps = centred(seeds[3], (27, C), 27 ** -0.5, 1.25, (), jnp.float32)
    point_weight = centred(seeds[4], (C, C), C ** -0.5, 1.0)
    bias = centred(seeds[5], (C,), 1.0, 4.0, (), jnp.float32)
    cotangent = centred(part_splits[6], (SAMPLES, C, NZ, NX, NY), 0.5, 3.0, ((0, 4), (2, 4)))
    return {"feats": feats, "grains": grains, "spec_weight": spec_weight, "taps": taps, "point_weight": point_weight, "bias": bias, "cotangent": cotangent}


HIGHEST = lax.Precision.HIGHEST

def tables(count, length, start, span):
    indices = jnp.arange(count, dtype=jnp.int32)
    frequency = jnp.where(indices < count // 2, indices, length - count + indices)
    position = start + jnp.arange(span, dtype=jnp.int32)
    phases = frequency[:, None] * position[None, :] % length
    angles = phases.astype(jnp.float32) * (2.0 * math.pi / length)
    return (jnp.cos(angles), jnp.sin(angles))

def mobility(grains):
    leading = [(0, 0)] * (grains.ndim - 2)
    along_x = (grains[..., 1:, :] != grains[..., :-1, :]).astype(jnp.float32)
    along_y = (grains[..., :, 1:] != grains[..., :, :-1]).astype(jnp.float32)
    differ = jnp.pad(along_x, leading + [(1, 0), (0, 0)]) + jnp.pad(along_x, leading + [(0, 1), (0, 0)])
    differ = differ + jnp.pad(along_y, leading + [(0, 0), (1, 0)]) + jnp.pad(along_y, leading + [(0, 0), (0, 1)])
    return 0.25 * (1.0 + differ)

def stencil(padded, taps, adjoint):
    planes = padded.shape[-3] - 2
    rows_x = padded.shape[-2] - 2
    rows_y = padded.shape[-1] - 2
    total = jnp.zeros(padded.shape[:-3] + (planes, rows_x, rows_y), jnp.float32)
    for offset in range(27):
        shift_z, shift_x, shift_y = (offset // 9, offset // 3 % 3, offset % 3)
        if adjoint:
            shift_z, shift_x, shift_y = (2 - shift_z, 2 - shift_x, 2 - shift_y)
        window = padded[..., shift_z:shift_z + planes, shift_x:shift_x + rows_x, shift_y:shift_y + rows_y]
        total = total + taps[offset][:, None, None, None] * window.astype(jnp.float32)
    return total

def plane_forward(field, cos_x, sin_x, cos_y, sin_y):
    real_y = jnp.einsum('...xy,ky->...xk', field, cos_y, precision=HIGHEST)
    imag_y = -jnp.einsum('...xy,ky->...xk', field, sin_y, precision=HIGHEST)
    real_part = jnp.einsum('...xk,jx->...jk', real_y, cos_x, precision=HIGHEST) + jnp.einsum('...xk,jx->...jk', imag_y, sin_x, precision=HIGHEST)
    imag_part = jnp.einsum('...xk,jx->...jk', imag_y, cos_x, precision=HIGHEST) - jnp.einsum('...xk,jx->...jk', real_y, sin_x, precision=HIGHEST)
    return (real_part, imag_part)

def plane_inverse(real_part, imag_part, cos_x, sin_x, cos_y, sin_y):
    real_x = jnp.einsum('...jk,jx->...xk', real_part, cos_x, precision=HIGHEST) - jnp.einsum('...jk,jx->...xk', imag_part, sin_x, precision=HIGHEST)
    imag_x = jnp.einsum('...jk,jx->...xk', imag_part, cos_x, precision=HIGHEST) + jnp.einsum('...jk,jx->...xk', real_part, sin_x, precision=HIGHEST)
    return jnp.einsum('...xk,ky->...xy', real_x, cos_y, precision=HIGHEST) - jnp.einsum('...xk,ky->...xy', imag_x, sin_y, precision=HIGHEST)

def reference(feats, grains, spec_weight, taps, point_weight, bias, cotangent):
    cos_x, sin_x = tables(KX, NX, 0, NX)
    cos_y, sin_y = tables(KY, NY, 0, NY)
    cos_z, sin_z = tables(KZ, NZ, 0, NZ)
    cell_scale = math.sqrt(NX * NY * NZ)
    mode_scale = math.sqrt(KX * KY * KZ)
    weights = spec_weight.astype(jnp.float32).reshape(KX * KY, KZ, 2, C, C)
    w_real = weights[:, :, 0]
    w_imag = weights[:, :, 1]
    point_wide = point_weight.astype(jnp.float32)

    def forward_modes(field):
        real_plane, imag_plane = plane_forward(field, cos_x, sin_x, cos_y, sin_y)
        real_modes = jnp.einsum('czjk,lz->cljk', real_plane, cos_z, precision=HIGHEST) + jnp.einsum('czjk,lz->cljk', imag_plane, sin_z, precision=HIGHEST)
        imag_modes = jnp.einsum('czjk,lz->cljk', imag_plane, cos_z, precision=HIGHEST) - jnp.einsum('czjk,lz->cljk', real_plane, sin_z, precision=HIGHEST)
        real_modes = real_modes.transpose(2, 3, 1, 0).reshape(KX * KY, KZ, C)
        imag_modes = imag_modes.transpose(2, 3, 1, 0).reshape(KX * KY, KZ, C)
        return (real_modes, imag_modes)

    def inverse_modes(real_modes, imag_modes):
        real_in = real_modes.reshape(KX, KY, KZ, C).transpose(3, 2, 0, 1)
        imag_in = imag_modes.reshape(KX, KY, KZ, C).transpose(3, 2, 0, 1)
        real_plane = jnp.einsum('cljk,lz->czjk', real_in, cos_z, precision=HIGHEST) - jnp.einsum('cljk,lz->czjk', imag_in, sin_z, precision=HIGHEST)
        imag_plane = jnp.einsum('cljk,lz->czjk', imag_in, cos_z, precision=HIGHEST) + jnp.einsum('cljk,lz->czjk', real_in, sin_z, precision=HIGHEST)
        return plane_inverse(real_plane, imag_plane, cos_x, sin_x, cos_y, sin_y)

    def one_sample(carry, inputs):
        field, sample_grains, sample_cotangent = inputs
        moving = mobility(sample_grains)[None]
        padded = jnp.pad(field, ((0, 0), (1, 1), (1, 1), (1, 1)))
        smooth = stencil(padded, taps, False).astype(jnp.bfloat16)
        local_part = moving * jnp.einsum('czxy,co->ozxy', smooth.astype(jnp.float32), point_wide, precision=HIGHEST)
        spec_real, spec_imag = forward_modes(field.astype(jnp.float32))
        spec_real = spec_real / cell_scale
        spec_imag = spec_imag / cell_scale
        mixed_real = jnp.einsum('pkc,pkco->pko', spec_real, w_real, precision=HIGHEST) - jnp.einsum('pkc,pkco->pko', spec_imag, w_imag, precision=HIGHEST)
        mixed_imag = jnp.einsum('pkc,pkco->pko', spec_real, w_imag, precision=HIGHEST) + jnp.einsum('pkc,pkco->pko', spec_imag, w_real, precision=HIGHEST)
        spectral = inverse_modes(mixed_real, mixed_imag) / mode_scale
        pre = spectral + local_part + bias[:, None, None, None]
        gate = jax.nn.sigmoid(pre)
        delta = (sample_cotangent.astype(jnp.float32) * gate * (1.0 + pre * (1.0 - gate))).astype(jnp.bfloat16)
        dual_real, dual_imag = forward_modes(delta.astype(jnp.float32))
        dual_real = dual_real / mode_scale
        dual_imag = dual_imag / mode_scale
        grad_real = jnp.einsum('pkc,pko->pkco', spec_real, dual_real, precision=HIGHEST) + jnp.einsum('pkc,pko->pkco', spec_imag, dual_imag, precision=HIGHEST)
        grad_imag = jnp.einsum('pkc,pko->pkco', spec_real, dual_imag, precision=HIGHEST) - jnp.einsum('pkc,pko->pkco', spec_imag, dual_real, precision=HIGHEST)
        back_real = jnp.einsum('pko,pkco->pkc', dual_real, w_real, precision=HIGHEST) + jnp.einsum('pko,pkco->pkc', dual_imag, w_imag, precision=HIGHEST)
        back_imag = jnp.einsum('pko,pkco->pkc', dual_imag, w_real, precision=HIGHEST) - jnp.einsum('pko,pkco->pkc', dual_real, w_imag, precision=HIGHEST)
        spectral_back = inverse_modes(back_real, back_imag) / cell_scale
        spread = (moving * jnp.einsum('ozxy,co->czxy', delta.astype(jnp.float32), point_wide, precision=HIGHEST)).astype(jnp.bfloat16)
        local_back = stencil(jnp.pad(spread, ((0, 0), (1, 1), (1, 1), (1, 1))), taps, True)
        grad_field = (spectral_back + local_back).astype(jnp.bfloat16)
        carry = carry + jnp.stack([grad_real, grad_imag], axis=2)
        return (carry, grad_field)
    start = jnp.zeros((KX * KY, KZ, 2, C, C), jnp.float32)
    summed, grad_feats = lax.scan(one_sample, start, (feats, grains, cotangent))
    grad_spec = (summed / SAMPLES).reshape(KX * KY, KZ, 2 * C * C)
    return (grad_feats, grad_spec)
```

```python
import functools
import math

import jax
import jax.numpy as jnp
import numpy as np
from jax import lax
from jax.experimental import pallas as pl
from jax.experimental.pallas import tpu as pltpu
from jax.sharding import PartitionSpec as P

NX = 128
NY = 128
NZ = 32
KX = 16
KY = 16
KZ = 16
F32 = jnp.float32
BF16 = jnp.bfloat16
HIGHEST = lax.Precision.HIGHEST
MIB = 1 << 20


def waves(count, length):
    index = np.arange(count)
    frequency = np.where(index < count // 2, index, length - count + index)
    phases = frequency[:, None] * np.arange(length)[None, :] % length
    angles = phases * (2.0 * math.pi / length)
    return np.cos(angles), np.sin(angles)


class Plan:
    def __init__(self, planes, slabs):
        self.planes = planes
        self.slabs = slabs
        rows = KX * KY // slabs
        self.rows = rows
        self.groups = slabs if rows >= KY else KX
        self.jl = KX // self.groups
        self.kq = slabs // self.groups
        self.kk = KY // self.kq
        self.width = max(128, planes * KY)
        self.used = planes * KY
        self.pk = planes * self.kk
        self.lanes = self.kk * KZ
        self.lead = self.groups if (2 * self.jl) % 8 == 0 else 1
        width, jl = self.width, self.jl
        cos_x, sin_x = waves(KX, NX)
        cos_y, sin_y = waves(KY, NY)
        cos_z, sin_z = waves(KZ, NZ)
        forward = np.zeros((planes, NY, 2, width))
        for z in range(planes):
            forward[z, :, 0, z * KY : (z + 1) * KY] = cos_y.T
            forward[z, :, 1, z * KY : (z + 1) * KY] = -sin_y.T
        forward = forward.reshape(planes * NY, 2 * width)
        self.y_forward = forward
        self.y_inverse = forward.T
        table = np.zeros((self.groups, 2, jl, 2, NX))
        back = np.zeros((2, NX, self.groups, 2, jl))
        for j in range(KX):
            g, i = divmod(j, jl)
            table[g, 0, i, 0], table[g, 0, i, 1] = cos_x[j], sin_x[j]
            table[g, 1, i, 1], table[g, 1, i, 0] = cos_x[j], -sin_x[j]
            back[0, :, g, 0, i], back[0, :, g, 1, i] = cos_x[j], -sin_x[j]
            back[1, :, g, 1, i], back[1, :, g, 0, i] = cos_x[j], sin_x[j]
        self.x_forward = table.reshape(2 * KX, 2 * NX)
        self.x_inverse = back.reshape(2 * NX, 2 * KX)
        kk, pk, lanes = self.kk, self.pk, self.lanes
        zf = np.zeros((slabs, planes, kk, 2, kk, KZ))
        self.pw = max(128, pk)
        zi = np.zeros((slabs, 2, kk, KZ, 2, planes, kk))
        for s in range(slabs):
            for z in range(planes):
                c, n = cos_z[:, s * planes + z], sin_z[:, s * planes + z]
                for k in range(kk):
                    zf[s, z, k, 0, k], zf[s, z, k, 1, k] = c, n
                    zi[s, 0, k, :, 0, z, k], zi[s, 1, k, :, 0, z, k] = c, -n
                    zi[s, 1, k, :, 1, z, k], zi[s, 0, k, :, 1, z, k] = c, n
        self.z_forward = zf.reshape(slabs, pk, 2 * lanes)
        zi = zi.reshape(slabs, 2 * lanes, 2, pk)
        zi = np.pad(zi, ((0, 0), (0, 0), (0, 0), (0, self.pw - pk)))
        self.z_inverse = zi.reshape(slabs, 2 * lanes, 2 * self.pw)


def whole(shape):
    zeros = (0,) * len(shape)
    return pl.BlockSpec(shape, lambda *_: zeros)


def params(mib):
    return pltpu.CompilerParams(vmem_limit_bytes=mib * MIB)


def dot(a, b, **kw):
    return jnp.dot(a, b, preferred_element_type=F32, **kw)


def channel_modes(plan, planes_of, ty, tx):
    field = jnp.concatenate([planes_of(z) for z in range(plan.planes)], axis=1)
    along = dot(field, ty).astype(BF16)
    stacked = jnp.concatenate([along[:, : plan.width], along[:, plan.width :]], axis=0)
    return dot(tx, stacked)


def put_modes(plan, out_ref, c, value):
    if plan.lead == 1:
        out_ref[0, c] = value.astype(BF16)
    else:
        step = 2 * KX // plan.lead
        for g in range(plan.lead):
            out_ref[g, c] = value[g * step : (g + 1) * step].astype(BF16)


def get_modes(plan, ref, c):
    if plan.lead == 1:
        return ref[0, c]
    parts = [ref[g, c].astype(F32) for g in range(plan.lead)]
    return jnp.concatenate(parts, axis=0).astype(BF16)


def planes_kernel(plan, batch, x_ref, ty_ref, tx_ref, out_ref):
    for c in range(batch):
        value = channel_modes(plan, lambda z: x_ref[c, z], ty_ref[...], tx_ref[...])
        put_modes(plan, out_ref, c, value)


def planes_call(plan, field, ty, tx):
    channels, planes = field.shape[:2]
    batch = 4
    step = 2 * KX // plan.lead
    return pl.pallas_call(
        functools.partial(planes_kernel, plan, batch),
        grid=(channels // batch,),
        in_specs=[
            pl.BlockSpec((batch, planes, NX, NY), lambda i: (i, 0, 0, 0)),
            whole(ty.shape),
            whole(tx.shape),
        ],
        out_specs=pl.BlockSpec((plan.lead, batch, step, plan.width), lambda i: (0, i, 0, 0)),
        out_shape=jax.ShapeDtypeStruct((plan.lead, channels, step, plan.width), BF16),
        compiler_params=params(60),
        cost_estimate=pl.CostEstimate(
            flops=2 * channels * NX * planes * NY * 256, bytes_accessed=field.size * 2, transcendentals=0
        ),
        name="plane_modes",
    )(field, ty, tx)


def rims_kernel(low_ref, high_ref, first_ref, last_ref):
    first_ref[...] = low_ref[:, 0]
    last_ref[...] = high_ref[:, 0]


def rims_call(field):
    channels, planes = field.shape[:2]
    batch = 8
    rim = pl.BlockSpec((batch, NX, NY), lambda i: (i, 0, 0))
    shape = jax.ShapeDtypeStruct((channels, NX, NY), field.dtype)
    return pl.pallas_call(
        rims_kernel,
        grid=(channels // batch,),
        in_specs=[
            pl.BlockSpec((batch, 1, NX, NY), lambda i: (i, 0, 0, 0)),
            pl.BlockSpec((batch, 1, NX, NY), lambda i: (i, planes - 1, 0, 0)),
        ],
        out_specs=[rim, rim],
        out_shape=[shape, shape],
        compiler_params=params(60),
        name="rims",
    )(field, field)


def bands(taps_ref, c, adjoint, group, band_ref):
    row = lax.broadcasted_iota(jnp.int32, (NY, NY), 0)
    col = lax.broadcasted_iota(jnp.int32, (NY, NY), 1)
    diff = row - col
    for dz in range(3):
        for dx in range(3):
            base = 9 * dz + 3 * dx
            t = [taps_ref[base + i, c] for i in range(3)]
            if adjoint:
                t = t[::-1]
            band = jnp.where(
                diff == 0,
                t[1],
                jnp.where(diff == 1, t[2], jnp.where(diff == -1, t[0], 0.0)),
            ).astype(BF16)
            zi, xi = (2 - dz, 2 - dx) if adjoint else (dz, dx)
            for z in range(group):
                top = (xi * (group + 2) + z + zi) * NY
                band_ref[top : top + NY, z * NY : (z + 1) * NY] = band


def shifted(plan, x_ref, before_ref, after_ref, c, rows_ref):
    edge = lax.broadcasted_iota(jnp.int32, (NX, NY), 0)
    for i in range(plan.planes + 2):
        if before_ref is None and i in (0, plan.planes + 1):
            continue
        if i == 0:
            plane = before_ref[c]
        elif i == plan.planes + 1:
            plane = after_ref[c]
        else:
            plane = x_ref[c, i - 1]
        wide = plane.astype(F32)
        lower = jnp.where(edge == 0, 0.0, pltpu.roll(wide, 1, 0))
        upper = jnp.where(edge == NX - 1, 0.0, pltpu.roll(wide, NX - 1, 0))
        cols = slice(i * NY, (i + 1) * NY)
        rows_ref[0, :, cols] = lower.astype(BF16)
        rows_ref[1, :, cols] = plane
        rows_ref[2, :, cols] = upper.astype(BF16)


def stencil_kernel(plan, batch, adjoint, group, offset, *refs):
    if offset:
        refs = refs[1:]
    if adjoint:
        taps_ref, x_ref, out_ref, band_ref, rows_ref = refs
        before_ref = after_ref = None
    else:
        taps_ref, x_ref, before_ref, after_ref, out_ref, band_ref, rows_ref = refs

    @pl.when(pl.program_id(0) == 0)
    def _():
        band_ref[...] = jnp.zeros_like(band_ref)
        rows_ref[...] = jnp.zeros_like(rows_ref)

    first = pl.program_id(0) * batch + offset
    for c in range(batch):
        half = c % 2
        band, rows = band_ref.at[half], rows_ref.at[half]
        bands(taps_ref, first + c, adjoint, group, band)
        shifted(plan, x_ref, before_ref, after_ref, c, rows)
        for z in range(0, plan.planes, group):
            cols = slice(z * NY, (z + group + 2) * NY)
            near = jnp.concatenate([rows[d, :, cols] for d in range(3)], axis=1)
            total = dot(near, band[...])
            for i in range(group):
                out_ref[c, z + i] = total[:, i * NY : (i + 1) * NY].astype(BF16)


def stencil_call(plan, taps, field, rims, adjoint, done=None):
    channels, planes = field.shape[:2]
    batch = 4
    group = 2 if planes % 2 == 0 else 1
    offset = 0 if done is None else channels // 2
    skip = offset // batch
    block = pl.BlockSpec((batch, planes, NX, NY), lambda i: (i + skip, 0, 0, 0))
    specs = [pl.BlockSpec(memory_space=pltpu.SMEM), block]
    specs += [pl.BlockSpec((batch, NX, NY), lambda i: (i + skip, 0, 0))] * len(rims)
    operands = (taps, field, *rims)
    if done is not None:
        specs = [pl.BlockSpec(memory_space=pl.ANY)] + specs
        operands = (done,) + operands
    return pl.pallas_call(
        functools.partial(stencil_kernel, plan, batch, adjoint, group, offset),
        grid=(channels // 2 // batch,),
        in_specs=specs,
        out_specs=block,
        out_shape=jax.ShapeDtypeStruct(field.shape, BF16),
        input_output_aliases={} if done is None else {0: 0},
        scratch_shapes=[
            pltpu.VMEM((2, 3 * (group + 2) * NY, group * NY), BF16),
            pltpu.VMEM((2, 3, NX, (planes + 2) * NY), BF16),
        ],
        compiler_params=params(60),
        cost_estimate=pl.CostEstimate(
            flops=field.size * 3 * (group + 2) * NY, bytes_accessed=field.size * 2, transcendentals=0
        ),
        name="stencil_back" if adjoint else "stencil",
    )(*operands)


def final_kernel(plan, batch, taps_ref, x_ref, before_ref, after_ref, m_ref, tx_ref, ty_ref, out_ref):
    first = pl.program_id(0) * batch
    edge = lax.broadcasted_iota(jnp.int32, (NX, NY), 0)
    diff = lax.broadcasted_iota(jnp.int32, (NY, NY), 0) - lax.broadcasted_iota(jnp.int32, (NY, NY), 1)

    def rim(c, plane, dz):
        wide = plane.astype(F32)
        lower = jnp.where(edge == 0, 0.0, pltpu.roll(wide, 1, 0)).astype(BF16)
        upper = jnp.where(edge == NX - 1, 0.0, pltpu.roll(wide, NX - 1, 0)).astype(BF16)
        band = []
        for dx in (2, 1, 0):
            t = [taps_ref[9 * dz + 3 * dx + i, first + c] for i in range(3)]
            band.append(jnp.where(
                diff == 0,
                t[1],
                jnp.where(diff == 1, t[0], jnp.where(diff == -1, t[2], 0.0)),
            ).astype(BF16))
        return dot(jnp.concatenate([lower, plane, upper], axis=1), jnp.concatenate(band, axis=0))

    for c in range(batch):
        wave = dot(tx_ref[...], get_modes(plan, m_ref, c)).astype(BF16)
        wave = jnp.concatenate([wave[:NX], wave[NX:]], axis=1)
        full = dot(wave, ty_ref[...])
        for z in range(plan.planes):
            total = full[:, z * NY : (z + 1) * NY] + x_ref[c, z].astype(F32)
            if z == 0:
                total = total + rim(c, before_ref[c], 2)
            if z == plan.planes - 1:
                total = total + rim(c, after_ref[c], 0)
            out_ref[c, z] = total.astype(BF16)


def final_call(plan, taps, partial, before, after, modes, tx, ty):
    channels, planes = partial.shape[:2]
    batch = 4
    block = pl.BlockSpec((batch, planes, NX, NY), lambda i: (i, 0, 0, 0))
    rim = pl.BlockSpec((batch, NX, NY), lambda i: (i, 0, 0))
    return pl.pallas_call(
        functools.partial(final_kernel, plan, batch),
        grid=(channels // batch,),
        in_specs=[
            pl.BlockSpec(memory_space=pltpu.SMEM),
            block,
            rim,
            rim,
            pl.BlockSpec((modes.shape[0], batch) + modes.shape[2:], lambda i: (0, i, 0, 0)),
            whole(tx.shape),
            whole(ty.shape),
        ],
        out_specs=block,
        out_shape=jax.ShapeDtypeStruct(partial.shape, BF16),
        compiler_params=params(60),
        cost_estimate=pl.CostEstimate(
            flops=2 * partial.size * 512, bytes_accessed=partial.size * 4, transcendentals=0
        ),
        name="final",
    )(taps, partial, before, after, modes, tx, ty)


def mix_kernel(plan, channels, adjoint, scale_in, scale_out, r_ref, zf_ref, zi_ref, w_ref,
               out_ref, turned_ref, z_scr, s_scr, m_scr, o_scr):
    jl, lanes, pk, pw = plan.jl, plan.lanes, plan.pk, plan.pw
    chunks = 2 * lanes // 128
    total = None
    for s in range(plan.slabs):
        part = dot(r_ref[s].astype(F32), zf_ref[s], precision=HIGHEST)
        total = part if total is None else total + part
    total = total * scale_in
    for q in range(chunks):
        z_scr[q] = total[:, q * 128 : (q + 1) * 128]

    def rows_of(start):
        return jnp.concatenate(
            [z_scr[q, pl.ds(start, channels, stride=2 * jl), :] for q in range(chunks)], axis=1)

    for j in range(jl):
        re, im = rows_of(j), rows_of(jl + j)
        real = re[:, :lanes] + im[:, lanes:]
        imag = im[:, :lanes] - re[:, lanes:]
        s_scr[j, 0] = real
        s_scr[j, 1] = imag
        both = jnp.concatenate([real, imag], axis=0)
        turned_ref[j * lanes : (j + 1) * lanes, :] = both.T.astype(BF16)
        cols = slice(j * lanes, (j + 1) * lanes)
        rows = slice(j * channels, (j + 1) * channels)
        if adjoint:
            for c in range(channels):
                wr = w_ref[0, c, :, cols].astype(F32)
                wi = w_ref[1, c, :, cols].astype(F32)
                br = jnp.sum(wr * real + wi * imag, axis=0, keepdims=True)
                bi = jnp.sum(wr * imag - wi * real, axis=0, keepdims=True)
                m_scr[j * channels + c : j * channels + c + 1, :lanes] = br
                m_scr[j * channels + c : j * channels + c + 1, lanes:] = bi
        else:
            mr = jnp.zeros((channels, lanes), F32)
            mi = jnp.zeros((channels, lanes), F32)
            for c in range(channels):
                wr = w_ref[0, c, :, cols].astype(F32)
                wi = w_ref[1, c, :, cols].astype(F32)
                sr = s_scr[j, 0, c : c + 1, :]
                si = s_scr[j, 1, c : c + 1, :]
                mr = mr + (sr * wr - si * wi)
                mi = mi + (sr * wi + si * wr)
            m_scr[rows, :lanes] = mr
            m_scr[rows, lanes:] = mi
    mixed = m_scr[...] * scale_out
    for s in range(plan.slabs):
        planar = dot(mixed, zi_ref[s], precision=HIGHEST)
        for j in range(jl):
            for part in range(2):
                o_scr[pl.ds(part * jl + j, channels, stride=2 * jl), :] = planar[
                    j * channels : (j + 1) * channels, part * pw : (part + 1) * pw
                ]
        out_ref[s] = o_scr[:, :pk].astype(BF16)


def mix_call(plan, received, weights, zf, zi, adjoint, scale_in, scale_out):
    channels = weights.shape[1]
    rows = channels * 2 * plan.jl
    modes = plan.jl * plan.lanes
    return pl.pallas_call(
        functools.partial(mix_kernel, plan, channels, adjoint, scale_in, scale_out),
        out_shape=(
            jax.ShapeDtypeStruct((plan.slabs, rows, plan.pk), BF16),
            jax.ShapeDtypeStruct((modes, 2 * channels), BF16),
        ),
        scratch_shapes=[
            pltpu.VMEM((2 * plan.lanes // 128, rows, 128), F32),
            pltpu.VMEM((plan.jl, 2, channels, plan.lanes), F32),
            pltpu.VMEM((plan.jl * channels, 2 * plan.lanes), F32),
            pltpu.VMEM((rows, plan.pw), F32),
        ],
        compiler_params=params(60),
        name="mix_back" if adjoint else "mix",
    )(received, zf, zi, weights)


def middle_kernel(plan, channels, g_ref, sm_ref, cot_ref, m_ref, bias_ref, pw_ref, pt_ref,
                  txi_ref, tyi_ref, ty_ref, tx_ref,
                  spread_ref, first_ref, last_ref, modes_ref, wave_scr, delta_scr, move_scr, kp_ref, kt_ref):
    z = pl.program_id(0)
    planes = plan.planes
    width = plan.width

    @pl.when(z == 0)
    def _():
        def body(c, carry):
            wave = dot(txi_ref[...], get_modes(plan, m_ref, c)).astype(BF16)
            wave_scr[c, :, :width] = wave[:NX]
            wave_scr[c, :, width:] = wave[NX:]
            return carry
        lax.fori_loop(0, channels, body, 0, unroll=4)
        rows = channels * 16
        pick = lax.broadcasted_iota(jnp.int32, (rows, channels), 0) >> 4
        pick = pick == lax.broadcasted_iota(jnp.int32, (rows, channels), 1)
        pick = jnp.where(pick, 1.0, 0.0).astype(BF16)
        same = lax.broadcasted_iota(jnp.int32, (rows, rows), 0) & 15
        same = same == (lax.broadcasted_iota(jnp.int32, (rows, rows), 1) & 15)
        for src, dst in ((pt_ref, kp_ref), (pw_ref, kt_ref)):
            tall = dot(pick, src[...]).astype(BF16)
            full = lax.dot_general(tall, pick, (((1,), (1,)), ((), ())), preferred_element_type=F32)
            dst[...] = jnp.where(same, full, 0.0).astype(BF16)

    g = g_ref[0]
    row = lax.broadcasted_iota(jnp.int32, (NX, NY), 0)
    col = lax.broadcasted_iota(jnp.int32, (NX, NY), 1)

    def differs(shift, axis, inside):
        return jnp.where((g != pltpu.roll(g, shift, axis)) & inside, 0.25, 0.0)

    move_scr[...] = (
        0.25
        + differs(1, 0, row > 0)
        + differs(NX - 1, 0, row < NX - 1)
        + differs(1, 1, col > 0)
        + differs(NY - 1, 1, col < NY - 1)
    )
    height = channels * 16
    bias = bias_ref[...]

    def body(pair, carry):
        starts = [pair * 32 + 16 * i for i in range(2)]

        def tile(ref):
            return [ref[:, 0, pl.ds(x, 16), :].reshape(height, NY) for x in starts]

        mixed = dot(kp_ref[...], jnp.concatenate(tile(sm_ref), axis=1))
        cot = tile(cot_ref)
        deltas = []
        for i, x in enumerate(starts):
            moving = move_scr[pl.ds(x, 16), :]
            wave = wave_scr[:, pl.ds(x, 16), :].reshape(height, 2 * width)
            spectral = dot(wave, tyi_ref[...])
            local = mixed[:, i * NY : (i + 1) * NY].reshape(channels, 16, NY) * moving[None]
            pre = spectral.reshape(channels, 16, NY) + local + bias
            gate = 0.5 + 0.5 * jnp.tanh(0.5 * pre)
            delta = cot[i].astype(F32).reshape(channels, 16, NY) * gate * (1.0 + pre * (1.0 - gate))
            delta = delta.astype(BF16)
            delta_scr[:, z, pl.ds(x, 16), :] = delta
            deltas.append(delta.reshape(height, NY))
        turned = dot(kt_ref[...], jnp.concatenate(deltas, axis=1))
        for i, x in enumerate(starts):
            moving = move_scr[pl.ds(x, 16), :]
            value = turned[:, i * NY : (i + 1) * NY].reshape(channels, 16, NY) * moving[None]
            spread_ref[:, 0, pl.ds(x, 16), :] = value.astype(BF16)
        return carry

    for pair in range(NX // 32):
        body(pair, 0)

    @pl.when(z == 0)
    def _():
        first_ref[...] = spread_ref[:, 0]

    @pl.when(z == planes - 1)
    def _():
        last_ref[...] = spread_ref[:, 0]

        def body(i, carry):
            for c in (2 * i, 2 * i + 1):
                value = channel_modes(plan, lambda p: delta_scr[c, p], ty_ref[...], tx_ref[...])
                put_modes(plan, modes_ref, c, value)
            return carry

        lax.fori_loop(0, channels // 2, body, 0)


def middle_call(plan, grains, smooth, cotangent, modes, bias, kp, kt, txi, tyi, ty, tx):
    channels, planes = smooth.shape[:2]
    width = plan.width
    block = pl.BlockSpec((channels, 1, NX, NY), lambda z: (0, z, 0, 0))
    rim = jax.ShapeDtypeStruct((channels, NX, NY), BF16)
    return pl.pallas_call(
        functools.partial(middle_kernel, plan, channels),
        grid=(planes,),
        in_specs=[
            pl.BlockSpec((1, NX, NY), lambda z: (z, 0, 0)),
            block,
            block,
            whole(modes.shape),
            whole((channels, 1, 1)),
            whole(kp.shape),
            whole(kt.shape),
            whole(txi.shape),
            pl.BlockSpec((2 * width, NY), lambda z: (0, z)),
            whole(ty.shape),
            whole(tx.shape),
        ],
        out_specs=[block, whole(rim.shape), whole(rim.shape), whole(modes.shape)],
        out_shape=[jax.ShapeDtypeStruct(smooth.shape, BF16), rim, rim,
                   jax.ShapeDtypeStruct(modes.shape, BF16)],
        scratch_shapes=[
            pltpu.VMEM((channels, NX, 2 * width), BF16),
            pltpu.VMEM((channels, planes, NX, NY), BF16),
            pltpu.VMEM((NX, NY), F32),
            pltpu.VMEM((16 * channels, 16 * channels), BF16),
            pltpu.VMEM((16 * channels, 16 * channels), BF16),
        ],
        compiler_params=params(60),
        name="middle",
    )(grains, smooth, cotangent, modes, bias.reshape(channels, 1, 1), kp, kt, txi, tyi, ty, tx)


def grad_kernel(samples, both_ref, e_ref, out_ref):
    total = None
    for i in range(samples):
        half = both_ref.shape[-1] // 2
        spec, dual = both_ref[i, :, :half], both_ref[i, :, half:]
        term = dot(spec, e_ref[0]) * dot(dual, e_ref[1]) + dot(spec, e_ref[2]) * dot(dual, e_ref[3])
        total = term if total is None else total + term
    out_ref[...] = total


def grad_call(both, pick):
    samples, modes, width = both.shape
    columns = pick.shape[-1]
    batch = min(256, modes)
    return pl.pallas_call(
        functools.partial(grad_kernel, samples),
        grid=(modes // batch,),
        in_specs=[
            pl.BlockSpec((samples, batch, width), lambda i: (0, i, 0)),
            whole(pick.shape),
        ],
        out_specs=pl.BlockSpec((batch, columns), lambda i: (i, 0)),
        out_shape=jax.ShapeDtypeStruct((modes, columns), F32),
        compiler_params=params(60),
        cost_estimate=pl.CostEstimate(
            flops=8 * samples * modes * width * columns, bytes_accessed=modes * columns * 4, transcendentals=0
        ),
        name="grad_modes",
    )(both, pick)


def slab_peer(me, d, slabs):
    return lax.rem(me + d, slabs)


def slab_barrier(me, slabs):
    barrier = pltpu.get_barrier_semaphore()
    for d in range(1, slabs):
        pl.semaphore_signal(
            barrier, inc=1, device_id={"slab": slab_peer(me, d, slabs)}, device_id_type=pl.DeviceIdType.MESH)
    pl.semaphore_wait(barrier, slabs - 1)


def exchange(me, slabs, send_ref, recv_ref, send_sem, recv_sem):
    copies = []
    for d in range(1, slabs):
        peer = slab_peer(me, d, slabs)
        copies.append(pltpu.make_async_remote_copy(
            src_ref=send_ref.at[peer],
            dst_ref=recv_ref.at[me],
            send_sem=send_sem.at[d - 1],
            recv_sem=recv_sem.at[d - 1],
            device_id={"slab": peer},
            device_id_type=pl.DeviceIdType.MESH,
        ))
    return copies


def halo_copies(me, slabs, field_ref, before_ref, after_ref, planes, chunk, index, send_sem, recv_sem):
    rows = pl.ds(index * chunk, chunk)
    up = pltpu.make_async_remote_copy(
        src_ref=field_ref.at[rows, planes - 1],
        dst_ref=before_ref.at[rows],
        send_sem=send_sem.at[0, index],
        recv_sem=recv_sem.at[0, index],
        device_id={"slab": lax.rem(me + 1, slabs)},
        device_id_type=pl.DeviceIdType.MESH,
    )
    down = pltpu.make_async_remote_copy(
        src_ref=field_ref.at[rows, 0],
        dst_ref=after_ref.at[rows],
        send_sem=send_sem.at[1, index],
        recv_sem=recv_sem.at[1, index],
        device_id={"slab": lax.rem(me + slabs - 1, slabs)},
        device_id_type=pl.DeviceIdType.MESH,
    )
    return up, down


def halo_start(me, slabs, copies):
    up, down = copies

    @pl.when(me < slabs - 1)
    def _():
        up.start()

    @pl.when(me > 0)
    def _():
        down.start()


def halo_wait_recv(me, slabs, copies):
    up, down = copies

    @pl.when(me > 0)
    def _():
        up.wait_recv()

    @pl.when(me < slabs - 1)
    def _():
        down.wait_recv()


def halo_wait_send(me, slabs, copies):
    up, down = copies

    @pl.when(me < slabs - 1)
    def _():
        up.wait_send()

    @pl.when(me > 0)
    def _():
        down.wait_send()


def batch_modes(plan, out_ref, row, lines, ty_ref, tx_ref):
    count = len(lines)
    along = dot(jnp.concatenate(lines, axis=0), ty_ref[...]).astype(BF16)
    width = plan.width
    values = []
    for c in range(0, count, 2):
        top = along[c * NX : (c + 1) * NX]
        low = along[(c + 1) * NX : (c + 2) * NX]
        pair = jnp.concatenate([
            jnp.concatenate([top[:, :width], low[:, :width]], axis=1),
            jnp.concatenate([top[:, width:], low[:, width:]], axis=1),
        ], axis=0)
        both = dot(tx_ref[...], pair)
        values += [both[:, :width], both[:, width:]]
    step = 2 * KX // plan.lead
    for g in range(plan.lead):
        part = jnp.concatenate([v[g * step : (g + 1) * step] for v in values], axis=0)
        out_ref[g, pl.ds(row, count * step), :] = part.astype(BF16)


def band_masks():
    diff = lax.broadcasted_iota(jnp.int32, (NY, NY), 0) - lax.broadcasted_iota(jnp.int32, (NY, NY), 1)
    return diff == 1, diff == 0, diff == -1


def fill_band(taps_ref, c, adjoint, masks, band_ref):
    low, mid, upp = masks
    for dz in range(3):
        for dx in range(3):
            base = 9 * dz + 3 * dx
            t = [taps_ref[base + i, c] for i in range(3)]
            if adjoint:
                t = t[::-1]
            band = jnp.where(mid, t[1], jnp.where(low, t[2], jnp.where(upp, t[0], 0.0))).astype(BF16)
            zi, xi = (2 - dz, 2 - dx) if adjoint else (dz, dx)
            for z in range(2):
                top = (xi * 4 + z + zi) * NY
                band_ref[top : top + NY, z * NY : (z + 1) * NY] = band


def stencil_part(plan, taps_ref, x_ref, before_ref, after_ref, c, groups, adjoint, masks, out_ref,
                 band_ref, wide_ref, lower_ref, upper_ref):
    fill_band(taps_ref, c, adjoint, masks, band_ref)
    planes = plan.planes

    def plane(i):
        if i == 0:
            return before_ref[c]
        if i == planes + 1:
            return after_ref[c]
        return x_ref[c, i - 1]

    needed = sorted({2 * g + i for g in groups for i in range(4)})
    slot = {i: n for n, i in enumerate(needed)}
    for i in needed:
        n = slot[i]
        wide_ref[n, 8 : NX + 8, :] = plane(i).astype(F32)
        lower_ref[n] = wide_ref[n, 7 : NX + 7, :].astype(BF16)
        upper_ref[n] = wide_ref[n, 9 : NX + 9, :].astype(BF16)

    def moved(dx, i):
        if dx == 1:
            return plane(i)
        return (lower_ref if dx == 0 else upper_ref)[slot[i]]

    near = jnp.concatenate([
        jnp.concatenate([moved(dx, 2 * g + i) for dx in range(3) for i in range(4)], axis=1)
        for g in groups
    ], axis=0)
    total = dot(near, band_ref[...])
    for n, g in enumerate(groups):
        for i in range(2):
            out_ref[c, 2 * g + i] = total[n * NX : (n + 1) * NX, i * NY : (i + 1) * NY].astype(BF16)


def mix_modes(plan, channels, me, adjoint, scale_in, scale_out, own_ref, r_ref, zf_ref, zi_ref, w_ref,
              out_ref, turned_ref, z_scr, s_scr, m_scr, o_scr):
    jl, lanes, pk, pw = plan.jl, plan.lanes, plan.pk, plan.pw
    chunks = 2 * lanes // 128
    r_ref[me] = own_ref[me]
    total = dot(jnp.concatenate([r_ref[s] for s in range(plan.slabs)], axis=1), zf_ref[...])
    total = total * scale_in
    for q in range(chunks):
        z_scr[q] = total[:, q * 128 : (q + 1) * 128]

    def rows_of(start):
        return jnp.concatenate(
            [z_scr[q, pl.ds(start, channels, stride=2 * jl), :] for q in range(chunks)], axis=1)

    for j in range(jl):
        re, im = rows_of(j), rows_of(jl + j)
        real = re[:, :lanes] + im[:, lanes:]
        imag = im[:, :lanes] - re[:, lanes:]
        s_scr[j, 0] = real
        s_scr[j, 1] = imag
        both = jnp.concatenate([real, imag], axis=0)
        turned_ref[j * lanes : (j + 1) * lanes, :] = both.T.astype(BF16)
        cols = slice(j * lanes, (j + 1) * lanes)
        rows = slice(j * channels, (j + 1) * channels)
        if adjoint:
            def body(i, carry):
                parts = []
                for k in range(8):
                    c = 8 * i + k
                    wr = w_ref[0, c, :, cols].astype(F32)
                    wi = w_ref[1, c, :, cols].astype(F32)
                    real, imag = s_scr[j, 0], s_scr[j, 1]
                    br = jnp.sum(wr * real + wi * imag, axis=0, keepdims=True)
                    bi = jnp.sum(wr * imag - wi * real, axis=0, keepdims=True)
                    parts.append(jnp.concatenate([br, bi], axis=1))
                m_scr[pl.ds(pl.multiple_of(j * channels + 8 * i, 8), 8), :] = jnp.concatenate(parts, axis=0)
                return carry
            lax.fori_loop(0, channels // 8, body, 0)
        else:
            def body(i, carry):
                mr, mi = carry
                for k in range(8):
                    c = 8 * i + k
                    wr = w_ref[0, c, :, cols].astype(F32)
                    wi = w_ref[1, c, :, cols].astype(F32)
                    sr = s_scr[j, 0, pl.ds(c, 1), :]
                    si = s_scr[j, 1, pl.ds(c, 1), :]
                    mr = mr + (sr * wr - si * wi)
                    mi = mi + (sr * wi + si * wr)
                return mr, mi
            zero = jnp.zeros((channels, lanes), F32)
            mr, mi = lax.fori_loop(0, channels // 8, body, (zero, zero))
            m_scr[rows, :lanes] = mr
            m_scr[rows, lanes:] = mi
    mixed = (m_scr[...] * scale_out).astype(BF16)
    for s in range(plan.slabs):
        planar = dot(mixed, zi_ref[s])
        for j in range(jl):
            for part in range(2):
                o_scr[pl.ds(part * jl + j, channels, stride=2 * jl), :] = planar[
                    j * channels : (j + 1) * channels, part * pw : (part + 1) * pw
                ]
        out_ref[s] = o_scr[:, :pk].astype(BF16)


def ahead_kernel(plan, channels, scale_in, scale_out, taps_ref, x_hbm, w_hbm, ty_ref, tx_ref, zf_ref, zi_ref,
                 smooth_hbm, modes_ref, spec_ref,
                 x_ref, y_ref, before_ref, after_ref, w_ref, send1, recv1, send2,
                 band_ref, wide_ref, lower_ref, upper_ref, z_scr, s_scr, m_scr, o_scr,
                 load_sem, w_sem, store_sem, halo_send, halo_recv, send_sem, recv_sem):
    planes, slabs = plan.planes, plan.slabs
    me = lax.axis_index("slab")
    chunk = 8
    chunks = channels // chunk
    step = 2 * KX // plan.lead

    def load(i):
        rows = pl.ds(i * chunk, chunk)
        return pltpu.make_async_copy(x_hbm.at[rows], x_ref.at[rows], load_sem.at[i])

    for i in range(chunks):
        load(i).start()
    slab_barrier(me, slabs)
    halos = [halo_copies(me, slabs, x_hbm, before_ref, after_ref, planes, chunk, i, halo_send, halo_recv)
             for i in range(chunks)]
    for copies in halos:
        halo_start(me, slabs, copies)
    load_w = pltpu.make_async_copy(w_hbm, w_ref, w_sem)
    load_w.start()

    @pl.when(me == 0)
    def _():
        before_ref[...] = jnp.zeros_like(before_ref)

    @pl.when(me == slabs - 1)
    def _():
        after_ref[...] = jnp.zeros_like(after_ref)

    band_ref[...] = jnp.zeros_like(band_ref)
    for u in range(4):
        for n in range(wide_ref.shape[1]):
            wide_ref[u, n, 0:8, :] = jnp.zeros((8, NY), F32)
            wide_ref[u, n, NX + 8 : NX + 16, :] = jnp.zeros((8, NY), F32)

    def spectra(i, carry):
        load(i).wait()
        lines = [jnp.concatenate([x_ref[i * chunk + c, z] for z in range(planes)], axis=1) for c in range(chunk)]
        batch_modes(plan, send1, pl.multiple_of(i * chunk * step, chunk * step), lines, ty_ref, tx_ref)
        return carry

    lax.fori_loop(0, chunks, spectra, 0)
    first = exchange(me, slabs, send1, recv1, send_sem.at[0], recv_sem.at[0])
    for copy in first:
        copy.start()

    masks = band_masks()
    pairs = planes // 2

    def part(groups):
        def body(i, carry):
            for u in range(4):
                stencil_part(plan, taps_ref, x_ref, before_ref, after_ref, i * 4 + u, groups, False, masks, y_ref,
                             band_ref.at[u], wide_ref.at[u], lower_ref.at[u], upper_ref.at[u])
            return carry
        return body

    if pairs > 2:
        lax.fori_loop(0, channels // 4, part(list(range(1, pairs - 1))), 0)
    load_w.wait()
    for copy in first:
        copy.wait()
    mix_modes(plan, channels, me, False, scale_in, scale_out, send1, recv1, zf_ref, zi_ref, w_ref,
              send2, spec_ref, z_scr, s_scr, m_scr, o_scr)
    second = exchange(me, slabs, send2, modes_ref, send_sem.at[1], recv_sem.at[1])
    for copy in second:
        copy.start()
    modes_ref[me] = send2[me]

    def store(i):
        rows = pl.ds(i * chunk, chunk)
        return pltpu.make_async_copy(y_ref.at[rows], smooth_hbm.at[rows], store_sem.at[i])

    edge = part([0, pairs - 1] if pairs > 1 else [0])
    for i in range(chunks):
        halo_wait_recv(me, slabs, halos[i])
        lax.fori_loop(2 * i, 2 * i + 2, edge, 0)
        store(i).start()
    for copy in second:
        copy.wait()
    for copies in halos:
        halo_wait_send(me, slabs, copies)
    for i in range(chunks):
        store(i).wait()


def ahead_call(plan, taps, field, weights, ty, tx, zf, zi, scale_in, scale_out):
    channels, planes = field.shape[:2]
    slabs = plan.slabs
    rows = channels * 2 * plan.jl
    modes = plan.jl * plan.lanes
    whole_vmem = pl.BlockSpec(memory_space=pltpu.VMEM)
    anywhere = pl.BlockSpec(memory_space=pl.ANY)
    slots = min(planes + 2, 8)
    chunks = channels // 8
    return pl.pallas_call(
        functools.partial(ahead_kernel, plan, channels, scale_in, scale_out),
        in_specs=[pl.BlockSpec(memory_space=pltpu.SMEM), anywhere, anywhere] + [whole_vmem] * 4,
        out_specs=[anywhere, whole_vmem, whole_vmem],
        out_shape=[
            jax.ShapeDtypeStruct(field.shape, BF16),
            jax.ShapeDtypeStruct((slabs, rows, plan.pk), BF16),
            jax.ShapeDtypeStruct((modes, 2 * channels), BF16),
        ],
        scratch_shapes=[
            pltpu.VMEM(field.shape, BF16),
            pltpu.VMEM(field.shape, BF16),
            pltpu.VMEM((channels, NX, NY), BF16),
            pltpu.VMEM((channels, NX, NY), BF16),
            pltpu.VMEM(weights.shape, BF16),
            pltpu.VMEM((slabs, rows, plan.pk), BF16),
            pltpu.VMEM((slabs, rows, plan.pk), BF16),
            pltpu.VMEM((slabs, rows, plan.pk), BF16),
            pltpu.VMEM((4, 12 * NY, 2 * NY), BF16),
            pltpu.VMEM((4, slots, NX + 16, NY), F32),
            pltpu.VMEM((4, slots, NX, NY), BF16),
            pltpu.VMEM((4, slots, NX, NY), BF16),
            pltpu.VMEM((2 * plan.lanes // 128, rows, 128), F32),
            pltpu.VMEM((plan.jl, 2, channels, plan.lanes), F32),
            pltpu.VMEM((plan.jl * channels, 2 * plan.lanes), F32),
            pltpu.VMEM((rows, plan.pw), F32),
            pltpu.SemaphoreType.DMA((chunks,)),
            pltpu.SemaphoreType.DMA,
            pltpu.SemaphoreType.DMA((chunks,)),
            pltpu.SemaphoreType.DMA((2, chunks)),
            pltpu.SemaphoreType.DMA((2, chunks)),
            pltpu.SemaphoreType.DMA((2, slabs - 1)),
            pltpu.SemaphoreType.DMA((2, slabs - 1)),
        ],
        compiler_params=pltpu.CompilerParams(
            vmem_limit_bytes=60 * MIB, collective_id=0, has_side_effects=True),
        name="ahead",
    )(taps, field, weights, ty, tx, zf, zi)


def column_picks(channels, columns):
    column = lax.axis_index("dp") * columns + jnp.arange(columns)
    part = column // (channels * channels)
    c = column // channels % channels
    o = column % channels
    index = jnp.arange(2 * channels)[:, None]
    spec_real = (index == c).astype(F32)
    spec_imag = (index == channels + c).astype(F32) * jnp.where(part == 0, 1.0, -1.0)
    dual_same = (index == part * channels + o).astype(F32)
    dual_other = (index == (1 - part) * channels + o).astype(F32)
    return jnp.stack([spec_real, dual_same, spec_imag, dual_other]).astype(BF16)


def local(feats, grains, spec_weight, taps, point_weight, bias, cotangent):
    samples_here, channels, planes = feats.shape[:3]
    assert samples_here == 1
    slabs = lax.axis_size("slab")
    dp = lax.axis_size("dp")
    plan = Plan(planes, slabs)
    mode_rows = spec_weight.shape[0]
    half = lambda t: jnp.asarray(t.astype(jnp.bfloat16))
    ty, tx = half(plan.y_forward), half(plan.x_forward)
    tyi, txi = half(plan.y_inverse), half(plan.x_inverse)
    zf = jnp.asarray(plan.z_forward.astype(np.float32))
    zi = jnp.asarray(plan.z_inverse.astype(np.float32))
    cell_scale = 1.0 / math.sqrt(NX * NY * NZ)
    mode_scale = 1.0 / math.sqrt(KX * KY * KZ)
    jl, kq, kk, groups = plan.jl, plan.kq, plan.kk, plan.groups

    def swap(value):
        return lax.all_to_all(value, "slab", split_axis=0, concat_axis=0, tiled=True)

    def scatter_modes(modes):
        if plan.lead == 1 or kq > 1 or plan.used < plan.width:
            modes = modes[..., : plan.used].reshape(plan.lead, channels, -1, 2 * jl, planes, kq, kk)
            modes = modes.transpose(0, 2, 5, 1, 3, 4, 6)
        return swap(modes.reshape(slabs, channels * 2 * jl, plan.pk))

    def gather_planes(planar):
        planar = swap(planar)
        if plan.lead == 1 or kq > 1 or plan.used < plan.width:
            planar = planar.reshape(plan.lead, groups // plan.lead, kq, channels, 2 * jl, planes, kk)
            planar = planar.transpose(0, 3, 1, 4, 5, 2, 6).reshape(
                plan.lead, channels, 2 * KX // plan.lead, plan.used)
            return jnp.pad(planar, ((0, 0), (0, 0), (0, 0), (0, plan.width - plan.used)))
        return planar.reshape(plan.lead, channels, 2 * KX // plan.lead, plan.width)

    up = [(i, i + 1) for i in range(slabs - 1)]
    down = [(j, i) for i, j in up]
    field = feats[0]
    weights = spec_weight.reshape(mode_rows * KZ, 2 * channels * channels).T
    weights = weights.reshape(2, channels, channels, mode_rows * KZ)
    kp, kt = point_weight, point_weight.T

    fused = plan.lead == slabs and kq == 1 and plan.used == plan.width and planes % 4 == 0
    if fused:
        zfb = half(plan.z_forward.reshape(slabs * plan.pk, 2 * plan.lanes))
        zib = half(plan.z_inverse)
        smooth, modes, spec = ahead_call(
            plan, taps, field, weights, ty, tx, zfb, zib, cell_scale, mode_scale)
        modes = modes.reshape(plan.lead, channels, 2 * KX // plan.lead, plan.width)
    else:
        low, high = rims_call(field)
        before = lax.ppermute(high, "slab", up)
        after = lax.ppermute(low, "slab", down)
        received = scatter_modes(planes_call(plan, field, ty, tx))
        smooth = stencil_call(plan, taps, field, (before, after), False)
        received, smooth = lax.optimization_barrier((received, smooth))
        mixed, spec = mix_call(plan, received, weights, zf, zi, False, cell_scale, mode_scale)
        mixed, smooth = lax.optimization_barrier((mixed, smooth))
        modes = gather_planes(mixed)
        smooth = stencil_call(plan, taps, field, (before, after), False, smooth)
    spread, first, last, dual_modes = middle_call(
        plan, grains[0], smooth, cotangent[0], modes, bias, kp, kt, txi, tyi, ty, tx)
    spread_before = lax.ppermute(last, "slab", up)
    spread_after = lax.ppermute(first, "slab", down)
    received = scatter_modes(dual_modes)
    partial = stencil_call(plan, taps, spread, (), True)
    received, partial = lax.optimization_barrier((received, partial))
    back, dual = mix_call(plan, received, weights, zf, zi, True, mode_scale, cell_scale)
    back, partial = lax.optimization_barrier((back, partial))
    back_modes = gather_planes(back)
    partial = stencil_call(plan, taps, spread, (), True, partial)
    both = jnp.concatenate([spec, dual], axis=1)
    both = lax.all_to_all(
        jnp.broadcast_to(both[None], (dp,) + both.shape), "dp", split_axis=0, concat_axis=0, tiled=True)
    columns = 2 * channels * channels // dp
    pick = column_picks(channels, columns)
    scale = 1.0 / (samples_here * dp)
    grad_spec = grad_call(both, pick * jnp.array([scale, 1, scale, 1], BF16)[:, None, None])
    grad_feats = final_call(plan, taps, partial, spread_before, spread_after, back_modes, txi, tyi)
    return grad_feats[None], grad_spec.reshape(mode_rows, KZ, columns)


def solution(mesh):
    in_specs = (
        P(("grp", "dp"), None, "slab", None, None),
        P(("grp", "dp"), "slab", None, None),
        P("slab", None, None),
        P(),
        P(),
        P(),
        P(("grp", "dp"), None, "slab", None, None),
    )
    out_specs = (P(("grp", "dp"), None, "slab", None, None), P("slab", "grp", "dp"))
    return jax.shard_map(local, mesh=mesh, in_specs=in_specs, out_specs=out_specs, check_vma=False)
```

```python
import functools
import math

import jax
import jax.numpy as jnp
import numpy as np
from jax import lax
from jax.experimental import pallas as pl
from jax.experimental.pallas import tpu as pltpu
from jax.sharding import PartitionSpec as P

NX = 128
NY = 128
NZ = 32
KX = 16
KY = 16
KZ = 16
F32 = jnp.float32
BF16 = jnp.bfloat16
HIGHEST = lax.Precision.HIGHEST
MIB = 1 << 20


def waves(count, length):
    index = np.arange(count)
    frequency = np.where(index < count // 2, index, length - count + index)
    phases = frequency[:, None] * np.arange(length)[None, :] % length
    angles = phases * (2.0 * math.pi / length)
    return np.cos(angles), np.sin(angles)


class Plan:
    def __init__(self, planes, slabs):
        self.planes = planes
        self.slabs = slabs
        rows = KX * KY // slabs
        self.rows = rows
        self.groups = slabs if rows >= KY else KX
        self.jl = KX // self.groups
        self.kq = slabs // self.groups
        self.kk = KY // self.kq
        self.width = max(128, planes * KY)
        self.used = planes * KY
        self.pk = planes * self.kk
        self.lanes = self.kk * KZ
        self.lead = self.groups if (2 * self.jl) % 8 == 0 else 1
        width, jl = self.width, self.jl
        cos_x, sin_x = waves(KX, NX)
        cos_y, sin_y = waves(KY, NY)
        cos_z, sin_z = waves(KZ, NZ)
        forward = np.zeros((planes, NY, 2, width))
        for z in range(planes):
            forward[z, :, 0, z * KY : (z + 1) * KY] = cos_y.T
            forward[z, :, 1, z * KY : (z + 1) * KY] = -sin_y.T
        forward = forward.reshape(planes * NY, 2 * width)
        self.y_forward = forward
        self.y_inverse = forward.T
        table = np.zeros((self.groups, 2, jl, 2, NX))
        back = np.zeros((2, NX, self.groups, 2, jl))
        for j in range(KX):
            g, i = divmod(j, jl)
            table[g, 0, i, 0], table[g, 0, i, 1] = cos_x[j], sin_x[j]
            table[g, 1, i, 1], table[g, 1, i, 0] = cos_x[j], -sin_x[j]
            back[0, :, g, 0, i], back[0, :, g, 1, i] = cos_x[j], -sin_x[j]
            back[1, :, g, 1, i], back[1, :, g, 0, i] = cos_x[j], sin_x[j]
        self.x_forward = table.reshape(2 * KX, 2 * NX)
        self.x_inverse = back.reshape(2 * NX, 2 * KX)
        kk, pk, lanes = self.kk, self.pk, self.lanes
        zf = np.zeros((slabs, planes, kk, 2, kk, KZ))
        self.pw = max(128, pk)
        zi = np.zeros((slabs, 2, kk, KZ, 2, planes, kk))
        for s in range(slabs):
            for z in range(planes):
                c, n = cos_z[:, s * planes + z], sin_z[:, s * planes + z]
                for k in range(kk):
                    zf[s, z, k, 0, k], zf[s, z, k, 1, k] = c, n
                    zi[s, 0, k, :, 0, z, k], zi[s, 1, k, :, 0, z, k] = c, -n
                    zi[s, 1, k, :, 1, z, k], zi[s, 0, k, :, 1, z, k] = c, n
        self.z_forward = zf.reshape(slabs, pk, 2 * lanes)
        zi = zi.reshape(slabs, 2 * lanes, 2, pk)
        zi = np.pad(zi, ((0, 0), (0, 0), (0, 0), (0, self.pw - pk)))
        self.z_inverse = zi.reshape(slabs, 2 * lanes, 2 * self.pw)


def whole(shape):
    zeros = (0,) * len(shape)
    return pl.BlockSpec(shape, lambda *_: zeros)


def params(mib):
    return pltpu.CompilerParams(vmem_limit_bytes=mib * MIB)


def dot(a, b, **kw):
    return jnp.dot(a, b, preferred_element_type=F32, **kw)


def channel_modes(plan, planes_of, ty, tx):
    field = jnp.concatenate([planes_of(z) for z in range(plan.planes)], axis=1)
    along = dot(field, ty).astype(BF16)
    stacked = jnp.concatenate([along[:, : plan.width], along[:, plan.width :]], axis=0)
    return dot(tx, stacked)


def put_modes(plan, out_ref, c, value):
    if plan.lead == 1:
        out_ref[0, c] = value.astype(BF16)
    else:
        step = 2 * KX // plan.lead
        for g in range(plan.lead):
            out_ref[g, c] = value[g * step : (g + 1) * step].astype(BF16)


def get_modes(plan, ref, c):
    if plan.lead == 1:
        return ref[0, c]
    parts = [ref[g, c].astype(F32) for g in range(plan.lead)]
    return jnp.concatenate(parts, axis=0).astype(BF16)


def planes_kernel(plan, batch, x_ref, ty_ref, tx_ref, out_ref):
    for c in range(batch):
        value = channel_modes(plan, lambda z: x_ref[c, z], ty_ref[...], tx_ref[...])
        put_modes(plan, out_ref, c, value)


def planes_call(plan, field, ty, tx):
    channels, planes = field.shape[:2]
    batch = 4
    step = 2 * KX // plan.lead
    return pl.pallas_call(
        functools.partial(planes_kernel, plan, batch),
        grid=(channels // batch,),
        in_specs=[
            pl.BlockSpec((batch, planes, NX, NY), lambda i: (i, 0, 0, 0)),
            whole(ty.shape),
            whole(tx.shape),
        ],
        out_specs=pl.BlockSpec((plan.lead, batch, step, plan.width), lambda i: (0, i, 0, 0)),
        out_shape=jax.ShapeDtypeStruct((plan.lead, channels, step, plan.width), BF16),
        compiler_params=params(60),
        cost_estimate=pl.CostEstimate(
            flops=2 * channels * NX * planes * NY * 256, bytes_accessed=field.size * 2, transcendentals=0
        ),
        name="plane_modes",
    )(field, ty, tx)


def rims_kernel(low_ref, high_ref, first_ref, last_ref):
    first_ref[...] = low_ref[:, 0]
    last_ref[...] = high_ref[:, 0]


def rims_call(field):
    channels, planes = field.shape[:2]
    batch = 8
    rim = pl.BlockSpec((batch, NX, NY), lambda i: (i, 0, 0))
    shape = jax.ShapeDtypeStruct((channels, NX, NY), field.dtype)
    return pl.pallas_call(
        rims_kernel,
        grid=(channels // batch,),
        in_specs=[
            pl.BlockSpec((batch, 1, NX, NY), lambda i: (i, 0, 0, 0)),
            pl.BlockSpec((batch, 1, NX, NY), lambda i: (i, planes - 1, 0, 0)),
        ],
        out_specs=[rim, rim],
        out_shape=[shape, shape],
        compiler_params=params(60),
        name="rims",
    )(field, field)


def bands(taps_ref, c, adjoint, group, band_ref):
    row = lax.broadcasted_iota(jnp.int32, (NY, NY), 0)
    col = lax.broadcasted_iota(jnp.int32, (NY, NY), 1)
    diff = row - col
    for dz in range(3):
        for dx in range(3):
            base = 9 * dz + 3 * dx
            t = [taps_ref[base + i, c] for i in range(3)]
            if adjoint:
                t = t[::-1]
            band = jnp.where(
                diff == 0,
                t[1],
                jnp.where(diff == 1, t[2], jnp.where(diff == -1, t[0], 0.0)),
            ).astype(BF16)
            zi, xi = (2 - dz, 2 - dx) if adjoint else (dz, dx)
            for z in range(group):
                top = (xi * (group + 2) + z + zi) * NY
                band_ref[top : top + NY, z * NY : (z + 1) * NY] = band


def shifted(plan, x_ref, before_ref, after_ref, c, rows_ref):
    edge = lax.broadcasted_iota(jnp.int32, (NX, NY), 0)
    for i in range(plan.planes + 2):
        if before_ref is None and i in (0, plan.planes + 1):
            continue
        if i == 0:
            plane = before_ref[c]
        elif i == plan.planes + 1:
            plane = after_ref[c]
        else:
            plane = x_ref[c, i - 1]
        wide = plane.astype(F32)
        lower = jnp.where(edge == 0, 0.0, pltpu.roll(wide, 1, 0))
        upper = jnp.where(edge == NX - 1, 0.0, pltpu.roll(wide, NX - 1, 0))
        cols = slice(i * NY, (i + 1) * NY)
        rows_ref[0, :, cols] = lower.astype(BF16)
        rows_ref[1, :, cols] = plane
        rows_ref[2, :, cols] = upper.astype(BF16)


def stencil_kernel(plan, batch, adjoint, group, offset, *refs):
    if offset:
        refs = refs[1:]
    if adjoint:
        taps_ref, x_ref, out_ref, band_ref, rows_ref = refs
        before_ref = after_ref = None
    else:
        taps_ref, x_ref, before_ref, after_ref, out_ref, band_ref, rows_ref = refs

    @pl.when(pl.program_id(0) == 0)
    def _():
        band_ref[...] = jnp.zeros_like(band_ref)
        rows_ref[...] = jnp.zeros_like(rows_ref)

    first = pl.program_id(0) * batch + offset
    for c in range(batch):
        half = c % 2
        band, rows = band_ref.at[half], rows_ref.at[half]
        bands(taps_ref, first + c, adjoint, group, band)
        shifted(plan, x_ref, before_ref, after_ref, c, rows)
        for z in range(0, plan.planes, group):
            cols = slice(z * NY, (z + group + 2) * NY)
            near = jnp.concatenate([rows[d, :, cols] for d in range(3)], axis=1)
            total = dot(near, band[...])
            for i in range(group):
                out_ref[c, z + i] = total[:, i * NY : (i + 1) * NY].astype(BF16)


def stencil_call(plan, taps, field, rims, adjoint, done=None):
    channels, planes = field.shape[:2]
    batch = 4
    group = 2 if planes % 2 == 0 else 1
    offset = 0 if done is None else channels // 2
    skip = offset // batch
    block = pl.BlockSpec((batch, planes, NX, NY), lambda i: (i + skip, 0, 0, 0))
    specs = [pl.BlockSpec(memory_space=pltpu.SMEM), block]
    specs += [pl.BlockSpec((batch, NX, NY), lambda i: (i + skip, 0, 0))] * len(rims)
    operands = (taps, field, *rims)
    if done is not None:
        specs = [pl.BlockSpec(memory_space=pl.ANY)] + specs
        operands = (done,) + operands
    return pl.pallas_call(
        functools.partial(stencil_kernel, plan, batch, adjoint, group, offset),
        grid=(channels // 2 // batch,),
        in_specs=specs,
        out_specs=block,
        out_shape=jax.ShapeDtypeStruct(field.shape, BF16),
        input_output_aliases={} if done is None else {0: 0},
        scratch_shapes=[
            pltpu.VMEM((2, 3 * (group + 2) * NY, group * NY), BF16),
            pltpu.VMEM((2, 3, NX, (planes + 2) * NY), BF16),
        ],
        compiler_params=params(60),
        cost_estimate=pl.CostEstimate(
            flops=field.size * 3 * (group + 2) * NY, bytes_accessed=field.size * 2, transcendentals=0
        ),
        name="stencil_back" if adjoint else "stencil",
    )(*operands)


def final_kernel(plan, batch, taps_ref, x_ref, before_ref, after_ref, m_ref, tx_ref, ty_ref, out_ref):
    first = pl.program_id(0) * batch
    edge = lax.broadcasted_iota(jnp.int32, (NX, NY), 0)
    diff = lax.broadcasted_iota(jnp.int32, (NY, NY), 0) - lax.broadcasted_iota(jnp.int32, (NY, NY), 1)

    def rim(c, plane, dz):
        wide = plane.astype(F32)
        lower = jnp.where(edge == 0, 0.0, pltpu.roll(wide, 1, 0)).astype(BF16)
        upper = jnp.where(edge == NX - 1, 0.0, pltpu.roll(wide, NX - 1, 0)).astype(BF16)
        band = []
        for dx in (2, 1, 0):
            t = [taps_ref[9 * dz + 3 * dx + i, first + c] for i in range(3)]
            band.append(jnp.where(
                diff == 0,
                t[1],
                jnp.where(diff == 1, t[0], jnp.where(diff == -1, t[2], 0.0)),
            ).astype(BF16))
        return dot(jnp.concatenate([lower, plane, upper], axis=1), jnp.concatenate(band, axis=0))

    for c in range(batch):
        wave = dot(tx_ref[...], get_modes(plan, m_ref, c)).astype(BF16)
        wave = jnp.concatenate([wave[:NX], wave[NX:]], axis=1)
        full = dot(wave, ty_ref[...])
        for z in range(plan.planes):
            total = full[:, z * NY : (z + 1) * NY] + x_ref[c, z].astype(F32)
            if z == 0:
                total = total + rim(c, before_ref[c], 2)
            if z == plan.planes - 1:
                total = total + rim(c, after_ref[c], 0)
            out_ref[c, z] = total.astype(BF16)


def final_call(plan, taps, partial, before, after, modes, tx, ty):
    channels, planes = partial.shape[:2]
    batch = 4
    block = pl.BlockSpec((batch, planes, NX, NY), lambda i: (i, 0, 0, 0))
    rim = pl.BlockSpec((batch, NX, NY), lambda i: (i, 0, 0))
    return pl.pallas_call(
        functools.partial(final_kernel, plan, batch),
        grid=(channels // batch,),
        in_specs=[
            pl.BlockSpec(memory_space=pltpu.SMEM),
            block,
            rim,
            rim,
            pl.BlockSpec((modes.shape[0], batch) + modes.shape[2:], lambda i: (0, i, 0, 0)),
            whole(tx.shape),
            whole(ty.shape),
        ],
        out_specs=block,
        out_shape=jax.ShapeDtypeStruct(partial.shape, BF16),
        compiler_params=params(60),
        cost_estimate=pl.CostEstimate(
            flops=2 * partial.size * 512, bytes_accessed=partial.size * 4, transcendentals=0
        ),
        name="final",
    )(taps, partial, before, after, modes, tx, ty)


def mix_kernel(plan, channels, adjoint, scale_in, scale_out, r_ref, zf_ref, zi_ref, w_ref,
               out_ref, turned_ref, z_scr, s_scr, m_scr, o_scr):
    jl, lanes, pk, pw = plan.jl, plan.lanes, plan.pk, plan.pw
    chunks = 2 * lanes // 128
    total = None
    for s in range(plan.slabs):
        part = dot(r_ref[s].astype(F32), zf_ref[s], precision=HIGHEST)
        total = part if total is None else total + part
    total = total * scale_in
    for q in range(chunks):
        z_scr[q] = total[:, q * 128 : (q + 1) * 128]

    def rows_of(start):
        return jnp.concatenate(
            [z_scr[q, pl.ds(start, channels, stride=2 * jl), :] for q in range(chunks)], axis=1)

    for j in range(jl):
        re, im = rows_of(j), rows_of(jl + j)
        real = re[:, :lanes] + im[:, lanes:]
        imag = im[:, :lanes] - re[:, lanes:]
        s_scr[j, 0] = real
        s_scr[j, 1] = imag
        both = jnp.concatenate([real, imag], axis=0)
        turned_ref[j * lanes : (j + 1) * lanes, :] = both.T.astype(BF16)
        cols = slice(j * lanes, (j + 1) * lanes)
        rows = slice(j * channels, (j + 1) * channels)
        if adjoint:
            for c in range(channels):
                wr = w_ref[0, c, :, cols].astype(F32)
                wi = w_ref[1, c, :, cols].astype(F32)
                br = jnp.sum(wr * real + wi * imag, axis=0, keepdims=True)
                bi = jnp.sum(wr * imag - wi * real, axis=0, keepdims=True)
                m_scr[j * channels + c : j * channels + c + 1, :lanes] = br
                m_scr[j * channels + c : j * channels + c + 1, lanes:] = bi
        else:
            mr = jnp.zeros((channels, lanes), F32)
            mi = jnp.zeros((channels, lanes), F32)
            for c in range(channels):
                wr = w_ref[0, c, :, cols].astype(F32)
                wi = w_ref[1, c, :, cols].astype(F32)
                sr = s_scr[j, 0, c : c + 1, :]
                si = s_scr[j, 1, c : c + 1, :]
                mr = mr + (sr * wr - si * wi)
                mi = mi + (sr * wi + si * wr)
            m_scr[rows, :lanes] = mr
            m_scr[rows, lanes:] = mi
    mixed = m_scr[...] * scale_out
    for s in range(plan.slabs):
        planar = dot(mixed, zi_ref[s], precision=HIGHEST)
        for j in range(jl):
            for part in range(2):
                o_scr[pl.ds(part * jl + j, channels, stride=2 * jl), :] = planar[
                    j * channels : (j + 1) * channels, part * pw : (part + 1) * pw
                ]
        out_ref[s] = o_scr[:, :pk].astype(BF16)


def mix_call(plan, received, weights, zf, zi, adjoint, scale_in, scale_out):
    channels = weights.shape[1]
    rows = channels * 2 * plan.jl
    modes = plan.jl * plan.lanes
    return pl.pallas_call(
        functools.partial(mix_kernel, plan, channels, adjoint, scale_in, scale_out),
        out_shape=(
            jax.ShapeDtypeStruct((plan.slabs, rows, plan.pk), BF16),
            jax.ShapeDtypeStruct((modes, 2 * channels), BF16),
        ),
        scratch_shapes=[
            pltpu.VMEM((2 * plan.lanes // 128, rows, 128), F32),
            pltpu.VMEM((plan.jl, 2, channels, plan.lanes), F32),
            pltpu.VMEM((plan.jl * channels, 2 * plan.lanes), F32),
            pltpu.VMEM((rows, plan.pw), F32),
        ],
        compiler_params=params(60),
        name="mix_back" if adjoint else "mix",
    )(received, zf, zi, weights)


def middle_kernel(plan, channels, g_ref, sm_ref, cot_ref, m_ref, bias_ref, pw_ref, pt_ref,
                  txi_ref, tyi_ref, ty_ref, tx_ref,
                  spread_ref, first_ref, last_ref, modes_ref, wave_scr, delta_scr, move_scr, kp_ref, kt_ref):
    z = pl.program_id(0)
    planes = plan.planes
    width = plan.width

    @pl.when(z == 0)
    def _():
        def body(c, carry):
            wave = dot(txi_ref[...], get_modes(plan, m_ref, c)).astype(BF16)
            wave_scr[c, :, :width] = wave[:NX]
            wave_scr[c, :, width:] = wave[NX:]
            return carry
        lax.fori_loop(0, channels, body, 0, unroll=4)
        rows = channels * 16
        pick = lax.broadcasted_iota(jnp.int32, (rows, channels), 0) >> 4
        pick = pick == lax.broadcasted_iota(jnp.int32, (rows, channels), 1)
        pick = jnp.where(pick, 1.0, 0.0).astype(BF16)
        same = lax.broadcasted_iota(jnp.int32, (rows, rows), 0) & 15
        same = same == (lax.broadcasted_iota(jnp.int32, (rows, rows), 1) & 15)
        for src, dst in ((pt_ref, kp_ref), (pw_ref, kt_ref)):
            tall = dot(pick, src[...]).astype(BF16)
            full = lax.dot_general(tall, pick, (((1,), (1,)), ((), ())), preferred_element_type=F32)
            dst[...] = jnp.where(same, full, 0.0).astype(BF16)

    g = g_ref[0]
    row = lax.broadcasted_iota(jnp.int32, (NX, NY), 0)
    col = lax.broadcasted_iota(jnp.int32, (NX, NY), 1)

    def differs(shift, axis, inside):
        return jnp.where((g != pltpu.roll(g, shift, axis)) & inside, 0.25, 0.0)

    move_scr[...] = (
        0.25
        + differs(1, 0, row > 0)
        + differs(NX - 1, 0, row < NX - 1)
        + differs(1, 1, col > 0)
        + differs(NY - 1, 1, col < NY - 1)
    )
    height = channels * 16
    bias = bias_ref[...]

    def body(pair, carry):
        starts = [pair * 32 + 16 * i for i in range(2)]

        def tile(ref):
            return [ref[:, 0, pl.ds(x, 16), :].reshape(height, NY) for x in starts]

        mixed = dot(kp_ref[...], jnp.concatenate(tile(sm_ref), axis=1))
        cot = tile(cot_ref)
        deltas = []
        for i, x in enumerate(starts):
            moving = move_scr[pl.ds(x, 16), :]
            wave = wave_scr[:, pl.ds(x, 16), :].reshape(height, 2 * width)
            spectral = dot(wave, tyi_ref[...])
            local = mixed[:, i * NY : (i + 1) * NY].reshape(channels, 16, NY) * moving[None]
            pre = spectral.reshape(channels, 16, NY) + local + bias
            gate = 0.5 + 0.5 * jnp.tanh(0.5 * pre)
            delta = cot[i].astype(F32).reshape(channels, 16, NY) * gate * (1.0 + pre * (1.0 - gate))
            delta = delta.astype(BF16)
            delta_scr[:, z, pl.ds(x, 16), :] = delta
            deltas.append(delta.reshape(height, NY))
        turned = dot(kt_ref[...], jnp.concatenate(deltas, axis=1))
        for i, x in enumerate(starts):
            moving = move_scr[pl.ds(x, 16), :]
            value = turned[:, i * NY : (i + 1) * NY].reshape(channels, 16, NY) * moving[None]
            spread_ref[:, 0, pl.ds(x, 16), :] = value.astype(BF16)
        return carry

    for pair in range(NX // 32):
        body(pair, 0)

    @pl.when(z == 0)
    def _():
        first_ref[...] = spread_ref[:, 0]

    @pl.when(z == planes - 1)
    def _():
        last_ref[...] = spread_ref[:, 0]

        def body(i, carry):
            for c in (2 * i, 2 * i + 1):
                value = channel_modes(plan, lambda p: delta_scr[c, p], ty_ref[...], tx_ref[...])
                put_modes(plan, modes_ref, c, value)
            return carry

        lax.fori_loop(0, channels // 2, body, 0)


def middle_call(plan, grains, smooth, cotangent, modes, bias, kp, kt, txi, tyi, ty, tx):
    channels, planes = smooth.shape[:2]
    width = plan.width
    block = pl.BlockSpec((channels, 1, NX, NY), lambda z: (0, z, 0, 0))
    rim = jax.ShapeDtypeStruct((channels, NX, NY), BF16)
    return pl.pallas_call(
        functools.partial(middle_kernel, plan, channels),
        grid=(planes,),
        in_specs=[
            pl.BlockSpec((1, NX, NY), lambda z: (z, 0, 0)),
            block,
            block,
            whole(modes.shape),
            whole((channels, 1, 1)),
            whole(kp.shape),
            whole(kt.shape),
            whole(txi.shape),
            pl.BlockSpec((2 * width, NY), lambda z: (0, z)),
            whole(ty.shape),
            whole(tx.shape),
        ],
        out_specs=[block, whole(rim.shape), whole(rim.shape), whole(modes.shape)],
        out_shape=[jax.ShapeDtypeStruct(smooth.shape, BF16), rim, rim,
                   jax.ShapeDtypeStruct(modes.shape, BF16)],
        scratch_shapes=[
            pltpu.VMEM((channels, NX, 2 * width), BF16),
            pltpu.VMEM((channels, planes, NX, NY), BF16),
            pltpu.VMEM((NX, NY), F32),
            pltpu.VMEM((16 * channels, 16 * channels), BF16),
            pltpu.VMEM((16 * channels, 16 * channels), BF16),
        ],
        compiler_params=params(60),
        name="middle",
    )(grains, smooth, cotangent, modes, bias.reshape(channels, 1, 1), kp, kt, txi, tyi, ty, tx)


def grad_kernel(samples, both_ref, e_ref, out_ref):
    total = None
    for i in range(samples):
        half = both_ref.shape[-1] // 2
        spec, dual = both_ref[i, :, :half], both_ref[i, :, half:]
        term = dot(spec, e_ref[0]) * dot(dual, e_ref[1]) + dot(spec, e_ref[2]) * dot(dual, e_ref[3])
        total = term if total is None else total + term
    out_ref[...] = total


def grad_call(both, pick):
    samples, modes, width = both.shape
    columns = pick.shape[-1]
    batch = min(256, modes)
    return pl.pallas_call(
        functools.partial(grad_kernel, samples),
        grid=(modes // batch,),
        in_specs=[
            pl.BlockSpec((samples, batch, width), lambda i: (0, i, 0)),
            whole(pick.shape),
        ],
        out_specs=pl.BlockSpec((batch, columns), lambda i: (i, 0)),
        out_shape=jax.ShapeDtypeStruct((modes, columns), F32),
        compiler_params=params(60),
        cost_estimate=pl.CostEstimate(
            flops=8 * samples * modes * width * columns, bytes_accessed=modes * columns * 4, transcendentals=0
        ),
        name="grad_modes",
    )(both, pick)


def slab_peer(me, d, slabs):
    return lax.rem(me + d, slabs)


def enter(sizes):
    barrier = pltpu.get_barrier_semaphore()
    total = 0
    for axis, size in sizes.items():
        me = lax.axis_index(axis)
        for d in range(1, size):
            pl.semaphore_signal(
                barrier, inc=1, device_id={axis: slab_peer(me, d, size)}, device_id_type=pl.DeviceIdType.MESH)
        total += size - 1
    pl.semaphore_wait(barrier, total)


def exchange(me, slabs, send_ref, recv_ref, send_sem, recv_sem):
    copies = []
    for d in range(1, slabs):
        peer = slab_peer(me, d, slabs)
        copies.append(pltpu.make_async_remote_copy(
            src_ref=send_ref.at[peer],
            dst_ref=recv_ref.at[me],
            send_sem=send_sem.at[d - 1],
            recv_sem=recv_sem.at[d - 1],
            device_id={"slab": peer},
            device_id_type=pl.DeviceIdType.MESH,
        ))
    return copies


def halo_copies(me, slabs, field_ref, before_ref, after_ref, planes, chunk, index, send_sem, recv_sem):
    rows = pl.ds(index * chunk, chunk)
    up = pltpu.make_async_remote_copy(
        src_ref=field_ref.at[rows, planes - 1],
        dst_ref=before_ref.at[rows],
        send_sem=send_sem.at[0, index],
        recv_sem=recv_sem.at[0, index],
        device_id={"slab": lax.rem(me + 1, slabs)},
        device_id_type=pl.DeviceIdType.MESH,
    )
    down = pltpu.make_async_remote_copy(
        src_ref=field_ref.at[rows, 0],
        dst_ref=after_ref.at[rows],
        send_sem=send_sem.at[1, index],
        recv_sem=recv_sem.at[1, index],
        device_id={"slab": lax.rem(me + slabs - 1, slabs)},
        device_id_type=pl.DeviceIdType.MESH,
    )
    return up, down


def halo_start(me, slabs, copies):
    up, down = copies

    @pl.when(me < slabs - 1)
    def _():
        up.start()

    @pl.when(me > 0)
    def _():
        down.start()


def halo_wait_recv(me, slabs, copies):
    up, down = copies

    @pl.when(me > 0)
    def _():
        up.wait_recv()

    @pl.when(me < slabs - 1)
    def _():
        down.wait_recv()


def halo_wait_send(me, slabs, copies):
    up, down = copies

    @pl.when(me < slabs - 1)
    def _():
        up.wait_send()

    @pl.when(me > 0)
    def _():
        down.wait_send()


def batch_modes(plan, out_ref, row, lines, ty_ref, tx_ref):
    count = len(lines)
    along = dot(jnp.concatenate(lines, axis=0), ty_ref[...]).astype(BF16)
    width = plan.width
    values = []
    for c in range(0, count, 2):
        top = along[c * NX : (c + 1) * NX]
        low = along[(c + 1) * NX : (c + 2) * NX]
        pair = jnp.concatenate([
            jnp.concatenate([top[:, :width], low[:, :width]], axis=1),
            jnp.concatenate([top[:, width:], low[:, width:]], axis=1),
        ], axis=0)
        both = dot(tx_ref[...], pair)
        values += [both[:, :width], both[:, width:]]
    step = 2 * KX // plan.lead
    for g in range(plan.lead):
        part = jnp.concatenate([v[g * step : (g + 1) * step] for v in values], axis=0)
        out_ref[g, pl.ds(row, count * step), :] = part.astype(BF16)


def band_masks():
    diff = lax.broadcasted_iota(jnp.int32, (NY, NY), 0) - lax.broadcasted_iota(jnp.int32, (NY, NY), 1)
    return diff == 1, diff == 0, diff == -1


def fill_band(taps_ref, c, adjoint, masks, band_ref):
    low, mid, upp = masks
    for dz in range(3):
        for dx in range(3):
            base = 9 * dz + 3 * dx
            t = [taps_ref[base + i, c] for i in range(3)]
            if adjoint:
                t = t[::-1]
            band = jnp.where(mid, t[1], jnp.where(low, t[2], jnp.where(upp, t[0], 0.0))).astype(BF16)
            zi, xi = (2 - dz, 2 - dx) if adjoint else (dz, dx)
            for z in range(2):
                top = (xi * 4 + z + zi) * NY
                band_ref[top : top + NY, z * NY : (z + 1) * NY] = band


def stencil_part(plan, taps_ref, x_ref, before_ref, after_ref, c, groups, adjoint, masks, out_ref,
                 band_ref, wide_ref, lower_ref, upper_ref):
    fill_band(taps_ref, c, adjoint, masks, band_ref)
    planes = plan.planes

    def plane(i):
        if i == 0:
            return before_ref[c]
        if i == planes + 1:
            return after_ref[c]
        return x_ref[c, i - 1]

    needed = sorted({2 * g + i for g in groups for i in range(4)})
    slot = {i: n for n, i in enumerate(needed)}
    for i in needed:
        n = slot[i]
        wide_ref[n, 8 : NX + 8, :] = plane(i).astype(F32)
        lower_ref[n] = wide_ref[n, 7 : NX + 7, :].astype(BF16)
        upper_ref[n] = wide_ref[n, 9 : NX + 9, :].astype(BF16)

    def moved(dx, i):
        if dx == 1:
            return plane(i)
        return (lower_ref if dx == 0 else upper_ref)[slot[i]]

    near = jnp.concatenate([
        jnp.concatenate([moved(dx, 2 * g + i) for dx in range(3) for i in range(4)], axis=1)
        for g in groups
    ], axis=0)
    total = dot(near, band_ref[...])
    for n, g in enumerate(groups):
        for i in range(2):
            out_ref[c, 2 * g + i] = total[n * NX : (n + 1) * NX, i * NY : (i + 1) * NY].astype(BF16)


def mix_modes(plan, channels, me, adjoint, scale_in, scale_out, own_ref, r_ref, zf_ref, zi_ref, w_ref,
              out_ref, turned_ref, z_scr, s_scr, m_scr, o_scr):
    jl, lanes, pk, pw = plan.jl, plan.lanes, plan.pk, plan.pw
    chunks = 2 * lanes // 128
    r_ref[me] = own_ref[me]
    total = dot(jnp.concatenate([r_ref[s] for s in range(plan.slabs)], axis=1), zf_ref[...])
    total = total * scale_in
    for q in range(chunks):
        z_scr[q] = total[:, q * 128 : (q + 1) * 128]

    def rows_of(start):
        return jnp.concatenate(
            [z_scr[q, pl.ds(start, channels, stride=2 * jl), :] for q in range(chunks)], axis=1)

    for j in range(jl):
        re, im = rows_of(j), rows_of(jl + j)
        real = re[:, :lanes] + im[:, lanes:]
        imag = im[:, :lanes] - re[:, lanes:]
        s_scr[j, 0] = real
        s_scr[j, 1] = imag
        both = jnp.concatenate([real, imag], axis=0)
        turned_ref[j * lanes : (j + 1) * lanes, :] = both.T.astype(BF16)
        cols = slice(j * lanes, (j + 1) * lanes)
        rows = slice(j * channels, (j + 1) * channels)
        if adjoint:
            def body(i, carry):
                parts = []
                for k in range(8):
                    c = 8 * i + k
                    wr = w_ref[0, c, :, cols].astype(F32)
                    wi = w_ref[1, c, :, cols].astype(F32)
                    real, imag = s_scr[j, 0], s_scr[j, 1]
                    br = jnp.sum(wr * real + wi * imag, axis=0, keepdims=True)
                    bi = jnp.sum(wr * imag - wi * real, axis=0, keepdims=True)
                    parts.append(jnp.concatenate([br, bi], axis=1))
                m_scr[pl.ds(pl.multiple_of(j * channels + 8 * i, 8), 8), :] = jnp.concatenate(parts, axis=0)
                return carry
            lax.fori_loop(0, channels // 8, body, 0)
        else:
            def body(i, carry):
                mr, mi = carry
                for k in range(8):
                    c = 8 * i + k
                    wr = w_ref[0, c, :, cols].astype(F32)
                    wi = w_ref[1, c, :, cols].astype(F32)
                    sr = s_scr[j, 0, pl.ds(c, 1), :]
                    si = s_scr[j, 1, pl.ds(c, 1), :]
                    mr = mr + (sr * wr - si * wi)
                    mi = mi + (sr * wi + si * wr)
                return mr, mi
            zero = jnp.zeros((channels, lanes), F32)
            mr, mi = lax.fori_loop(0, channels // 8, body, (zero, zero))
            m_scr[rows, :lanes] = mr
            m_scr[rows, lanes:] = mi
    mixed = (m_scr[...] * scale_out).astype(BF16)
    for s in range(plan.slabs):
        planar = dot(mixed, zi_ref[s])
        for j in range(jl):
            for part in range(2):
                o_scr[pl.ds(part * jl + j, channels, stride=2 * jl), :] = planar[
                    j * channels : (j + 1) * channels, part * pw : (part + 1) * pw
                ]
        out_ref[s] = o_scr[:, :pk].astype(BF16)


def ahead_kernel(plan, channels, scale_in, scale_out, taps_ref, x_hbm, w_hbm, ty_ref, tx_ref, zf_ref, zi_ref,
                 smooth_hbm, modes_ref, spec_ref,
                 x_ref, y_ref, before_ref, after_ref, w_ref, send1, recv1, send2,
                 band_ref, wide_ref, lower_ref, upper_ref, z_scr, s_scr, m_scr, o_scr,
                 load_sem, w_sem, store_sem, halo_send, halo_recv, send_sem, recv_sem):
    planes, slabs = plan.planes, plan.slabs
    me = lax.axis_index("slab")
    chunk = 8
    chunks = channels // chunk
    step = 2 * KX // plan.lead

    def load(i):
        rows = pl.ds(i * chunk, chunk)
        return pltpu.make_async_copy(x_hbm.at[rows], x_ref.at[rows], load_sem.at[i])

    for i in range(chunks):
        load(i).start()
    enter({"slab": slabs})
    halos = [halo_copies(me, slabs, x_hbm, before_ref, after_ref, planes, chunk, i, halo_send, halo_recv)
             for i in range(chunks)]
    for copies in halos[:1]:
        halo_start(me, slabs, copies)
    load_w = pltpu.make_async_copy(w_hbm, w_ref, w_sem)
    load_w.start()

    @pl.when(me == 0)
    def _():
        before_ref[...] = jnp.zeros_like(before_ref)

    @pl.when(me == slabs - 1)
    def _():
        after_ref[...] = jnp.zeros_like(after_ref)

    band_ref[...] = jnp.zeros_like(band_ref)
    for u in range(4):
        for n in range(wide_ref.shape[1]):
            wide_ref[u, n, 0:8, :] = jnp.zeros((8, NY), F32)
            wide_ref[u, n, NX + 8 : NX + 16, :] = jnp.zeros((8, NY), F32)

    def spectra(i, carry):
        load(i).wait()
        lines = [jnp.concatenate([x_ref[i * chunk + c, z] for z in range(planes)], axis=1) for c in range(chunk)]
        batch_modes(plan, send1, pl.multiple_of(i * chunk * step, chunk * step), lines, ty_ref, tx_ref)
        return carry

    lax.fori_loop(0, chunks, spectra, 0)
    first = exchange(me, slabs, send1, recv1, send_sem.at[0], recv_sem.at[0])
    for copy in first:
        copy.start()
    for copies in halos[1:2]:
        halo_start(me, slabs, copies)

    masks = band_masks()
    pairs = planes // 2

    def part(groups):
        def body(i, carry):
            for u in range(4):
                stencil_part(plan, taps_ref, x_ref, before_ref, after_ref, i * 4 + u, groups, False, masks, y_ref,
                             band_ref.at[u], wide_ref.at[u], lower_ref.at[u], upper_ref.at[u])
            return carry
        return body

    if pairs > 2:
        lax.fori_loop(0, channels // 4, part(list(range(1, pairs - 1))), 0)
    load_w.wait()
    for copy in first:
        copy.wait()
    mix_modes(plan, channels, me, False, scale_in, scale_out, send1, recv1, zf_ref, zi_ref, w_ref,
              send2, spec_ref, z_scr, s_scr, m_scr, o_scr)
    second = exchange(me, slabs, send2, modes_ref, send_sem.at[1], recv_sem.at[1])
    for copy in second:
        copy.start()
    for copies in halos[2:]:
        halo_start(me, slabs, copies)
    modes_ref[me] = send2[me]

    def store(i):
        rows = pl.ds(i * chunk, chunk)
        return pltpu.make_async_copy(y_ref.at[rows], smooth_hbm.at[rows], store_sem.at[i])

    edge = part([0, pairs - 1] if pairs > 1 else [0])
    for i in range(chunks):
        halo_wait_recv(me, slabs, halos[i])
        lax.fori_loop(2 * i, 2 * i + 2, edge, 0)
        store(i).start()
    for copy in second:
        copy.wait()
    for copies in halos:
        halo_wait_send(me, slabs, copies)
    for i in range(chunks):
        store(i).wait()


def ahead_call(plan, taps, field, weights, ty, tx, zf, zi, scale_in, scale_out):
    channels, planes = field.shape[:2]
    slabs = plan.slabs
    rows = channels * 2 * plan.jl
    modes = plan.jl * plan.lanes
    whole_vmem = pl.BlockSpec(memory_space=pltpu.VMEM)
    anywhere = pl.BlockSpec(memory_space=pl.ANY)
    slots = min(planes + 2, 8)
    chunks = channels // 8
    return pl.pallas_call(
        functools.partial(ahead_kernel, plan, channels, scale_in, scale_out),
        in_specs=[pl.BlockSpec(memory_space=pltpu.SMEM), anywhere, anywhere] + [whole_vmem] * 4,
        out_specs=[anywhere, whole_vmem, whole_vmem],
        out_shape=[
            jax.ShapeDtypeStruct(field.shape, BF16),
            jax.ShapeDtypeStruct((slabs, rows, plan.pk), BF16),
            jax.ShapeDtypeStruct((modes, 2 * channels), BF16),
        ],
        scratch_shapes=[
            pltpu.VMEM(field.shape, BF16),
            pltpu.VMEM(field.shape, BF16),
            pltpu.VMEM((channels, NX, NY), BF16),
            pltpu.VMEM((channels, NX, NY), BF16),
            pltpu.VMEM(weights.shape, BF16),
            pltpu.VMEM((slabs, rows, plan.pk), BF16),
            pltpu.VMEM((slabs, rows, plan.pk), BF16),
            pltpu.VMEM((slabs, rows, plan.pk), BF16),
            pltpu.VMEM((4, 12 * NY, 2 * NY), BF16),
            pltpu.VMEM((4, slots, NX + 16, NY), F32),
            pltpu.VMEM((4, slots, NX, NY), BF16),
            pltpu.VMEM((4, slots, NX, NY), BF16),
            pltpu.VMEM((2 * plan.lanes // 128, rows, 128), F32),
            pltpu.VMEM((plan.jl, 2, channels, plan.lanes), F32),
            pltpu.VMEM((plan.jl * channels, 2 * plan.lanes), F32),
            pltpu.VMEM((rows, plan.pw), F32),
            pltpu.SemaphoreType.DMA((chunks,)),
            pltpu.SemaphoreType.DMA,
            pltpu.SemaphoreType.DMA((chunks,)),
            pltpu.SemaphoreType.DMA((2, chunks)),
            pltpu.SemaphoreType.DMA((2, chunks)),
            pltpu.SemaphoreType.DMA((2, slabs - 1)),
            pltpu.SemaphoreType.DMA((2, slabs - 1)),
        ],
        compiler_params=pltpu.CompilerParams(
            vmem_limit_bytes=60 * MIB, collective_id=0, has_side_effects=True),
        name="ahead",
    )(taps, field, weights, ty, tx, zf, zi)


def behind_kernel(plan, channels, peers, scale_in, scale_out, taps_ref, x_hbm, w_hbm, dual_ref, spec_ref, zf_ref, zi_ref,
                  partial_hbm, modes_ref, gather_ref,
                  x_ref, y_ref, before_ref, after_ref, w_ref, recv1, send2, turned_ref, both_ref,
                  band_ref, wide_ref, lower_ref, upper_ref, z_scr, s_scr, m_scr, o_scr,
                  load_sem, w_sem, store_sem, halo_send, halo_recv, send_sem, recv_sem, both_send, both_recv):
    planes, slabs = plan.planes, plan.slabs
    me = lax.axis_index("slab")
    lane = lax.axis_index("dp")
    chunk = 8
    chunks = channels // chunk

    def load(i):
        rows = pl.ds(i * chunk, chunk)
        return pltpu.make_async_copy(x_hbm.at[rows], x_ref.at[rows], load_sem.at[i])

    for i in range(chunks):
        load(i).start()
    enter({"slab": slabs, "dp": peers})
    first = exchange(me, slabs, dual_ref, recv1, send_sem.at[0], recv_sem.at[0])
    for copy in first:
        copy.start()
    halos = [halo_copies(me, slabs, x_hbm, before_ref, after_ref, planes, chunk, i, halo_send, halo_recv)
             for i in range(chunks)]
    for copies in halos[:2]:
        halo_start(me, slabs, copies)
    load_w = pltpu.make_async_copy(w_hbm, w_ref, w_sem)
    load_w.start()

    @pl.when(me == 0)
    def _():
        before_ref[...] = jnp.zeros_like(before_ref)

    @pl.when(me == slabs - 1)
    def _():
        after_ref[...] = jnp.zeros_like(after_ref)

    band_ref[...] = jnp.zeros_like(band_ref)
    for u in range(4):
        for n in range(wide_ref.shape[1]):
            wide_ref[u, n, 0:8, :] = jnp.zeros((8, NY), F32)
            wide_ref[u, n, NX + 8 : NX + 16, :] = jnp.zeros((8, NY), F32)

    masks = band_masks()
    pairs = planes // 2

    def part(groups, loading):
        def body(i, carry):
            if loading:
                @pl.when(lax.rem(i, 2) == 0)
                def _():
                    load(i // 2).wait()
            for u in range(4):
                stencil_part(plan, taps_ref, x_ref, before_ref, after_ref, i * 4 + u, groups, True, masks, y_ref,
                             band_ref.at[u], wide_ref.at[u], lower_ref.at[u], upper_ref.at[u])
            return carry
        return body

    if pairs > 2:
        lax.fori_loop(0, channels // 4, part(list(range(1, pairs - 1)), True), 0)
    else:
        for i in range(chunks):
            load(i).wait()
    load_w.wait()
    for copy in first:
        copy.wait()
    mix_modes(plan, channels, me, True, scale_in, scale_out, dual_ref, recv1, zf_ref, zi_ref, w_ref,
              send2, turned_ref, z_scr, s_scr, m_scr, o_scr)
    second = exchange(me, slabs, send2, modes_ref, send_sem.at[1], recv_sem.at[1])
    for copy in second:
        copy.start()
    for copies in halos[2:]:
        halo_start(me, slabs, copies)
    modes_ref[me] = send2[me]
    both_ref[...] = jnp.concatenate([spec_ref[...], turned_ref[...]], axis=1)
    shares = []
    for d in range(1, peers):
        shares.append(pltpu.make_async_remote_copy(
            src_ref=both_ref,
            dst_ref=gather_ref.at[lane],
            send_sem=both_send.at[d - 1],
            recv_sem=both_recv.at[d - 1],
            device_id={"dp": slab_peer(lane, d, peers)},
            device_id_type=pl.DeviceIdType.MESH,
        ))
    for copy in shares:
        copy.start()
    gather_ref[lane] = both_ref[...]

    def store(i):
        rows = pl.ds(i * chunk, chunk)
        return pltpu.make_async_copy(y_ref.at[rows], partial_hbm.at[rows], store_sem.at[i])

    edge = part([0, pairs - 1] if pairs > 1 else [0], False)
    for i in range(chunks):
        halo_wait_recv(me, slabs, halos[i])
        lax.fori_loop(2 * i, 2 * i + 2, edge, 0)
        store(i).start()
    for copy in second + shares:
        copy.wait()
    for copies in halos:
        halo_wait_send(me, slabs, copies)
    for i in range(chunks):
        store(i).wait()


def behind_call(plan, taps, field, weights, dual, spec, zf, zi, scale_in, scale_out, peers):
    channels, planes = field.shape[:2]
    slabs = plan.slabs
    rows = channels * 2 * plan.jl
    modes = plan.jl * plan.lanes
    whole_vmem = pl.BlockSpec(memory_space=pltpu.VMEM)
    anywhere = pl.BlockSpec(memory_space=pl.ANY)
    slots = min(planes + 2, 8)
    chunks = channels // 8
    return pl.pallas_call(
        functools.partial(behind_kernel, plan, channels, peers, scale_in, scale_out),
        in_specs=[pl.BlockSpec(memory_space=pltpu.SMEM), anywhere, anywhere] + [whole_vmem] * 4,
        out_specs=[anywhere, whole_vmem, whole_vmem],
        out_shape=[
            jax.ShapeDtypeStruct(field.shape, BF16),
            jax.ShapeDtypeStruct((slabs, rows, plan.pk), BF16),
            jax.ShapeDtypeStruct((peers, modes, 4 * channels), BF16),
        ],
        scratch_shapes=[
            pltpu.VMEM(field.shape, BF16),
            pltpu.VMEM(field.shape, BF16),
            pltpu.VMEM((channels, NX, NY), BF16),
            pltpu.VMEM((channels, NX, NY), BF16),
            pltpu.VMEM(weights.shape, BF16),
            pltpu.VMEM((slabs, rows, plan.pk), BF16),
            pltpu.VMEM((slabs, rows, plan.pk), BF16),
            pltpu.VMEM((modes, 2 * channels), BF16),
            pltpu.VMEM((modes, 4 * channels), BF16),
            pltpu.VMEM((4, 12 * NY, 2 * NY), BF16),
            pltpu.VMEM((4, slots, NX + 16, NY), F32),
            pltpu.VMEM((4, slots, NX, NY), BF16),
            pltpu.VMEM((4, slots, NX, NY), BF16),
            pltpu.VMEM((2 * plan.lanes // 128, rows, 128), F32),
            pltpu.VMEM((plan.jl, 2, channels, plan.lanes), F32),
            pltpu.VMEM((plan.jl * channels, 2 * plan.lanes), F32),
            pltpu.VMEM((rows, plan.pw), F32),
            pltpu.SemaphoreType.DMA((chunks,)),
            pltpu.SemaphoreType.DMA,
            pltpu.SemaphoreType.DMA((chunks,)),
            pltpu.SemaphoreType.DMA((2, chunks)),
            pltpu.SemaphoreType.DMA((2, chunks)),
            pltpu.SemaphoreType.DMA((2, slabs - 1)),
            pltpu.SemaphoreType.DMA((2, slabs - 1)),
            pltpu.SemaphoreType.DMA((peers - 1,)),
            pltpu.SemaphoreType.DMA((peers - 1,)),
        ],
        compiler_params=pltpu.CompilerParams(
            vmem_limit_bytes=60 * MIB, collective_id=1, has_side_effects=True),
        name="behind",
    )(taps, field, weights, dual, spec, zf, zi)


def close_kernel(plan, batch, x_ref, m_ref, tx_ref, ty_ref, out_ref):
    width = plan.width
    step = m_ref.shape[2]
    waves_of = []
    for c in range(0, batch, 2):
        pair = jnp.concatenate([
            jnp.concatenate([m_ref[g, c + k].astype(F32) for g in range(plan.lead)], axis=0) for k in range(2)
        ], axis=1).astype(BF16)
        wave = dot(tx_ref[...], pair).astype(BF16)
        for k in range(2):
            cols = slice(k * width, (k + 1) * width)
            waves_of.append(jnp.concatenate([wave[:NX, cols], wave[NX:, cols]], axis=1))
    full = dot(jnp.concatenate(waves_of, axis=0), ty_ref[...])
    for c in range(batch):
        for z in range(plan.planes):
            total = full[c * NX : (c + 1) * NX, z * NY : (z + 1) * NY] + x_ref[c, z].astype(F32)
            out_ref[c, z] = total.astype(BF16)


def close_call(plan, partial, modes, tx, ty):
    channels, planes = partial.shape[:2]
    batch = 8
    block = pl.BlockSpec((batch, planes, NX, NY), lambda i: (i, 0, 0, 0))
    return pl.pallas_call(
        functools.partial(close_kernel, plan, batch),
        grid=(channels // batch,),
        in_specs=[
            block,
            pl.BlockSpec((modes.shape[0], batch) + modes.shape[2:], lambda i: (0, i, 0, 0)),
            whole(tx.shape),
            whole(ty.shape),
        ],
        out_specs=block,
        out_shape=jax.ShapeDtypeStruct(partial.shape, BF16),
        compiler_params=params(60),
        name="close",
    )(partial, modes, tx, ty)


def column_picks(channels, columns):
    column = lax.axis_index("dp") * columns + jnp.arange(columns)
    part = column // (channels * channels)
    c = column // channels % channels
    o = column % channels
    index = jnp.arange(2 * channels)[:, None]
    spec_real = (index == c).astype(F32)
    spec_imag = (index == channels + c).astype(F32) * jnp.where(part == 0, 1.0, -1.0)
    dual_same = (index == part * channels + o).astype(F32)
    dual_other = (index == (1 - part) * channels + o).astype(F32)
    return jnp.stack([spec_real, dual_same, spec_imag, dual_other]).astype(BF16)


def local(feats, grains, spec_weight, taps, point_weight, bias, cotangent):
    samples_here, channels, planes = feats.shape[:3]
    assert samples_here == 1
    slabs = lax.axis_size("slab")
    dp = lax.axis_size("dp")
    plan = Plan(planes, slabs)
    mode_rows = spec_weight.shape[0]
    half = lambda t: jnp.asarray(t.astype(jnp.bfloat16))
    ty, tx = half(plan.y_forward), half(plan.x_forward)
    tyi, txi = half(plan.y_inverse), half(plan.x_inverse)
    zf = jnp.asarray(plan.z_forward.astype(np.float32))
    zi = jnp.asarray(plan.z_inverse.astype(np.float32))
    cell_scale = 1.0 / math.sqrt(NX * NY * NZ)
    mode_scale = 1.0 / math.sqrt(KX * KY * KZ)
    jl, kq, kk, groups = plan.jl, plan.kq, plan.kk, plan.groups

    def swap(value):
        return lax.all_to_all(value, "slab", split_axis=0, concat_axis=0, tiled=True)

    def scatter_modes(modes):
        if plan.lead == 1 or kq > 1 or plan.used < plan.width:
            modes = modes[..., : plan.used].reshape(plan.lead, channels, -1, 2 * jl, planes, kq, kk)
            modes = modes.transpose(0, 2, 5, 1, 3, 4, 6)
        return swap(modes.reshape(slabs, channels * 2 * jl, plan.pk))

    def gather_planes(planar):
        planar = swap(planar)
        if plan.lead == 1 or kq > 1 or plan.used < plan.width:
            planar = planar.reshape(plan.lead, groups // plan.lead, kq, channels, 2 * jl, planes, kk)
            planar = planar.transpose(0, 3, 1, 4, 5, 2, 6).reshape(
                plan.lead, channels, 2 * KX // plan.lead, plan.used)
            return jnp.pad(planar, ((0, 0), (0, 0), (0, 0), (0, plan.width - plan.used)))
        return planar.reshape(plan.lead, channels, 2 * KX // plan.lead, plan.width)

    up = [(i, i + 1) for i in range(slabs - 1)]
    down = [(j, i) for i, j in up]
    field = feats[0]
    weights = spec_weight.reshape(mode_rows * KZ, 2 * channels * channels).T
    weights = weights.reshape(2, channels, channels, mode_rows * KZ)
    kp, kt = point_weight, point_weight.T

    fused = plan.lead == slabs and kq == 1 and plan.used == plan.width and planes % 4 == 0
    if fused:
        zfb = half(plan.z_forward.reshape(slabs * plan.pk, 2 * plan.lanes))
        zib = half(plan.z_inverse)
        smooth, modes, spec = ahead_call(
            plan, taps, field, weights, ty, tx, zfb, zib, cell_scale, mode_scale)
        modes = modes.reshape(plan.lead, channels, 2 * KX // plan.lead, plan.width)
    else:
        low, high = rims_call(field)
        before = lax.ppermute(high, "slab", up)
        after = lax.ppermute(low, "slab", down)
        received = scatter_modes(planes_call(plan, field, ty, tx))
        smooth = stencil_call(plan, taps, field, (before, after), False)
        received, smooth = lax.optimization_barrier((received, smooth))
        mixed, spec = mix_call(plan, received, weights, zf, zi, False, cell_scale, mode_scale)
        mixed, smooth = lax.optimization_barrier((mixed, smooth))
        modes = gather_planes(mixed)
        smooth = stencil_call(plan, taps, field, (before, after), False, smooth)
    spread, first, last, dual_modes = middle_call(
        plan, grains[0], smooth, cotangent[0], modes, bias, kp, kt, txi, tyi, ty, tx)
    columns = 2 * channels * channels // dp
    pick = column_picks(channels, columns)
    scale = 1.0 / (samples_here * dp)
    pick = pick * jnp.array([scale, 1, scale, 1], BF16)[:, None, None]
    if fused:
        dual_modes = dual_modes.reshape(slabs, channels * 2 * jl, plan.pk)
        partial, back_modes, both = behind_call(
            plan, taps, spread, weights, dual_modes, spec, zfb, zib, mode_scale, cell_scale, dp)
        back_modes = back_modes.reshape(plan.lead, channels, 2 * KX // plan.lead, plan.width)
        grad_spec = grad_call(both, pick)
        grad_feats = close_call(plan, partial, back_modes, txi, tyi)
        return grad_feats[None], grad_spec.reshape(mode_rows, KZ, columns)
    spread_before = lax.ppermute(last, "slab", up)
    spread_after = lax.ppermute(first, "slab", down)
    received = scatter_modes(dual_modes)
    partial = stencil_call(plan, taps, spread, (), True)
    received, partial = lax.optimization_barrier((received, partial))
    back, dual = mix_call(plan, received, weights, zf, zi, True, mode_scale, cell_scale)
    back, partial = lax.optimization_barrier((back, partial))
    back_modes = gather_planes(back)
    partial = stencil_call(plan, taps, spread, (), True, partial)
    both = jnp.concatenate([spec, dual], axis=1)
    both = lax.all_to_all(
        jnp.broadcast_to(both[None], (dp,) + both.shape), "dp", split_axis=0, concat_axis=0, tiled=True)
    grad_spec = grad_call(both, pick)
    grad_feats = final_call(plan, taps, partial, spread_before, spread_after, back_modes, txi, tyi)
    return grad_feats[None], grad_spec.reshape(mode_rows, KZ, columns)


def solution(mesh):
    in_specs = (
        P(("grp", "dp"), None, "slab", None, None),
        P(("grp", "dp"), "slab", None, None),
        P("slab", None, None),
        P(),
        P(),
        P(),
        P(("grp", "dp"), None, "slab", None, None),
    )
    out_specs = (P(("grp", "dp"), None, "slab", None, None), P("slab", "grp", "dp"))
    return jax.shard_map(local, mesh=mesh, in_specs=in_specs, out_specs=out_specs, check_vma=False)
```

```python
import functools
import math

import jax
import jax.numpy as jnp
import numpy as np
from jax import lax
from jax.experimental import pallas as pl
from jax.experimental.pallas import tpu as pltpu
from jax.sharding import PartitionSpec as P

NX = 128
NY = 128
NZ = 32
KX = 16
KY = 16
KZ = 16
F32 = jnp.float32
BF16 = jnp.bfloat16
HIGHEST = lax.Precision.HIGHEST
MIB = 1 << 20


def waves(count, length):
    index = np.arange(count)
    frequency = np.where(index < count // 2, index, length - count + index)
    phases = frequency[:, None] * np.arange(length)[None, :] % length
    angles = phases * (2.0 * math.pi / length)
    return np.cos(angles), np.sin(angles)


class Plan:
    def __init__(self, planes, slabs):
        self.planes = planes
        self.slabs = slabs
        rows = KX * KY // slabs
        self.rows = rows
        self.groups = slabs if rows >= KY else KX
        self.jl = KX // self.groups
        self.kq = slabs // self.groups
        self.kk = KY // self.kq
        self.width = max(128, planes * KY)
        self.used = planes * KY
        self.pk = planes * self.kk
        self.lanes = self.kk * KZ
        self.lead = self.groups if (2 * self.jl) % 8 == 0 else 1
        width, jl = self.width, self.jl
        cos_x, sin_x = waves(KX, NX)
        cos_y, sin_y = waves(KY, NY)
        cos_z, sin_z = waves(KZ, NZ)
        forward = np.zeros((planes, NY, 2, width))
        for z in range(planes):
            forward[z, :, 0, z * KY : (z + 1) * KY] = cos_y.T
            forward[z, :, 1, z * KY : (z + 1) * KY] = -sin_y.T
        forward = forward.reshape(planes * NY, 2 * width)
        self.y_forward = forward
        self.y_inverse = forward.T
        table = np.zeros((self.groups, 2, jl, 2, NX))
        back = np.zeros((2, NX, self.groups, 2, jl))
        for j in range(KX):
            g, i = divmod(j, jl)
            table[g, 0, i, 0], table[g, 0, i, 1] = cos_x[j], sin_x[j]
            table[g, 1, i, 1], table[g, 1, i, 0] = cos_x[j], -sin_x[j]
            back[0, :, g, 0, i], back[0, :, g, 1, i] = cos_x[j], -sin_x[j]
            back[1, :, g, 1, i], back[1, :, g, 0, i] = cos_x[j], sin_x[j]
        self.x_forward = table.reshape(2 * KX, 2 * NX)
        self.x_inverse = back.reshape(2 * NX, 2 * KX)
        kk, pk, lanes = self.kk, self.pk, self.lanes
        zf = np.zeros((slabs, planes, kk, 2, kk, KZ))
        self.pw = max(128, pk)
        zi = np.zeros((slabs, 2, kk, KZ, 2, planes, kk))
        for s in range(slabs):
            for z in range(planes):
                c, n = cos_z[:, s * planes + z], sin_z[:, s * planes + z]
                for k in range(kk):
                    zf[s, z, k, 0, k], zf[s, z, k, 1, k] = c, n
                    zi[s, 0, k, :, 0, z, k], zi[s, 1, k, :, 0, z, k] = c, -n
                    zi[s, 1, k, :, 1, z, k], zi[s, 0, k, :, 1, z, k] = c, n
        self.z_forward = zf.reshape(slabs, pk, 2 * lanes)
        zi = zi.reshape(slabs, 2 * lanes, 2, pk)
        zi = np.pad(zi, ((0, 0), (0, 0), (0, 0), (0, self.pw - pk)))
        self.z_inverse = zi.reshape(slabs, 2 * lanes, 2 * self.pw)


def whole(shape):
    zeros = (0,) * len(shape)
    return pl.BlockSpec(shape, lambda *_: zeros)


def params(mib):
    return pltpu.CompilerParams(vmem_limit_bytes=mib * MIB)


def dot(a, b, **kw):
    return jnp.dot(a, b, preferred_element_type=F32, **kw)


def channel_modes(plan, planes_of, ty, tx):
    field = jnp.concatenate([planes_of(z) for z in range(plan.planes)], axis=1)
    along = dot(field, ty).astype(BF16)
    stacked = jnp.concatenate([along[:, : plan.width], along[:, plan.width :]], axis=0)
    return dot(tx, stacked)


def put_modes(plan, out_ref, c, value):
    if plan.lead == 1:
        out_ref[0, c] = value.astype(BF16)
    else:
        step = 2 * KX // plan.lead
        for g in range(plan.lead):
            out_ref[g, c] = value[g * step : (g + 1) * step].astype(BF16)


def get_modes(plan, ref, c):
    if plan.lead == 1:
        return ref[0, c]
    parts = [ref[g, c].astype(F32) for g in range(plan.lead)]
    return jnp.concatenate(parts, axis=0).astype(BF16)


def planes_kernel(plan, batch, x_ref, ty_ref, tx_ref, out_ref):
    for c in range(batch):
        value = channel_modes(plan, lambda z: x_ref[c, z], ty_ref[...], tx_ref[...])
        put_modes(plan, out_ref, c, value)


def planes_call(plan, field, ty, tx):
    channels, planes = field.shape[:2]
    batch = 4
    step = 2 * KX // plan.lead
    return pl.pallas_call(
        functools.partial(planes_kernel, plan, batch),
        grid=(channels // batch,),
        in_specs=[
            pl.BlockSpec((batch, planes, NX, NY), lambda i: (i, 0, 0, 0)),
            whole(ty.shape),
            whole(tx.shape),
        ],
        out_specs=pl.BlockSpec((plan.lead, batch, step, plan.width), lambda i: (0, i, 0, 0)),
        out_shape=jax.ShapeDtypeStruct((plan.lead, channels, step, plan.width), BF16),
        compiler_params=params(60),
        cost_estimate=pl.CostEstimate(
            flops=2 * channels * NX * planes * NY * 256, bytes_accessed=field.size * 2, transcendentals=0
        ),
        name="plane_modes",
    )(field, ty, tx)


def rims_kernel(low_ref, high_ref, first_ref, last_ref):
    first_ref[...] = low_ref[:, 0]
    last_ref[...] = high_ref[:, 0]


def rims_call(field):
    channels, planes = field.shape[:2]
    batch = 8
    rim = pl.BlockSpec((batch, NX, NY), lambda i: (i, 0, 0))
    shape = jax.ShapeDtypeStruct((channels, NX, NY), field.dtype)
    return pl.pallas_call(
        rims_kernel,
        grid=(channels // batch,),
        in_specs=[
            pl.BlockSpec((batch, 1, NX, NY), lambda i: (i, 0, 0, 0)),
            pl.BlockSpec((batch, 1, NX, NY), lambda i: (i, planes - 1, 0, 0)),
        ],
        out_specs=[rim, rim],
        out_shape=[shape, shape],
        compiler_params=params(60),
        name="rims",
    )(field, field)


def bands(taps_ref, c, adjoint, group, band_ref):
    row = lax.broadcasted_iota(jnp.int32, (NY, NY), 0)
    col = lax.broadcasted_iota(jnp.int32, (NY, NY), 1)
    diff = row - col
    for dz in range(3):
        for dx in range(3):
            base = 9 * dz + 3 * dx
            t = [taps_ref[base + i, c] for i in range(3)]
            if adjoint:
                t = t[::-1]
            band = jnp.where(
                diff == 0,
                t[1],
                jnp.where(diff == 1, t[2], jnp.where(diff == -1, t[0], 0.0)),
            ).astype(BF16)
            zi, xi = (2 - dz, 2 - dx) if adjoint else (dz, dx)
            for z in range(group):
                top = (xi * (group + 2) + z + zi) * NY
                band_ref[top : top + NY, z * NY : (z + 1) * NY] = band


def shifted(plan, x_ref, before_ref, after_ref, c, rows_ref):
    edge = lax.broadcasted_iota(jnp.int32, (NX, NY), 0)
    for i in range(plan.planes + 2):
        if before_ref is None and i in (0, plan.planes + 1):
            continue
        if i == 0:
            plane = before_ref[c]
        elif i == plan.planes + 1:
            plane = after_ref[c]
        else:
            plane = x_ref[c, i - 1]
        wide = plane.astype(F32)
        lower = jnp.where(edge == 0, 0.0, pltpu.roll(wide, 1, 0))
        upper = jnp.where(edge == NX - 1, 0.0, pltpu.roll(wide, NX - 1, 0))
        cols = slice(i * NY, (i + 1) * NY)
        rows_ref[0, :, cols] = lower.astype(BF16)
        rows_ref[1, :, cols] = plane
        rows_ref[2, :, cols] = upper.astype(BF16)


def stencil_kernel(plan, batch, adjoint, group, offset, *refs):
    if offset:
        refs = refs[1:]
    if adjoint:
        taps_ref, x_ref, out_ref, band_ref, rows_ref = refs
        before_ref = after_ref = None
    else:
        taps_ref, x_ref, before_ref, after_ref, out_ref, band_ref, rows_ref = refs

    @pl.when(pl.program_id(0) == 0)
    def _():
        band_ref[...] = jnp.zeros_like(band_ref)
        rows_ref[...] = jnp.zeros_like(rows_ref)

    first = pl.program_id(0) * batch + offset
    for c in range(batch):
        half = c % 2
        band, rows = band_ref.at[half], rows_ref.at[half]
        bands(taps_ref, first + c, adjoint, group, band)
        shifted(plan, x_ref, before_ref, after_ref, c, rows)
        for z in range(0, plan.planes, group):
            cols = slice(z * NY, (z + group + 2) * NY)
            near = jnp.concatenate([rows[d, :, cols] for d in range(3)], axis=1)
            total = dot(near, band[...])
            for i in range(group):
                out_ref[c, z + i] = total[:, i * NY : (i + 1) * NY].astype(BF16)


def stencil_call(plan, taps, field, rims, adjoint, done=None):
    channels, planes = field.shape[:2]
    batch = 4
    group = 2 if planes % 2 == 0 else 1
    offset = 0 if done is None else channels // 2
    skip = offset // batch
    block = pl.BlockSpec((batch, planes, NX, NY), lambda i: (i + skip, 0, 0, 0))
    specs = [pl.BlockSpec(memory_space=pltpu.SMEM), block]
    specs += [pl.BlockSpec((batch, NX, NY), lambda i: (i + skip, 0, 0))] * len(rims)
    operands = (taps, field, *rims)
    if done is not None:
        specs = [pl.BlockSpec(memory_space=pl.ANY)] + specs
        operands = (done,) + operands
    return pl.pallas_call(
        functools.partial(stencil_kernel, plan, batch, adjoint, group, offset),
        grid=(channels // 2 // batch,),
        in_specs=specs,
        out_specs=block,
        out_shape=jax.ShapeDtypeStruct(field.shape, BF16),
        input_output_aliases={} if done is None else {0: 0},
        scratch_shapes=[
            pltpu.VMEM((2, 3 * (group + 2) * NY, group * NY), BF16),
            pltpu.VMEM((2, 3, NX, (planes + 2) * NY), BF16),
        ],
        compiler_params=params(60),
        cost_estimate=pl.CostEstimate(
            flops=field.size * 3 * (group + 2) * NY, bytes_accessed=field.size * 2, transcendentals=0
        ),
        name="stencil_back" if adjoint else "stencil",
    )(*operands)


def final_kernel(plan, batch, taps_ref, x_ref, before_ref, after_ref, m_ref, tx_ref, ty_ref, out_ref):
    first = pl.program_id(0) * batch
    edge = lax.broadcasted_iota(jnp.int32, (NX, NY), 0)
    diff = lax.broadcasted_iota(jnp.int32, (NY, NY), 0) - lax.broadcasted_iota(jnp.int32, (NY, NY), 1)

    def rim(c, plane, dz):
        wide = plane.astype(F32)
        lower = jnp.where(edge == 0, 0.0, pltpu.roll(wide, 1, 0)).astype(BF16)
        upper = jnp.where(edge == NX - 1, 0.0, pltpu.roll(wide, NX - 1, 0)).astype(BF16)
        band = []
        for dx in (2, 1, 0):
            t = [taps_ref[9 * dz + 3 * dx + i, first + c] for i in range(3)]
            band.append(jnp.where(
                diff == 0,
                t[1],
                jnp.where(diff == 1, t[0], jnp.where(diff == -1, t[2], 0.0)),
            ).astype(BF16))
        return dot(jnp.concatenate([lower, plane, upper], axis=1), jnp.concatenate(band, axis=0))

    for c in range(batch):
        wave = dot(tx_ref[...], get_modes(plan, m_ref, c)).astype(BF16)
        wave = jnp.concatenate([wave[:NX], wave[NX:]], axis=1)
        full = dot(wave, ty_ref[...])
        for z in range(plan.planes):
            total = full[:, z * NY : (z + 1) * NY] + x_ref[c, z].astype(F32)
            if z == 0:
                total = total + rim(c, before_ref[c], 2)
            if z == plan.planes - 1:
                total = total + rim(c, after_ref[c], 0)
            out_ref[c, z] = total.astype(BF16)


def final_call(plan, taps, partial, before, after, modes, tx, ty):
    channels, planes = partial.shape[:2]
    batch = 4
    block = pl.BlockSpec((batch, planes, NX, NY), lambda i: (i, 0, 0, 0))
    rim = pl.BlockSpec((batch, NX, NY), lambda i: (i, 0, 0))
    return pl.pallas_call(
        functools.partial(final_kernel, plan, batch),
        grid=(channels // batch,),
        in_specs=[
            pl.BlockSpec(memory_space=pltpu.SMEM),
            block,
            rim,
            rim,
            pl.BlockSpec((modes.shape[0], batch) + modes.shape[2:], lambda i: (0, i, 0, 0)),
            whole(tx.shape),
            whole(ty.shape),
        ],
        out_specs=block,
        out_shape=jax.ShapeDtypeStruct(partial.shape, BF16),
        compiler_params=params(60),
        cost_estimate=pl.CostEstimate(
            flops=2 * partial.size * 512, bytes_accessed=partial.size * 4, transcendentals=0
        ),
        name="final",
    )(taps, partial, before, after, modes, tx, ty)


def mix_kernel(plan, channels, adjoint, scale_in, scale_out, r_ref, zf_ref, zi_ref, w_ref,
               out_ref, turned_ref, z_scr, s_scr, m_scr, o_scr):
    jl, lanes, pk, pw = plan.jl, plan.lanes, plan.pk, plan.pw
    chunks = 2 * lanes // 128
    total = None
    for s in range(plan.slabs):
        part = dot(r_ref[s].astype(F32), zf_ref[s], precision=HIGHEST)
        total = part if total is None else total + part
    total = total * scale_in
    for q in range(chunks):
        z_scr[q] = total[:, q * 128 : (q + 1) * 128]

    def rows_of(start):
        return jnp.concatenate(
            [z_scr[q, pl.ds(start, channels, stride=2 * jl), :] for q in range(chunks)], axis=1)

    for j in range(jl):
        re, im = rows_of(j), rows_of(jl + j)
        real = re[:, :lanes] + im[:, lanes:]
        imag = im[:, :lanes] - re[:, lanes:]
        s_scr[j, 0] = real
        s_scr[j, 1] = imag
        both = jnp.concatenate([real, imag], axis=0)
        turned_ref[j * lanes : (j + 1) * lanes, :] = both.T.astype(BF16)
        cols = slice(j * lanes, (j + 1) * lanes)
        rows = slice(j * channels, (j + 1) * channels)
        if adjoint:
            for c in range(channels):
                wr = w_ref[0, c, :, cols].astype(F32)
                wi = w_ref[1, c, :, cols].astype(F32)
                br = jnp.sum(wr * real + wi * imag, axis=0, keepdims=True)
                bi = jnp.sum(wr * imag - wi * real, axis=0, keepdims=True)
                m_scr[j * channels + c : j * channels + c + 1, :lanes] = br
                m_scr[j * channels + c : j * channels + c + 1, lanes:] = bi
        else:
            mr = jnp.zeros((channels, lanes), F32)
            mi = jnp.zeros((channels, lanes), F32)
            for c in range(channels):
                wr = w_ref[0, c, :, cols].astype(F32)
                wi = w_ref[1, c, :, cols].astype(F32)
                sr = s_scr[j, 0, c : c + 1, :]
                si = s_scr[j, 1, c : c + 1, :]
                mr = mr + (sr * wr - si * wi)
                mi = mi + (sr * wi + si * wr)
            m_scr[rows, :lanes] = mr
            m_scr[rows, lanes:] = mi
    mixed = m_scr[...] * scale_out
    for s in range(plan.slabs):
        planar = dot(mixed, zi_ref[s], precision=HIGHEST)
        for j in range(jl):
            for part in range(2):
                o_scr[pl.ds(part * jl + j, channels, stride=2 * jl), :] = planar[
                    j * channels : (j + 1) * channels, part * pw : (part + 1) * pw
                ]
        out_ref[s] = o_scr[:, :pk].astype(BF16)


def mix_call(plan, received, weights, zf, zi, adjoint, scale_in, scale_out):
    channels = weights.shape[1]
    rows = channels * 2 * plan.jl
    modes = plan.jl * plan.lanes
    return pl.pallas_call(
        functools.partial(mix_kernel, plan, channels, adjoint, scale_in, scale_out),
        out_shape=(
            jax.ShapeDtypeStruct((plan.slabs, rows, plan.pk), BF16),
            jax.ShapeDtypeStruct((modes, 2 * channels), BF16),
        ),
        scratch_shapes=[
            pltpu.VMEM((2 * plan.lanes // 128, rows, 128), F32),
            pltpu.VMEM((plan.jl, 2, channels, plan.lanes), F32),
            pltpu.VMEM((plan.jl * channels, 2 * plan.lanes), F32),
            pltpu.VMEM((rows, plan.pw), F32),
        ],
        compiler_params=params(60),
        name="mix_back" if adjoint else "mix",
    )(received, zf, zi, weights)


def middle_kernel(plan, channels, g_ref, sm_ref, cot_ref, m_ref, bias_ref, pw_ref, pt_ref,
                  txi_ref, tyi_ref, ty_ref, tx_ref,
                  spread_ref, first_ref, last_ref, modes_ref, wave_scr, delta_scr, move_scr, kp_ref, kt_ref):
    z = pl.program_id(0)
    planes = plan.planes
    width = plan.width

    @pl.when(z == 0)
    def _():
        def body(c, carry):
            wave = dot(txi_ref[...], get_modes(plan, m_ref, c)).astype(BF16)
            wave_scr[c, :, :width] = wave[:NX]
            wave_scr[c, :, width:] = wave[NX:]
            return carry
        lax.fori_loop(0, channels, body, 0, unroll=4)
        rows = channels * 16
        pick = lax.broadcasted_iota(jnp.int32, (rows, channels), 0) >> 4
        pick = pick == lax.broadcasted_iota(jnp.int32, (rows, channels), 1)
        pick = jnp.where(pick, 1.0, 0.0).astype(BF16)
        same = lax.broadcasted_iota(jnp.int32, (rows, rows), 0) & 15
        same = same == (lax.broadcasted_iota(jnp.int32, (rows, rows), 1) & 15)
        for src, dst in ((pt_ref, kp_ref), (pw_ref, kt_ref)):
            tall = dot(pick, src[...]).astype(BF16)
            full = lax.dot_general(tall, pick, (((1,), (1,)), ((), ())), preferred_element_type=F32)
            dst[...] = jnp.where(same, full, 0.0).astype(BF16)

    g = g_ref[0]
    row = lax.broadcasted_iota(jnp.int32, (NX, NY), 0)
    col = lax.broadcasted_iota(jnp.int32, (NX, NY), 1)

    def differs(shift, axis, inside):
        return jnp.where((g != pltpu.roll(g, shift, axis)) & inside, 0.25, 0.0)

    move_scr[...] = (
        0.25
        + differs(1, 0, row > 0)
        + differs(NX - 1, 0, row < NX - 1)
        + differs(1, 1, col > 0)
        + differs(NY - 1, 1, col < NY - 1)
    )
    height = channels * 16
    bias = bias_ref[...]

    def body(pair, carry):
        starts = [pair * 32 + 16 * i for i in range(2)]

        def tile(ref):
            return [ref[:, 0, pl.ds(x, 16), :].reshape(height, NY) for x in starts]

        mixed = dot(kp_ref[...], jnp.concatenate(tile(sm_ref), axis=1))
        cot = tile(cot_ref)
        deltas = []
        for i, x in enumerate(starts):
            moving = move_scr[pl.ds(x, 16), :]
            wave = wave_scr[:, pl.ds(x, 16), :].reshape(height, 2 * width)
            spectral = dot(wave, tyi_ref[...])
            local = mixed[:, i * NY : (i + 1) * NY].reshape(channels, 16, NY) * moving[None]
            pre = spectral.reshape(channels, 16, NY) + local + bias
            gate = 0.5 + 0.5 * jnp.tanh(0.5 * pre)
            delta = cot[i].astype(F32).reshape(channels, 16, NY) * gate * (1.0 + pre * (1.0 - gate))
            delta = delta.astype(BF16)
            delta_scr[:, z, pl.ds(x, 16), :] = delta
            deltas.append(delta.reshape(height, NY))
        turned = dot(kt_ref[...], jnp.concatenate(deltas, axis=1))
        for i, x in enumerate(starts):
            moving = move_scr[pl.ds(x, 16), :]
            value = turned[:, i * NY : (i + 1) * NY].reshape(channels, 16, NY) * moving[None]
            spread_ref[:, 0, pl.ds(x, 16), :] = value.astype(BF16)
        return carry

    for pair in range(NX // 32):
        body(pair, 0)

    @pl.when(z == 0)
    def _():
        first_ref[...] = spread_ref[:, 0]

    @pl.when(z == planes - 1)
    def _():
        last_ref[...] = spread_ref[:, 0]

        def body(i, carry):
            for c in (2 * i, 2 * i + 1):
                value = channel_modes(plan, lambda p: delta_scr[c, p], ty_ref[...], tx_ref[...])
                put_modes(plan, modes_ref, c, value)
            return carry

        lax.fori_loop(0, channels // 2, body, 0)


def middle_call(plan, grains, smooth, cotangent, modes, bias, kp, kt, txi, tyi, ty, tx):
    channels, planes = smooth.shape[:2]
    width = plan.width
    block = pl.BlockSpec((channels, 1, NX, NY), lambda z: (0, z, 0, 0))
    rim = jax.ShapeDtypeStruct((channels, NX, NY), BF16)
    return pl.pallas_call(
        functools.partial(middle_kernel, plan, channels),
        grid=(planes,),
        in_specs=[
            pl.BlockSpec((1, NX, NY), lambda z: (z, 0, 0)),
            block,
            block,
            whole(modes.shape),
            whole((channels, 1, 1)),
            whole(kp.shape),
            whole(kt.shape),
            whole(txi.shape),
            pl.BlockSpec((2 * width, NY), lambda z: (0, z)),
            whole(ty.shape),
            whole(tx.shape),
        ],
        out_specs=[block, whole(rim.shape), whole(rim.shape), whole(modes.shape)],
        out_shape=[jax.ShapeDtypeStruct(smooth.shape, BF16), rim, rim,
                   jax.ShapeDtypeStruct(modes.shape, BF16)],
        scratch_shapes=[
            pltpu.VMEM((channels, NX, 2 * width), BF16),
            pltpu.VMEM((channels, planes, NX, NY), BF16),
            pltpu.VMEM((NX, NY), F32),
            pltpu.VMEM((16 * channels, 16 * channels), BF16),
            pltpu.VMEM((16 * channels, 16 * channels), BF16),
        ],
        compiler_params=params(60),
        name="middle",
    )(grains, smooth, cotangent, modes, bias.reshape(channels, 1, 1), kp, kt, txi, tyi, ty, tx)


def grad_kernel(samples, both_ref, e_ref, out_ref):
    total = None
    for i in range(samples):
        half = both_ref.shape[-1] // 2
        spec, dual = both_ref[i, :, :half], both_ref[i, :, half:]
        term = dot(spec, e_ref[0]) * dot(dual, e_ref[1]) + dot(spec, e_ref[2]) * dot(dual, e_ref[3])
        total = term if total is None else total + term
    out_ref[...] = total


def grad_call(both, pick):
    samples, modes, width = both.shape
    columns = pick.shape[-1]
    batch = min(256, modes)
    return pl.pallas_call(
        functools.partial(grad_kernel, samples),
        grid=(modes // batch,),
        in_specs=[
            pl.BlockSpec((samples, batch, width), lambda i: (0, i, 0)),
            whole(pick.shape),
        ],
        out_specs=pl.BlockSpec((batch, columns), lambda i: (i, 0)),
        out_shape=jax.ShapeDtypeStruct((modes, columns), F32),
        compiler_params=params(60),
        cost_estimate=pl.CostEstimate(
            flops=8 * samples * modes * width * columns, bytes_accessed=modes * columns * 4, transcendentals=0
        ),
        name="grad_modes",
    )(both, pick)


def slab_peer(me, d, slabs):
    return lax.rem(me + d, slabs)


def enter(sizes):
    barrier = pltpu.get_barrier_semaphore()
    total = 0
    for axis, size in sizes.items():
        me = lax.axis_index(axis)
        for d in range(1, size):
            pl.semaphore_signal(
                barrier, inc=1, device_id={axis: slab_peer(me, d, size)}, device_id_type=pl.DeviceIdType.MESH)
        total += size - 1
    pl.semaphore_wait(barrier, total)


def exchange(me, slabs, send_ref, recv_ref, send_sem, recv_sem):
    copies = []
    for d in range(1, slabs):
        peer = slab_peer(me, d, slabs)
        copies.append(pltpu.make_async_remote_copy(
            src_ref=send_ref.at[peer],
            dst_ref=recv_ref.at[me],
            send_sem=send_sem.at[d - 1],
            recv_sem=recv_sem.at[d - 1],
            device_id={"slab": peer},
            device_id_type=pl.DeviceIdType.MESH,
        ))
    return copies


def halo_copies(me, slabs, field_ref, before_ref, after_ref, planes, chunk, index, send_sem, recv_sem):
    rows = pl.ds(index * chunk, chunk)
    up = pltpu.make_async_remote_copy(
        src_ref=field_ref.at[rows, planes - 1],
        dst_ref=before_ref.at[rows],
        send_sem=send_sem.at[0, index],
        recv_sem=recv_sem.at[0, index],
        device_id={"slab": lax.rem(me + 1, slabs)},
        device_id_type=pl.DeviceIdType.MESH,
    )
    down = pltpu.make_async_remote_copy(
        src_ref=field_ref.at[rows, 0],
        dst_ref=after_ref.at[rows],
        send_sem=send_sem.at[1, index],
        recv_sem=recv_sem.at[1, index],
        device_id={"slab": lax.rem(me + slabs - 1, slabs)},
        device_id_type=pl.DeviceIdType.MESH,
    )
    return up, down


def halo_start(me, slabs, copies):
    up, down = copies

    @pl.when(me < slabs - 1)
    def _():
        up.start()

    @pl.when(me > 0)
    def _():
        down.start()


def halo_wait_recv(me, slabs, copies):
    up, down = copies

    @pl.when(me > 0)
    def _():
        up.wait_recv()

    @pl.when(me < slabs - 1)
    def _():
        down.wait_recv()


def halo_wait_send(me, slabs, copies):
    up, down = copies

    @pl.when(me < slabs - 1)
    def _():
        up.wait_send()

    @pl.when(me > 0)
    def _():
        down.wait_send()


def batch_modes(plan, out_ref, row, lines, ty_ref, tx_ref):
    count = len(lines)
    along = dot(jnp.concatenate(lines, axis=0), ty_ref[...]).astype(BF16)
    width = plan.width
    values = []
    for c in range(0, count, 2):
        top = along[c * NX : (c + 1) * NX]
        low = along[(c + 1) * NX : (c + 2) * NX]
        pair = jnp.concatenate([
            jnp.concatenate([top[:, :width], low[:, :width]], axis=1),
            jnp.concatenate([top[:, width:], low[:, width:]], axis=1),
        ], axis=0)
        both = dot(tx_ref[...], pair)
        values += [both[:, :width], both[:, width:]]
    step = 2 * KX // plan.lead
    for g in range(plan.lead):
        part = jnp.concatenate([v[g * step : (g + 1) * step] for v in values], axis=0)
        out_ref[g, pl.ds(row, count * step), :] = part.astype(BF16)


def band_masks():
    diff = lax.broadcasted_iota(jnp.int32, (NY, NY), 0) - lax.broadcasted_iota(jnp.int32, (NY, NY), 1)
    return diff == 1, diff == 0, diff == -1


def fill_band(taps_ref, c, adjoint, masks, band_ref):
    low, mid, upp = masks
    for dz in range(3):
        for dx in range(3):
            base = 9 * dz + 3 * dx
            t = [taps_ref[base + i, c] for i in range(3)]
            if adjoint:
                t = t[::-1]
            band = jnp.where(mid, t[1], jnp.where(low, t[2], jnp.where(upp, t[0], 0.0))).astype(BF16)
            zi, xi = (2 - dz, 2 - dx) if adjoint else (dz, dx)
            for z in range(2):
                top = (xi * 4 + z + zi) * NY
                band_ref[top : top + NY, z * NY : (z + 1) * NY] = band


def stencil_part(plan, taps_ref, x_ref, before_ref, after_ref, c, groups, adjoint, masks, out_ref,
                 band_ref, wide_ref, lower_ref, upper_ref):
    fill_band(taps_ref, c, adjoint, masks, band_ref)
    planes = plan.planes

    def plane(i):
        if i == 0:
            return before_ref[c]
        if i == planes + 1:
            return after_ref[c]
        return x_ref[c, i - 1]

    needed = sorted({2 * g + i for g in groups for i in range(4)})
    slot = {i: n for n, i in enumerate(needed)}
    for i in needed:
        n = slot[i]
        wide_ref[n, 8 : NX + 8, :] = plane(i).astype(F32)
        lower_ref[n] = wide_ref[n, 7 : NX + 7, :].astype(BF16)
        upper_ref[n] = wide_ref[n, 9 : NX + 9, :].astype(BF16)

    def moved(dx, i):
        if dx == 1:
            return plane(i)
        return (lower_ref if dx == 0 else upper_ref)[slot[i]]

    near = jnp.concatenate([
        jnp.concatenate([moved(dx, 2 * g + i) for dx in range(3) for i in range(4)], axis=1)
        for g in groups
    ], axis=0)
    total = dot(near, band_ref[...])
    for n, g in enumerate(groups):
        for i in range(2):
            out_ref[c, 2 * g + i] = total[n * NX : (n + 1) * NX, i * NY : (i + 1) * NY].astype(BF16)


def mix_modes(plan, channels, me, adjoint, scale_in, scale_out, own_ref, r_ref, zf_ref, zi_ref, w_ref,
              out_ref, turned_ref, z_scr, s_scr, m_scr, o_scr):
    jl, lanes, pk, pw = plan.jl, plan.lanes, plan.pk, plan.pw
    chunks = 2 * lanes // 128
    r_ref[me] = own_ref[me]
    total = dot(jnp.concatenate([r_ref[s] for s in range(plan.slabs)], axis=1), zf_ref[...])
    total = total * scale_in
    for q in range(chunks):
        z_scr[q] = total[:, q * 128 : (q + 1) * 128]

    def rows_of(start):
        return jnp.concatenate(
            [z_scr[q, pl.ds(start, channels, stride=2 * jl), :] for q in range(chunks)], axis=1)

    for j in range(jl):
        re, im = rows_of(j), rows_of(jl + j)
        real = re[:, :lanes] + im[:, lanes:]
        imag = im[:, :lanes] - re[:, lanes:]
        s_scr[j, 0] = real
        s_scr[j, 1] = imag
        both = jnp.concatenate([real, imag], axis=0)
        turned_ref[j * lanes : (j + 1) * lanes, :] = both.T.astype(BF16)
        cols = slice(j * lanes, (j + 1) * lanes)
        rows = slice(j * channels, (j + 1) * channels)
        if adjoint:
            def body(i, carry):
                parts = []
                for k in range(8):
                    c = 8 * i + k
                    wr = w_ref[0, c, :, cols].astype(F32)
                    wi = w_ref[1, c, :, cols].astype(F32)
                    real, imag = s_scr[j, 0], s_scr[j, 1]
                    br = jnp.sum(wr * real + wi * imag, axis=0, keepdims=True)
                    bi = jnp.sum(wr * imag - wi * real, axis=0, keepdims=True)
                    parts.append(jnp.concatenate([br, bi], axis=1))
                m_scr[pl.ds(pl.multiple_of(j * channels + 8 * i, 8), 8), :] = jnp.concatenate(parts, axis=0)
                return carry
            lax.fori_loop(0, channels // 8, body, 0)
        else:
            def body(i, carry):
                mr, mi = carry
                for k in range(8):
                    c = 8 * i + k
                    wr = w_ref[0, c, :, cols].astype(F32)
                    wi = w_ref[1, c, :, cols].astype(F32)
                    sr = s_scr[j, 0, pl.ds(c, 1), :]
                    si = s_scr[j, 1, pl.ds(c, 1), :]
                    mr = mr + (sr * wr - si * wi)
                    mi = mi + (sr * wi + si * wr)
                return mr, mi
            zero = jnp.zeros((channels, lanes), F32)
            mr, mi = lax.fori_loop(0, channels // 8, body, (zero, zero))
            m_scr[rows, :lanes] = mr
            m_scr[rows, lanes:] = mi
    mixed = (m_scr[...] * scale_out).astype(BF16)
    for s in range(plan.slabs):
        planar = dot(mixed, zi_ref[s])
        for j in range(jl):
            for part in range(2):
                o_scr[pl.ds(part * jl + j, channels, stride=2 * jl), :] = planar[
                    j * channels : (j + 1) * channels, part * pw : (part + 1) * pw
                ]
        out_ref[s] = o_scr[:, :pk].astype(BF16)


def mobility(g_ref, z, move_ref):
    row = lax.broadcasted_iota(jnp.int32, (NX, NY), 0)
    col = lax.broadcasted_iota(jnp.int32, (NX, NY), 1)
    for i in range(2):
        g = g_ref[z + i]

        def differs(shift, axis, inside):
            return jnp.where((g != pltpu.roll(g, shift, axis)) & inside, 0.25, 0.0)

        move_ref[i] = (
            0.25
            + differs(1, 0, row > 0)
            + differs(NX - 1, 0, row < NX - 1)
            + differs(1, 1, col > 0)
            + differs(NY - 1, 1, col < NY - 1)
        )


def spread_weights(channels, src_ref, dst_ref):
    rows = channels * 16
    pick = lax.broadcasted_iota(jnp.int32, (rows, channels), 0) >> 4
    pick = pick == lax.broadcasted_iota(jnp.int32, (rows, channels), 1)
    pick = jnp.where(pick, 1.0, 0.0).astype(BF16)
    same = lax.broadcasted_iota(jnp.int32, (rows, rows), 0) & 15
    same = same == (lax.broadcasted_iota(jnp.int32, (rows, rows), 1) & 15)
    tall = dot(pick, src_ref[...]).astype(BF16)
    full = lax.dot_general(tall, pick, (((1,), (1,)), ((), ())), preferred_element_type=F32)
    dst_ref[...] = jnp.where(same, full, 0.0).astype(BF16)


def gate_pair(plan, channels, z, g_ref, sm_ref, cot_ref, wave_ref, tyi_ref, kp_ref, kt_ref, bias_ref, move_ref):
    mobility(g_ref, z, move_ref)
    height = channels * 16
    bias = bias_ref[...]
    for k in range(NX // 16):
        rows = pl.ds(k * 16, 16)

        def tile(ref, n):
            return ref[:, z + n, rows, :].reshape(height, NY)

        mixed = dot(kp_ref[...], jnp.concatenate([tile(sm_ref, 0), tile(sm_ref, 1)], axis=1))
        wave = wave_ref[:, rows, :].reshape(height, 2 * plan.width)
        spectral = dot(wave, tyi_ref[z // 2])
        deltas = []
        for n in range(2):
            cols = slice(n * NY, (n + 1) * NY)
            moving = move_ref[n, rows, :]
            local = mixed[:, cols].reshape(channels, 16, NY) * moving[None]
            pre = spectral[:, cols].reshape(channels, 16, NY) + local + bias
            half = 0.5 * jnp.tanh(0.5 * pre)
            delta = tile(cot_ref, n).astype(F32).reshape(channels, 16, NY) * (0.5 + half) * (1.0 + pre * (0.5 - half))
            delta = delta.astype(BF16)
            cot_ref[:, z + n, rows, :] = delta
            deltas.append(delta.reshape(height, NY))
        turned = dot(kt_ref[...], jnp.concatenate(deltas, axis=1))
        for n in range(2):
            cols = slice(n * NY, (n + 1) * NY)
            value = turned[:, cols].reshape(channels, 16, NY) * move_ref[n, rows, :][None]
            sm_ref[:, z + n, rows, :] = value.astype(BF16)


def pair_waves(plan, read, tx_ref):
    width = plan.width
    pair = jnp.concatenate([
        jnp.concatenate([read(g, k).astype(F32) for g in range(plan.lead)], axis=0) for k in range(2)
    ], axis=1).astype(BF16)
    wave = dot(tx_ref[...], pair).astype(BF16)
    found = []
    for k in range(2):
        cols = slice(k * width, (k + 1) * width)
        found.append(jnp.concatenate([wave[:NX, cols], wave[NX:, cols]], axis=1))
    return found


def layer_kernel(plan, channels, peers, cell_scale, mode_scale,
                 taps_ref, x_hbm, cot_hbm, w_hbm, g_ref, bias_ref, pw_ref, pt_ref,
                 ty_ref, tx_ref, tyi_ref, txi_ref, zf_ref, zi_ref,
                 partial_hbm, back_ref, gather_ref,
                 x_ref, y_ref, cot_ref, w_ref, before_ref, after_ref, before2_ref, after2_ref,
                 send1, recv1, send2, recv2, send3, recv3, send4, wave_ref, kp_ref, kt_ref, move_ref,
                 spec_ref, dual_ref, both_ref,
                 band_ref, wide_ref, lower_ref, upper_ref, z_scr, s_scr, m_scr, o_scr,
                 load_sem, cot_sem, w_sem, store_sem, halo_send, halo_recv, send_sem, recv_sem, both_send, both_recv):
    planes, slabs = plan.planes, plan.slabs
    me = lax.axis_index("slab")
    lane = lax.axis_index("dp")
    chunk = 8
    chunks = channels // chunk
    step = 2 * KX // plan.lead
    pairs = planes // 2
    inner, outer = list(range(1, pairs - 1)), [0, pairs - 1]

    def load(i):
        rows = pl.ds(i * chunk, chunk)
        return pltpu.make_async_copy(x_hbm.at[rows], x_ref.at[rows], load_sem.at[i])

    for i in range(chunks):
        load(i).start()
    enter({"slab": slabs, "dp": peers})
    halos = [halo_copies(me, slabs, x_hbm, before_ref, after_ref, planes, chunk, i, halo_send.at[0], halo_recv.at[0])
             for i in range(chunks)]
    halo_start(me, slabs, halos[0])
    load_w = pltpu.make_async_copy(w_hbm, w_ref, w_sem)
    load_w.start()
    load_cot = pltpu.make_async_copy(cot_hbm, cot_ref, cot_sem)
    load_cot.start()

    @pl.when(me == 0)
    def _():
        before_ref[...] = jnp.zeros_like(before_ref)
        before2_ref[...] = jnp.zeros_like(before2_ref)

    @pl.when(me == slabs - 1)
    def _():
        after_ref[...] = jnp.zeros_like(after_ref)
        after2_ref[...] = jnp.zeros_like(after2_ref)

    band_ref[...] = jnp.zeros_like(band_ref)
    for u in range(4):
        for n in range(wide_ref.shape[1]):
            wide_ref[u, n, 0:8, :] = jnp.zeros((8, NY), F32)
            wide_ref[u, n, NX + 8 : NX + 16, :] = jnp.zeros((8, NY), F32)
    spread_weights(channels, pt_ref, kp_ref)
    spread_weights(channels, pw_ref, kt_ref)

    def spectra(src_ref, out_ref):
        def body(i, carry):
            if src_ref is x_ref:
                load(i).wait()
            lines = [jnp.concatenate([src_ref[i * chunk + c, z] for z in range(planes)], axis=1) for c in range(chunk)]
            batch_modes(plan, out_ref, pl.multiple_of(i * chunk * step, chunk * step), lines, ty_ref, tx_ref)
            return carry
        lax.fori_loop(0, chunks, body, 0)

    spectra(x_ref, send1)
    first = exchange(me, slabs, send1, recv1, send_sem.at[0], recv_sem.at[0])
    for copy in first:
        copy.start()
    halo_start(me, slabs, halos[1])

    masks = band_masks()

    def stencil(groups, adjoint):
        src, dst = (y_ref, x_ref) if adjoint else (x_ref, y_ref)
        low, high = (before2_ref, after2_ref) if adjoint else (before_ref, after_ref)

        def body(i, carry):
            for u in range(4):
                stencil_part(plan, taps_ref, src, low, high, i * 4 + u, groups, adjoint, masks, dst,
                             band_ref.at[u], wide_ref.at[u], lower_ref.at[u], upper_ref.at[u])
            return carry
        return body

    def gates(start, stride):
        def body(i, carry):
            gate_pair(plan, channels, 2 * (start + stride * i), g_ref, y_ref, cot_ref, wave_ref, tyi_ref,
                      kp_ref, kt_ref, bias_ref, move_ref)
            return carry
        return body

    lax.fori_loop(0, channels // 4, stencil(inner, False), 0)
    load_w.wait()
    for copy in first:
        copy.wait()
    mix_modes(plan, channels, me, False, cell_scale, mode_scale, send1, recv1, zf_ref, zi_ref, w_ref,
              send2, spec_ref, z_scr, s_scr, m_scr, o_scr)
    second = exchange(me, slabs, send2, recv2, send_sem.at[1], recv_sem.at[1])
    for copy in second:
        copy.start()
    for copies in halos[2:]:
        halo_start(me, slabs, copies)
    recv2[me] = send2[me]
    edge = stencil(outer, False)
    for i in range(2):
        halo_wait_recv(me, slabs, halos[i])
        lax.fori_loop(2 * i, 2 * i + 2, edge, 0)
    load_cot.wait()
    for copy in second:
        copy.wait()

    def unfold(i, carry):
        for k in range(0, 8, 2):
            c = i * 8 + k
            found = pl.ds(pl.multiple_of(c * step, 2 * step), 2 * step)
            for n, wave in enumerate(pair_waves(
                    plan, lambda g, j: recv2[g, found, :][j * step : (j + 1) * step], txi_ref)):
                wave_ref[c + n] = wave
        return carry

    lax.fori_loop(0, channels // 8, unfold, 0)
    lax.fori_loop(0, pairs - 2, gates(1, 1), 0)
    for i in range(2, chunks):
        halo_wait_recv(me, slabs, halos[i])
        lax.fori_loop(2 * i, 2 * i + 2, edge, 0)
    lax.fori_loop(0, 2, gates(0, pairs - 1), 0)

    turns = [halo_copies(me, slabs, y_ref, before2_ref, after2_ref, planes, chunk, i, halo_send.at[1], halo_recv.at[1])
             for i in range(chunks)]
    halo_start(me, slabs, turns[0])
    spectra(cot_ref, send3)
    third = exchange(me, slabs, send3, recv3, send_sem.at[2], recv_sem.at[2])
    for copy in third:
        copy.start()
    halo_start(me, slabs, turns[1])
    lax.fori_loop(0, channels // 4, stencil(inner, True), 0)
    for copy in third:
        copy.wait()
    mix_modes(plan, channels, me, True, mode_scale, cell_scale, send3, recv3, zf_ref, zi_ref, w_ref,
              send4, dual_ref, z_scr, s_scr, m_scr, o_scr)
    fourth = exchange(me, slabs, send4, back_ref, send_sem.at[3], recv_sem.at[3])
    for copy in fourth:
        copy.start()
    for copies in turns[2:]:
        halo_start(me, slabs, copies)
    back_ref[me] = send4[me]
    both_ref[...] = jnp.concatenate([spec_ref[...], dual_ref[...]], axis=1)
    shares = []
    for d in range(1, peers):
        shares.append(pltpu.make_async_remote_copy(
            src_ref=both_ref,
            dst_ref=gather_ref.at[lane],
            send_sem=both_send.at[d - 1],
            recv_sem=both_recv.at[d - 1],
            device_id={"dp": slab_peer(lane, d, peers)},
            device_id_type=pl.DeviceIdType.MESH,
        ))
    for copy in shares:
        copy.start()
    gather_ref[lane] = both_ref[...]

    def store(i):
        rows = pl.ds(i * chunk, chunk)
        return pltpu.make_async_copy(x_ref.at[rows], partial_hbm.at[rows], store_sem.at[i])

    edge = stencil(outer, True)
    for i in range(chunks):
        halo_wait_recv(me, slabs, turns[i])
        lax.fori_loop(2 * i, 2 * i + 2, edge, 0)
        store(i).start()
    for copy in fourth + shares:
        copy.wait()
    for copies in halos + turns:
        halo_wait_send(me, slabs, copies)
    for i in range(chunks):
        store(i).wait()


def layer_call(plan, taps, field, cotangent, weights, grains, bias, point, ty, tx, tyi, txi, zf, zi,
               cell_scale, mode_scale, peers):
    channels, planes = field.shape[:2]
    slabs = plan.slabs
    rows = channels * 2 * plan.jl
    modes = plan.jl * plan.lanes
    whole_vmem = pl.BlockSpec(memory_space=pltpu.VMEM)
    anywhere = pl.BlockSpec(memory_space=pl.ANY)
    chunks = channels // 8
    block = pltpu.VMEM((slabs, rows, plan.pk), BF16)
    rim = pltpu.VMEM((channels, NX, NY), BF16)
    wide = pltpu.VMEM((16 * channels, 16 * channels), BF16)
    dma = pltpu.SemaphoreType.DMA
    tyi = tyi.reshape(2 * plan.width, planes // 2, 2 * NY).transpose(1, 0, 2)
    return pl.pallas_call(
        functools.partial(layer_kernel, plan, channels, peers, cell_scale, mode_scale),
        in_specs=[pl.BlockSpec(memory_space=pltpu.SMEM)] + [anywhere] * 3 + [whole_vmem] * 10,
        out_specs=[anywhere, whole_vmem, whole_vmem],
        out_shape=[
            jax.ShapeDtypeStruct(field.shape, BF16),
            jax.ShapeDtypeStruct((slabs, rows, plan.pk), BF16),
            jax.ShapeDtypeStruct((peers, modes, 4 * channels), BF16),
        ],
        scratch_shapes=[
            pltpu.VMEM(field.shape, BF16),
            pltpu.VMEM(field.shape, BF16),
            pltpu.VMEM(field.shape, BF16),
            pltpu.VMEM(weights.shape, BF16),
            rim, rim, rim, rim,
            block, block, block, block, block, block, block,
            pltpu.VMEM((channels, NX, 2 * plan.width), BF16),
            wide, wide,
            pltpu.VMEM((2, NX, NY), F32),
            pltpu.VMEM((modes, 2 * channels), BF16),
            pltpu.VMEM((modes, 2 * channels), BF16),
            pltpu.VMEM((modes, 4 * channels), BF16),
            pltpu.VMEM((4, 12 * NY, 2 * NY), BF16),
            pltpu.VMEM((4, 8, NX + 16, NY), F32),
            pltpu.VMEM((4, 8, NX, NY), BF16),
            pltpu.VMEM((4, 8, NX, NY), BF16),
            pltpu.VMEM((2 * plan.lanes // 128, rows, 128), F32),
            pltpu.VMEM((plan.jl, 2, channels, plan.lanes), F32),
            pltpu.VMEM((plan.jl * channels, 2 * plan.lanes), F32),
            pltpu.VMEM((rows, plan.pw), F32),
            dma((chunks,)), dma, dma, dma((chunks,)),
            dma((2, 2, chunks)), dma((2, 2, chunks)),
            dma((4, slabs - 1)), dma((4, slabs - 1)),
            dma((peers - 1,)), dma((peers - 1,)),
        ],
        compiler_params=pltpu.CompilerParams(
            vmem_limit_bytes=62 * MIB, collective_id=0, has_side_effects=True),
        name="layer",
    )(taps, field, cotangent, weights, grains, bias.reshape(channels, 1, 1), point, point.T, ty, tx, tyi, txi, zf, zi)


def close_kernel(plan, batch, x_ref, m_ref, tx_ref, ty_ref, out_ref):
    waves_of = []
    for c in range(0, batch, 2):
        waves_of += pair_waves(plan, lambda g, k: m_ref[g, c + k], tx_ref)
    full = dot(jnp.concatenate(waves_of, axis=0), ty_ref[...])
    for c in range(batch):
        for z in range(plan.planes):
            total = full[c * NX : (c + 1) * NX, z * NY : (z + 1) * NY] + x_ref[c, z].astype(F32)
            out_ref[c, z] = total.astype(BF16)


def close_call(plan, partial, modes, tx, ty):
    channels, planes = partial.shape[:2]
    batch = 8
    block = pl.BlockSpec((batch, planes, NX, NY), lambda i: (i, 0, 0, 0))
    return pl.pallas_call(
        functools.partial(close_kernel, plan, batch),
        grid=(channels // batch,),
        in_specs=[
            block,
            pl.BlockSpec((modes.shape[0], batch) + modes.shape[2:], lambda i: (0, i, 0, 0)),
            whole(tx.shape),
            whole(ty.shape),
        ],
        out_specs=block,
        out_shape=jax.ShapeDtypeStruct(partial.shape, BF16),
        compiler_params=params(60),
        name="close",
    )(partial, modes, tx, ty)


def column_picks(channels, columns):
    column = lax.axis_index("dp") * columns + jnp.arange(columns)
    part = column // (channels * channels)
    c = column // channels % channels
    o = column % channels
    index = jnp.arange(2 * channels)[:, None]
    spec_real = (index == c).astype(F32)
    spec_imag = (index == channels + c).astype(F32) * jnp.where(part == 0, 1.0, -1.0)
    dual_same = (index == part * channels + o).astype(F32)
    dual_other = (index == (1 - part) * channels + o).astype(F32)
    return jnp.stack([spec_real, dual_same, spec_imag, dual_other]).astype(BF16)


def local(feats, grains, spec_weight, taps, point_weight, bias, cotangent):
    samples_here, channels, planes = feats.shape[:3]
    assert samples_here == 1
    slabs = lax.axis_size("slab")
    dp = lax.axis_size("dp")
    plan = Plan(planes, slabs)
    mode_rows = spec_weight.shape[0]
    half = lambda t: jnp.asarray(t.astype(jnp.bfloat16))
    ty, tx = half(plan.y_forward), half(plan.x_forward)
    tyi, txi = half(plan.y_inverse), half(plan.x_inverse)
    zf = jnp.asarray(plan.z_forward.astype(np.float32))
    zi = jnp.asarray(plan.z_inverse.astype(np.float32))
    cell_scale = 1.0 / math.sqrt(NX * NY * NZ)
    mode_scale = 1.0 / math.sqrt(KX * KY * KZ)
    jl, kq, kk, groups = plan.jl, plan.kq, plan.kk, plan.groups

    def swap(value):
        return lax.all_to_all(value, "slab", split_axis=0, concat_axis=0, tiled=True)

    def scatter_modes(modes):
        if plan.lead == 1 or kq > 1 or plan.used < plan.width:
            modes = modes[..., : plan.used].reshape(plan.lead, channels, -1, 2 * jl, planes, kq, kk)
            modes = modes.transpose(0, 2, 5, 1, 3, 4, 6)
        return swap(modes.reshape(slabs, channels * 2 * jl, plan.pk))

    def gather_planes(planar):
        planar = swap(planar)
        if plan.lead == 1 or kq > 1 or plan.used < plan.width:
            planar = planar.reshape(plan.lead, groups // plan.lead, kq, channels, 2 * jl, planes, kk)
            planar = planar.transpose(0, 3, 1, 4, 5, 2, 6).reshape(
                plan.lead, channels, 2 * KX // plan.lead, plan.used)
            return jnp.pad(planar, ((0, 0), (0, 0), (0, 0), (0, plan.width - plan.used)))
        return planar.reshape(plan.lead, channels, 2 * KX // plan.lead, plan.width)

    up = [(i, i + 1) for i in range(slabs - 1)]
    down = [(j, i) for i, j in up]
    field = feats[0]
    weights = spec_weight.reshape(mode_rows * KZ, 2 * channels * channels).T
    weights = weights.reshape(2, channels, channels, mode_rows * KZ)
    kp, kt = point_weight, point_weight.T

    fused = plan.lead == slabs and kq == 1 and plan.used == plan.width and planes % 2 == 0 and planes > 4
    columns = 2 * channels * channels // dp
    pick = column_picks(channels, columns)
    scale = 1.0 / (samples_here * dp)
    pick = pick * jnp.array([scale, 1, scale, 1], BF16)[:, None, None]
    if fused:
        zfb = half(plan.z_forward.reshape(slabs * plan.pk, 2 * plan.lanes))
        zib = half(plan.z_inverse)
        partial, back_modes, both = layer_call(
            plan, taps, field, cotangent[0], weights, grains[0], bias, point_weight, ty, tx, tyi, txi, zfb, zib,
            cell_scale, mode_scale, dp)
        back_modes = back_modes.reshape(plan.lead, channels, 2 * KX // plan.lead, plan.width)
        grad_spec = grad_call(both, pick)
        grad_feats = close_call(plan, partial, back_modes, txi, tyi)
        return grad_feats[None], grad_spec.reshape(mode_rows, KZ, columns)
    low, high = rims_call(field)
    before = lax.ppermute(high, "slab", up)
    after = lax.ppermute(low, "slab", down)
    received = scatter_modes(planes_call(plan, field, ty, tx))
    smooth = stencil_call(plan, taps, field, (before, after), False)
    received, smooth = lax.optimization_barrier((received, smooth))
    mixed, spec = mix_call(plan, received, weights, zf, zi, False, cell_scale, mode_scale)
    mixed, smooth = lax.optimization_barrier((mixed, smooth))
    modes = gather_planes(mixed)
    smooth = stencil_call(plan, taps, field, (before, after), False, smooth)
    spread, first, last, dual_modes = middle_call(
        plan, grains[0], smooth, cotangent[0], modes, bias, kp, kt, txi, tyi, ty, tx)
    spread_before = lax.ppermute(last, "slab", up)
    spread_after = lax.ppermute(first, "slab", down)
    received = scatter_modes(dual_modes)
    partial = stencil_call(plan, taps, spread, (), True)
    received, partial = lax.optimization_barrier((received, partial))
    back, dual = mix_call(plan, received, weights, zf, zi, True, mode_scale, cell_scale)
    back, partial = lax.optimization_barrier((back, partial))
    back_modes = gather_planes(back)
    partial = stencil_call(plan, taps, spread, (), True, partial)
    both = jnp.concatenate([spec, dual], axis=1)
    both = lax.all_to_all(
        jnp.broadcast_to(both[None], (dp,) + both.shape), "dp", split_axis=0, concat_axis=0, tiled=True)
    grad_spec = grad_call(both, pick)
    grad_feats = final_call(plan, taps, partial, spread_before, spread_after, back_modes, txi, tyi)
    return grad_feats[None], grad_spec.reshape(mode_rows, KZ, columns)


def solution(mesh):
    in_specs = (
        P(("grp", "dp"), None, "slab", None, None),
        P(("grp", "dp"), "slab", None, None),
        P("slab", None, None),
        P(),
        P(),
        P(),
        P(("grp", "dp"), None, "slab", None, None),
    )
    out_specs = (P(("grp", "dp"), None, "slab", None, None), P("slab", "grp", "dp"))
    return jax.shard_map(local, mesh=mesh, in_specs=in_specs, out_specs=out_specs, check_vma=False)
```

```python
import functools
import math

import jax
import jax.numpy as jnp
import numpy as np
from jax import lax
from jax.experimental import pallas as pl
from jax.experimental.pallas import tpu as pltpu
from jax.sharding import PartitionSpec as P

NX = 128
NY = 128
NZ = 32
KX = 16
KY = 16
KZ = 16
F32 = jnp.float32
BF16 = jnp.bfloat16
HIGHEST = lax.Precision.HIGHEST
MIB = 1 << 20


def waves(count, length):
    index = np.arange(count)
    frequency = np.where(index < count // 2, index, length - count + index)
    phases = frequency[:, None] * np.arange(length)[None, :] % length
    angles = phases * (2.0 * math.pi / length)
    return np.cos(angles), np.sin(angles)


class Plan:
    def __init__(self, planes, slabs):
        self.planes = planes
        self.slabs = slabs
        rows = KX * KY // slabs
        self.rows = rows
        self.groups = slabs if rows >= KY else KX
        self.jl = KX // self.groups
        self.kq = slabs // self.groups
        self.kk = KY // self.kq
        self.width = max(128, planes * KY)
        self.used = planes * KY
        self.pk = planes * self.kk
        self.lanes = self.kk * KZ
        self.lead = self.groups if (2 * self.jl) % 8 == 0 else 1
        width, jl = self.width, self.jl
        cos_x, sin_x = waves(KX, NX)
        cos_y, sin_y = waves(KY, NY)
        cos_z, sin_z = waves(KZ, NZ)
        forward = np.zeros((planes, NY, 2, width))
        for z in range(planes):
            forward[z, :, 0, z * KY : (z + 1) * KY] = cos_y.T
            forward[z, :, 1, z * KY : (z + 1) * KY] = -sin_y.T
        forward = forward.reshape(planes * NY, 2 * width)
        self.y_forward = forward
        self.y_inverse = forward.T
        table = np.zeros((self.groups, 2, jl, 2, NX))
        back = np.zeros((2, NX, self.groups, 2, jl))
        for j in range(KX):
            g, i = divmod(j, jl)
            table[g, 0, i, 0], table[g, 0, i, 1] = cos_x[j], sin_x[j]
            table[g, 1, i, 1], table[g, 1, i, 0] = cos_x[j], -sin_x[j]
            back[0, :, g, 0, i], back[0, :, g, 1, i] = cos_x[j], -sin_x[j]
            back[1, :, g, 1, i], back[1, :, g, 0, i] = cos_x[j], sin_x[j]
        self.x_forward = table.reshape(2 * KX, 2 * NX)
        self.x_inverse = back.reshape(2 * NX, 2 * KX)
        kk, pk, lanes = self.kk, self.pk, self.lanes
        zf = np.zeros((slabs, planes, kk, 2, kk, KZ))
        self.pw = max(128, pk)
        zi = np.zeros((slabs, 2, kk, KZ, 2, planes, kk))
        for s in range(slabs):
            for z in range(planes):
                c, n = cos_z[:, s * planes + z], sin_z[:, s * planes + z]
                for k in range(kk):
                    zf[s, z, k, 0, k], zf[s, z, k, 1, k] = c, n
                    zi[s, 0, k, :, 0, z, k], zi[s, 1, k, :, 0, z, k] = c, -n
                    zi[s, 1, k, :, 1, z, k], zi[s, 0, k, :, 1, z, k] = c, n
        self.z_forward = zf.reshape(slabs, pk, 2 * lanes)
        zi = zi.reshape(slabs, 2 * lanes, 2, pk)
        zi = np.pad(zi, ((0, 0), (0, 0), (0, 0), (0, self.pw - pk)))
        self.z_inverse = zi.reshape(slabs, 2 * lanes, 2 * self.pw)


def whole(shape):
    zeros = (0,) * len(shape)
    return pl.BlockSpec(shape, lambda *_: zeros)


def params(mib):
    return pltpu.CompilerParams(vmem_limit_bytes=mib * MIB)


def dot(a, b, **kw):
    return jnp.dot(a, b, preferred_element_type=F32, **kw)


def channel_modes(plan, planes_of, ty, tx):
    field = jnp.concatenate([planes_of(z) for z in range(plan.planes)], axis=1)
    along = dot(field, ty).astype(BF16)
    stacked = jnp.concatenate([along[:, : plan.width], along[:, plan.width :]], axis=0)
    return dot(tx, stacked)


def put_modes(plan, out_ref, c, value):
    if plan.lead == 1:
        out_ref[0, c] = value.astype(BF16)
    else:
        step = 2 * KX // plan.lead
        for g in range(plan.lead):
            out_ref[g, c] = value[g * step : (g + 1) * step].astype(BF16)


def get_modes(plan, ref, c):
    if plan.lead == 1:
        return ref[0, c]
    parts = [ref[g, c].astype(F32) for g in range(plan.lead)]
    return jnp.concatenate(parts, axis=0).astype(BF16)


def planes_kernel(plan, batch, x_ref, ty_ref, tx_ref, out_ref):
    for c in range(batch):
        value = channel_modes(plan, lambda z: x_ref[c, z], ty_ref[...], tx_ref[...])
        put_modes(plan, out_ref, c, value)


def planes_call(plan, field, ty, tx):
    channels, planes = field.shape[:2]
    batch = 4
    step = 2 * KX // plan.lead
    return pl.pallas_call(
        functools.partial(planes_kernel, plan, batch),
        grid=(channels // batch,),
        in_specs=[
            pl.BlockSpec((batch, planes, NX, NY), lambda i: (i, 0, 0, 0)),
            whole(ty.shape),
            whole(tx.shape),
        ],
        out_specs=pl.BlockSpec((plan.lead, batch, step, plan.width), lambda i: (0, i, 0, 0)),
        out_shape=jax.ShapeDtypeStruct((plan.lead, channels, step, plan.width), BF16),
        compiler_params=params(60),
        cost_estimate=pl.CostEstimate(
            flops=2 * channels * NX * planes * NY * 256, bytes_accessed=field.size * 2, transcendentals=0
        ),
        name="plane_modes",
    )(field, ty, tx)


def rims_kernel(low_ref, high_ref, first_ref, last_ref):
    first_ref[...] = low_ref[:, 0]
    last_ref[...] = high_ref[:, 0]


def rims_call(field):
    channels, planes = field.shape[:2]
    batch = 8
    rim = pl.BlockSpec((batch, NX, NY), lambda i: (i, 0, 0))
    shape = jax.ShapeDtypeStruct((channels, NX, NY), field.dtype)
    return pl.pallas_call(
        rims_kernel,
        grid=(channels // batch,),
        in_specs=[
            pl.BlockSpec((batch, 1, NX, NY), lambda i: (i, 0, 0, 0)),
            pl.BlockSpec((batch, 1, NX, NY), lambda i: (i, planes - 1, 0, 0)),
        ],
        out_specs=[rim, rim],
        out_shape=[shape, shape],
        compiler_params=params(60),
        name="rims",
    )(field, field)


def bands(taps_ref, c, adjoint, group, band_ref):
    row = lax.broadcasted_iota(jnp.int32, (NY, NY), 0)
    col = lax.broadcasted_iota(jnp.int32, (NY, NY), 1)
    diff = row - col
    for dz in range(3):
        for dx in range(3):
            base = 9 * dz + 3 * dx
            t = [taps_ref[base + i, c] for i in range(3)]
            if adjoint:
                t = t[::-1]
            band = jnp.where(
                diff == 0,
                t[1],
                jnp.where(diff == 1, t[2], jnp.where(diff == -1, t[0], 0.0)),
            ).astype(BF16)
            zi, xi = (2 - dz, 2 - dx) if adjoint else (dz, dx)
            for z in range(group):
                top = (xi * (group + 2) + z + zi) * NY
                band_ref[top : top + NY, z * NY : (z + 1) * NY] = band


def shifted(plan, x_ref, before_ref, after_ref, c, rows_ref):
    edge = lax.broadcasted_iota(jnp.int32, (NX, NY), 0)
    for i in range(plan.planes + 2):
        if before_ref is None and i in (0, plan.planes + 1):
            continue
        if i == 0:
            plane = before_ref[c]
        elif i == plan.planes + 1:
            plane = after_ref[c]
        else:
            plane = x_ref[c, i - 1]
        wide = plane.astype(F32)
        lower = jnp.where(edge == 0, 0.0, pltpu.roll(wide, 1, 0))
        upper = jnp.where(edge == NX - 1, 0.0, pltpu.roll(wide, NX - 1, 0))
        cols = slice(i * NY, (i + 1) * NY)
        rows_ref[0, :, cols] = lower.astype(BF16)
        rows_ref[1, :, cols] = plane
        rows_ref[2, :, cols] = upper.astype(BF16)


def stencil_kernel(plan, batch, adjoint, group, offset, *refs):
    if offset:
        refs = refs[1:]
    if adjoint:
        taps_ref, x_ref, out_ref, band_ref, rows_ref = refs
        before_ref = after_ref = None
    else:
        taps_ref, x_ref, before_ref, after_ref, out_ref, band_ref, rows_ref = refs

    @pl.when(pl.program_id(0) == 0)
    def _():
        band_ref[...] = jnp.zeros_like(band_ref)
        rows_ref[...] = jnp.zeros_like(rows_ref)

    first = pl.program_id(0) * batch + offset
    for c in range(batch):
        half = c % 2
        band, rows = band_ref.at[half], rows_ref.at[half]
        bands(taps_ref, first + c, adjoint, group, band)
        shifted(plan, x_ref, before_ref, after_ref, c, rows)
        for z in range(0, plan.planes, group):
            cols = slice(z * NY, (z + group + 2) * NY)
            near = jnp.concatenate([rows[d, :, cols] for d in range(3)], axis=1)
            total = dot(near, band[...])
            for i in range(group):
                out_ref[c, z + i] = total[:, i * NY : (i + 1) * NY].astype(BF16)


def stencil_call(plan, taps, field, rims, adjoint, done=None):
    channels, planes = field.shape[:2]
    batch = 4
    group = 2 if planes % 2 == 0 else 1
    offset = 0 if done is None else channels // 2
    skip = offset // batch
    block = pl.BlockSpec((batch, planes, NX, NY), lambda i: (i + skip, 0, 0, 0))
    specs = [pl.BlockSpec(memory_space=pltpu.SMEM), block]
    specs += [pl.BlockSpec((batch, NX, NY), lambda i: (i + skip, 0, 0))] * len(rims)
    operands = (taps, field, *rims)
    if done is not None:
        specs = [pl.BlockSpec(memory_space=pl.ANY)] + specs
        operands = (done,) + operands
    return pl.pallas_call(
        functools.partial(stencil_kernel, plan, batch, adjoint, group, offset),
        grid=(channels // 2 // batch,),
        in_specs=specs,
        out_specs=block,
        out_shape=jax.ShapeDtypeStruct(field.shape, BF16),
        input_output_aliases={} if done is None else {0: 0},
        scratch_shapes=[
            pltpu.VMEM((2, 3 * (group + 2) * NY, group * NY), BF16),
            pltpu.VMEM((2, 3, NX, (planes + 2) * NY), BF16),
        ],
        compiler_params=params(60),
        cost_estimate=pl.CostEstimate(
            flops=field.size * 3 * (group + 2) * NY, bytes_accessed=field.size * 2, transcendentals=0
        ),
        name="stencil_back" if adjoint else "stencil",
    )(*operands)


def final_kernel(plan, batch, taps_ref, x_ref, before_ref, after_ref, m_ref, tx_ref, ty_ref, out_ref):
    first = pl.program_id(0) * batch
    edge = lax.broadcasted_iota(jnp.int32, (NX, NY), 0)
    diff = lax.broadcasted_iota(jnp.int32, (NY, NY), 0) - lax.broadcasted_iota(jnp.int32, (NY, NY), 1)

    def rim(c, plane, dz):
        wide = plane.astype(F32)
        lower = jnp.where(edge == 0, 0.0, pltpu.roll(wide, 1, 0)).astype(BF16)
        upper = jnp.where(edge == NX - 1, 0.0, pltpu.roll(wide, NX - 1, 0)).astype(BF16)
        band = []
        for dx in (2, 1, 0):
            t = [taps_ref[9 * dz + 3 * dx + i, first + c] for i in range(3)]
            band.append(jnp.where(
                diff == 0,
                t[1],
                jnp.where(diff == 1, t[0], jnp.where(diff == -1, t[2], 0.0)),
            ).astype(BF16))
        return dot(jnp.concatenate([lower, plane, upper], axis=1), jnp.concatenate(band, axis=0))

    for c in range(batch):
        wave = dot(tx_ref[...], get_modes(plan, m_ref, c)).astype(BF16)
        wave = jnp.concatenate([wave[:NX], wave[NX:]], axis=1)
        full = dot(wave, ty_ref[...])
        for z in range(plan.planes):
            total = full[:, z * NY : (z + 1) * NY] + x_ref[c, z].astype(F32)
            if z == 0:
                total = total + rim(c, before_ref[c], 2)
            if z == plan.planes - 1:
                total = total + rim(c, after_ref[c], 0)
            out_ref[c, z] = total.astype(BF16)


def final_call(plan, taps, partial, before, after, modes, tx, ty):
    channels, planes = partial.shape[:2]
    batch = 4
    block = pl.BlockSpec((batch, planes, NX, NY), lambda i: (i, 0, 0, 0))
    rim = pl.BlockSpec((batch, NX, NY), lambda i: (i, 0, 0))
    return pl.pallas_call(
        functools.partial(final_kernel, plan, batch),
        grid=(channels // batch,),
        in_specs=[
            pl.BlockSpec(memory_space=pltpu.SMEM),
            block,
            rim,
            rim,
            pl.BlockSpec((modes.shape[0], batch) + modes.shape[2:], lambda i: (0, i, 0, 0)),
            whole(tx.shape),
            whole(ty.shape),
        ],
        out_specs=block,
        out_shape=jax.ShapeDtypeStruct(partial.shape, BF16),
        compiler_params=params(60),
        cost_estimate=pl.CostEstimate(
            flops=2 * partial.size * 512, bytes_accessed=partial.size * 4, transcendentals=0
        ),
        name="final",
    )(taps, partial, before, after, modes, tx, ty)


def mix_kernel(plan, channels, adjoint, scale_in, scale_out, r_ref, zf_ref, zi_ref, w_ref,
               out_ref, turned_ref, z_scr, s_scr, m_scr, o_scr):
    jl, lanes, pk, pw = plan.jl, plan.lanes, plan.pk, plan.pw
    chunks = 2 * lanes // 128
    total = None
    for s in range(plan.slabs):
        part = dot(r_ref[s].astype(F32), zf_ref[s], precision=HIGHEST)
        total = part if total is None else total + part
    total = total * scale_in
    for q in range(chunks):
        z_scr[q] = total[:, q * 128 : (q + 1) * 128]

    def rows_of(start):
        return jnp.concatenate(
            [z_scr[q, pl.ds(start, channels, stride=2 * jl), :] for q in range(chunks)], axis=1)

    for j in range(jl):
        re, im = rows_of(j), rows_of(jl + j)
        real = re[:, :lanes] + im[:, lanes:]
        imag = im[:, :lanes] - re[:, lanes:]
        s_scr[j, 0] = real
        s_scr[j, 1] = imag
        both = jnp.concatenate([real, imag], axis=0)
        turned_ref[j * lanes : (j + 1) * lanes, :] = both.T.astype(BF16)
        cols = slice(j * lanes, (j + 1) * lanes)
        rows = slice(j * channels, (j + 1) * channels)
        if adjoint:
            for c in range(channels):
                wr = w_ref[0, c, :, cols].astype(F32)
                wi = w_ref[1, c, :, cols].astype(F32)
                br = jnp.sum(wr * real + wi * imag, axis=0, keepdims=True)
                bi = jnp.sum(wr * imag - wi * real, axis=0, keepdims=True)
                m_scr[j * channels + c : j * channels + c + 1, :lanes] = br
                m_scr[j * channels + c : j * channels + c + 1, lanes:] = bi
        else:
            mr = jnp.zeros((channels, lanes), F32)
            mi = jnp.zeros((channels, lanes), F32)
            for c in range(channels):
                wr = w_ref[0, c, :, cols].astype(F32)
                wi = w_ref[1, c, :, cols].astype(F32)
                sr = s_scr[j, 0, c : c + 1, :]
                si = s_scr[j, 1, c : c + 1, :]
                mr = mr + (sr * wr - si * wi)
                mi = mi + (sr * wi + si * wr)
            m_scr[rows, :lanes] = mr
            m_scr[rows, lanes:] = mi
    mixed = m_scr[...] * scale_out
    for s in range(plan.slabs):
        planar = dot(mixed, zi_ref[s], precision=HIGHEST)
        for j in range(jl):
            for part in range(2):
                o_scr[pl.ds(part * jl + j, channels, stride=2 * jl), :] = planar[
                    j * channels : (j + 1) * channels, part * pw : (part + 1) * pw
                ]
        out_ref[s] = o_scr[:, :pk].astype(BF16)


def mix_call(plan, received, weights, zf, zi, adjoint, scale_in, scale_out):
    channels = weights.shape[1]
    rows = channels * 2 * plan.jl
    modes = plan.jl * plan.lanes
    return pl.pallas_call(
        functools.partial(mix_kernel, plan, channels, adjoint, scale_in, scale_out),
        out_shape=(
            jax.ShapeDtypeStruct((plan.slabs, rows, plan.pk), BF16),
            jax.ShapeDtypeStruct((modes, 2 * channels), BF16),
        ),
        scratch_shapes=[
            pltpu.VMEM((2 * plan.lanes // 128, rows, 128), F32),
            pltpu.VMEM((plan.jl, 2, channels, plan.lanes), F32),
            pltpu.VMEM((plan.jl * channels, 2 * plan.lanes), F32),
            pltpu.VMEM((rows, plan.pw), F32),
        ],
        compiler_params=params(60),
        name="mix_back" if adjoint else "mix",
    )(received, zf, zi, weights)


def middle_kernel(plan, channels, g_ref, sm_ref, cot_ref, m_ref, bias_ref, pw_ref, pt_ref,
                  txi_ref, tyi_ref, ty_ref, tx_ref,
                  spread_ref, first_ref, last_ref, modes_ref, wave_scr, delta_scr, move_scr, kp_ref, kt_ref):
    z = pl.program_id(0)
    planes = plan.planes
    width = plan.width

    @pl.when(z == 0)
    def _():
        def body(c, carry):
            wave = dot(txi_ref[...], get_modes(plan, m_ref, c)).astype(BF16)
            wave_scr[c, :, :width] = wave[:NX]
            wave_scr[c, :, width:] = wave[NX:]
            return carry
        lax.fori_loop(0, channels, body, 0, unroll=4)
        rows = channels * 16
        pick = lax.broadcasted_iota(jnp.int32, (rows, channels), 0) >> 4
        pick = pick == lax.broadcasted_iota(jnp.int32, (rows, channels), 1)
        pick = jnp.where(pick, 1.0, 0.0).astype(BF16)
        same = lax.broadcasted_iota(jnp.int32, (rows, rows), 0) & 15
        same = same == (lax.broadcasted_iota(jnp.int32, (rows, rows), 1) & 15)
        for src, dst in ((pt_ref, kp_ref), (pw_ref, kt_ref)):
            tall = dot(pick, src[...]).astype(BF16)
            full = lax.dot_general(tall, pick, (((1,), (1,)), ((), ())), preferred_element_type=F32)
            dst[...] = jnp.where(same, full, 0.0).astype(BF16)

    g = g_ref[0]
    row = lax.broadcasted_iota(jnp.int32, (NX, NY), 0)
    col = lax.broadcasted_iota(jnp.int32, (NX, NY), 1)

    def differs(shift, axis, inside):
        return jnp.where((g != pltpu.roll(g, shift, axis)) & inside, 0.25, 0.0)

    move_scr[...] = (
        0.25
        + differs(1, 0, row > 0)
        + differs(NX - 1, 0, row < NX - 1)
        + differs(1, 1, col > 0)
        + differs(NY - 1, 1, col < NY - 1)
    )
    height = channels * 16
    bias = bias_ref[...]

    def body(pair, carry):
        starts = [pair * 32 + 16 * i for i in range(2)]

        def tile(ref):
            return [ref[:, 0, pl.ds(x, 16), :].reshape(height, NY) for x in starts]

        mixed = dot(kp_ref[...], jnp.concatenate(tile(sm_ref), axis=1))
        cot = tile(cot_ref)
        deltas = []
        for i, x in enumerate(starts):
            moving = move_scr[pl.ds(x, 16), :]
            wave = wave_scr[:, pl.ds(x, 16), :].reshape(height, 2 * width)
            spectral = dot(wave, tyi_ref[...])
            local = mixed[:, i * NY : (i + 1) * NY].reshape(channels, 16, NY) * moving[None]
            pre = spectral.reshape(channels, 16, NY) + local + bias
            gate = 0.5 + 0.5 * jnp.tanh(0.5 * pre)
            delta = cot[i].astype(F32).reshape(channels, 16, NY) * gate * (1.0 + pre * (1.0 - gate))
            delta = delta.astype(BF16)
            delta_scr[:, z, pl.ds(x, 16), :] = delta
            deltas.append(delta.reshape(height, NY))
        turned = dot(kt_ref[...], jnp.concatenate(deltas, axis=1))
        for i, x in enumerate(starts):
            moving = move_scr[pl.ds(x, 16), :]
            value = turned[:, i * NY : (i + 1) * NY].reshape(channels, 16, NY) * moving[None]
            spread_ref[:, 0, pl.ds(x, 16), :] = value.astype(BF16)
        return carry

    for pair in range(NX // 32):
        body(pair, 0)

    @pl.when(z == 0)
    def _():
        first_ref[...] = spread_ref[:, 0]

    @pl.when(z == planes - 1)
    def _():
        last_ref[...] = spread_ref[:, 0]

        def body(i, carry):
            for c in (2 * i, 2 * i + 1):
                value = channel_modes(plan, lambda p: delta_scr[c, p], ty_ref[...], tx_ref[...])
                put_modes(plan, modes_ref, c, value)
            return carry

        lax.fori_loop(0, channels // 2, body, 0)


def middle_call(plan, grains, smooth, cotangent, modes, bias, kp, kt, txi, tyi, ty, tx):
    channels, planes = smooth.shape[:2]
    width = plan.width
    block = pl.BlockSpec((channels, 1, NX, NY), lambda z: (0, z, 0, 0))
    rim = jax.ShapeDtypeStruct((channels, NX, NY), BF16)
    return pl.pallas_call(
        functools.partial(middle_kernel, plan, channels),
        grid=(planes,),
        in_specs=[
            pl.BlockSpec((1, NX, NY), lambda z: (z, 0, 0)),
            block,
            block,
            whole(modes.shape),
            whole((channels, 1, 1)),
            whole(kp.shape),
            whole(kt.shape),
            whole(txi.shape),
            pl.BlockSpec((2 * width, NY), lambda z: (0, z)),
            whole(ty.shape),
            whole(tx.shape),
        ],
        out_specs=[block, whole(rim.shape), whole(rim.shape), whole(modes.shape)],
        out_shape=[jax.ShapeDtypeStruct(smooth.shape, BF16), rim, rim,
                   jax.ShapeDtypeStruct(modes.shape, BF16)],
        scratch_shapes=[
            pltpu.VMEM((channels, NX, 2 * width), BF16),
            pltpu.VMEM((channels, planes, NX, NY), BF16),
            pltpu.VMEM((NX, NY), F32),
            pltpu.VMEM((16 * channels, 16 * channels), BF16),
            pltpu.VMEM((16 * channels, 16 * channels), BF16),
        ],
        compiler_params=params(60),
        name="middle",
    )(grains, smooth, cotangent, modes, bias.reshape(channels, 1, 1), kp, kt, txi, tyi, ty, tx)


def grad_kernel(samples, both_ref, e_ref, out_ref):
    total = None
    for i in range(samples):
        half = both_ref.shape[-1] // 2
        spec, dual = both_ref[i, :, :half], both_ref[i, :, half:]
        term = dot(spec, e_ref[0]) * dot(dual, e_ref[1]) + dot(spec, e_ref[2]) * dot(dual, e_ref[3])
        total = term if total is None else total + term
    out_ref[...] = total


def grad_call(both, pick):
    samples, modes, width = both.shape
    columns = pick.shape[-1]
    batch = min(256, modes)
    return pl.pallas_call(
        functools.partial(grad_kernel, samples),
        grid=(modes // batch,),
        in_specs=[
            pl.BlockSpec((samples, batch, width), lambda i: (0, i, 0)),
            whole(pick.shape),
        ],
        out_specs=pl.BlockSpec((batch, columns), lambda i: (i, 0)),
        out_shape=jax.ShapeDtypeStruct((modes, columns), F32),
        compiler_params=params(60),
        cost_estimate=pl.CostEstimate(
            flops=8 * samples * modes * width * columns, bytes_accessed=modes * columns * 4, transcendentals=0
        ),
        name="grad_modes",
    )(both, pick)


def slab_peer(me, d, slabs):
    return lax.rem(me + d, slabs)


def enter(sizes):
    barrier = pltpu.get_barrier_semaphore()
    total = 0
    for axis, size in sizes.items():
        me = lax.axis_index(axis)
        for d in range(1, size):
            pl.semaphore_signal(
                barrier, inc=1, device_id={axis: slab_peer(me, d, size)}, device_id_type=pl.DeviceIdType.MESH)
        total += size - 1
    pl.semaphore_wait(barrier, total)


def exchange(me, slabs, send_ref, recv_ref, send_sem, recv_sem):
    copies = []
    for d in range(1, slabs):
        peer = slab_peer(me, d, slabs)
        copies.append(pltpu.make_async_remote_copy(
            src_ref=send_ref.at[peer],
            dst_ref=recv_ref.at[me],
            send_sem=send_sem.at[d - 1],
            recv_sem=recv_sem.at[d - 1],
            device_id={"slab": peer},
            device_id_type=pl.DeviceIdType.MESH,
        ))
    return copies


def halo_copies(me, slabs, field_ref, before_ref, after_ref, planes, chunk, index, send_sem, recv_sem):
    rows = pl.ds(index * chunk, chunk)
    up = pltpu.make_async_remote_copy(
        src_ref=field_ref.at[rows, planes - 1],
        dst_ref=before_ref.at[rows],
        send_sem=send_sem.at[0, index],
        recv_sem=recv_sem.at[0, index],
        device_id={"slab": lax.rem(me + 1, slabs)},
        device_id_type=pl.DeviceIdType.MESH,
    )
    down = pltpu.make_async_remote_copy(
        src_ref=field_ref.at[rows, 0],
        dst_ref=after_ref.at[rows],
        send_sem=send_sem.at[1, index],
        recv_sem=recv_sem.at[1, index],
        device_id={"slab": lax.rem(me + slabs - 1, slabs)},
        device_id_type=pl.DeviceIdType.MESH,
    )
    return up, down


def halo_start(me, slabs, copies):
    up, down = copies

    @pl.when(me < slabs - 1)
    def _():
        up.start()

    @pl.when(me > 0)
    def _():
        down.start()


def halo_wait_recv(me, slabs, copies):
    up, down = copies

    @pl.when(me > 0)
    def _():
        up.wait_recv()

    @pl.when(me < slabs - 1)
    def _():
        down.wait_recv()


def halo_wait_send(me, slabs, copies):
    up, down = copies

    @pl.when(me < slabs - 1)
    def _():
        up.wait_send()

    @pl.when(me > 0)
    def _():
        down.wait_send()


def batch_modes(plan, out_ref, row, lines, ty_ref, tx_ref):
    count = len(lines)
    along = dot(jnp.concatenate(lines, axis=0), ty_ref[...]).astype(BF16)
    width = plan.width
    values = []
    for c in range(0, count, 2):
        top = along[c * NX : (c + 1) * NX]
        low = along[(c + 1) * NX : (c + 2) * NX]
        pair = jnp.concatenate([
            jnp.concatenate([top[:, :width], low[:, :width]], axis=1),
            jnp.concatenate([top[:, width:], low[:, width:]], axis=1),
        ], axis=0)
        both = dot(tx_ref[...], pair)
        values += [both[:, :width], both[:, width:]]
    step = 2 * KX // plan.lead
    for g in range(plan.lead):
        part = jnp.concatenate([v[g * step : (g + 1) * step] for v in values], axis=0)
        out_ref[g, pl.ds(row, count * step), :] = part.astype(BF16)


def band_masks():
    diff = lax.broadcasted_iota(jnp.int32, (NY, NY), 0) - lax.broadcasted_iota(jnp.int32, (NY, NY), 1)
    return diff == 1, diff == 0, diff == -1


def fill_band(taps_ref, c, adjoint, masks, band_ref):
    low, mid, upp = masks
    for dz in range(3):
        for dx in range(3):
            base = 9 * dz + 3 * dx
            t = [taps_ref[base + i, c] for i in range(3)]
            if adjoint:
                t = t[::-1]
            band = jnp.where(mid, t[1], jnp.where(low, t[2], jnp.where(upp, t[0], 0.0))).astype(BF16)
            zi, xi = (2 - dz, 2 - dx) if adjoint else (dz, dx)
            for z in range(2):
                top = (xi * 4 + z + zi) * NY
                band_ref[top : top + NY, z * NY : (z + 1) * NY] = band


def stencil_part(plan, taps_ref, x_ref, before_ref, after_ref, c, groups, adjoint, masks, out_ref,
                 band_ref, wide_ref, lower_ref, upper_ref):
    fill_band(taps_ref, c, adjoint, masks, band_ref)
    planes = plan.planes

    def plane(i):
        if i == 0:
            return before_ref[c]
        if i == planes + 1:
            return after_ref[c]
        return x_ref[c, i - 1]

    needed = sorted({2 * g + i for g in groups for i in range(4)})
    slot = {i: n for n, i in enumerate(needed)}
    for i in needed:
        n = slot[i]
        wide_ref[n, 8 : NX + 8, :] = plane(i).astype(F32)
        lower_ref[n] = wide_ref[n, 7 : NX + 7, :].astype(BF16)
        upper_ref[n] = wide_ref[n, 9 : NX + 9, :].astype(BF16)

    def moved(dx, i):
        if dx == 1:
            return plane(i)
        return (lower_ref if dx == 0 else upper_ref)[slot[i]]

    near = jnp.concatenate([
        jnp.concatenate([moved(dx, 2 * g + i) for dx in range(3) for i in range(4)], axis=1)
        for g in groups
    ], axis=0)
    total = dot(near, band_ref[...])
    for n, g in enumerate(groups):
        for i in range(2):
            out_ref[c, 2 * g + i] = total[n * NX : (n + 1) * NX, i * NY : (i + 1) * NY].astype(BF16)


def mix_modes(plan, channels, me, adjoint, scale_in, scale_out, own_ref, r_ref, zf_ref, zi_ref, w_ref,
              out_ref, turned_ref, z_scr, s_scr, m_scr, o_scr):
    jl, lanes, pk, pw = plan.jl, plan.lanes, plan.pk, plan.pw
    chunks = 2 * lanes // 128
    r_ref[me] = own_ref[me]
    total = dot(jnp.concatenate([r_ref[s] for s in range(plan.slabs)], axis=1), zf_ref[...])
    total = total * scale_in
    for q in range(chunks):
        z_scr[q] = total[:, q * 128 : (q + 1) * 128]

    def rows_of(start):
        return jnp.concatenate(
            [z_scr[q, pl.ds(start, channels, stride=2 * jl), :] for q in range(chunks)], axis=1)

    for j in range(jl):
        re, im = rows_of(j), rows_of(jl + j)
        real = re[:, :lanes] + im[:, lanes:]
        imag = im[:, :lanes] - re[:, lanes:]
        s_scr[j, 0] = real
        s_scr[j, 1] = imag
        both = jnp.concatenate([real, imag], axis=0)
        turned_ref[j * lanes : (j + 1) * lanes, :] = both.T.astype(BF16)
        cols = slice(j * lanes, (j + 1) * lanes)
        rows = slice(j * channels, (j + 1) * channels)
        if adjoint:
            def body(i, carry):
                parts = []
                for k in range(8):
                    c = 8 * i + k
                    wr = w_ref[0, c, :, cols].astype(F32)
                    wi = w_ref[1, c, :, cols].astype(F32)
                    real, imag = s_scr[j, 0], s_scr[j, 1]
                    br = jnp.sum(wr * real + wi * imag, axis=0, keepdims=True)
                    bi = jnp.sum(wr * imag - wi * real, axis=0, keepdims=True)
                    parts.append(jnp.concatenate([br, bi], axis=1))
                m_scr[pl.ds(pl.multiple_of(j * channels + 8 * i, 8), 8), :] = jnp.concatenate(parts, axis=0)
                return carry
            lax.fori_loop(0, channels // 8, body, 0)
        else:
            def body(i, carry):
                mr, mi = carry
                for k in range(8):
                    c = 8 * i + k
                    wr = w_ref[0, c, :, cols].astype(F32)
                    wi = w_ref[1, c, :, cols].astype(F32)
                    sr = s_scr[j, 0, pl.ds(c, 1), :]
                    si = s_scr[j, 1, pl.ds(c, 1), :]
                    mr = mr + (sr * wr - si * wi)
                    mi = mi + (sr * wi + si * wr)
                return mr, mi
            zero = jnp.zeros((channels, lanes), F32)
            mr, mi = lax.fori_loop(0, channels // 8, body, (zero, zero))
            m_scr[rows, :lanes] = mr
            m_scr[rows, lanes:] = mi
    mixed = (m_scr[...] * scale_out).astype(BF16)
    for s in range(plan.slabs):
        planar = dot(mixed, zi_ref[s])
        for j in range(jl):
            for part in range(2):
                o_scr[pl.ds(part * jl + j, channels, stride=2 * jl), :] = planar[
                    j * channels : (j + 1) * channels, part * pw : (part + 1) * pw
                ]
        out_ref[s] = o_scr[:, :pk].astype(BF16)


def mobility(g_ref, z, move_ref):
    row = lax.broadcasted_iota(jnp.int32, (NX, NY), 0)
    col = lax.broadcasted_iota(jnp.int32, (NX, NY), 1)
    for i in range(2):
        g = g_ref[z + i]

        def differs(shift, axis, inside):
            return jnp.where((g != pltpu.roll(g, shift, axis)) & inside, 0.25, 0.0)

        move_ref[i] = (
            0.25
            + differs(1, 0, row > 0)
            + differs(NX - 1, 0, row < NX - 1)
            + differs(1, 1, col > 0)
            + differs(NY - 1, 1, col < NY - 1)
        )


def spread_weights(channels, src_ref, dst_ref, turned):
    rows = channels * 16
    pick = lax.broadcasted_iota(jnp.int32, (rows, channels), 0) >> 4
    pick = pick == lax.broadcasted_iota(jnp.int32, (rows, channels), 1)
    pick = jnp.where(pick, 1.0, 0.0).astype(BF16)
    same = lax.broadcasted_iota(jnp.int32, (rows, rows), 0) & 15
    same = same == (lax.broadcasted_iota(jnp.int32, (rows, rows), 1) & 15)
    axes = (((1,), (1 if turned else 0,)), ((), ()))
    tall = lax.dot_general(pick, src_ref[...], axes, preferred_element_type=F32).astype(BF16)
    full = lax.dot_general(tall, pick, (((1,), (1,)), ((), ())), preferred_element_type=F32)
    dst_ref[...] = jnp.where(same, full, 0.0).astype(BF16)


def turn_weights(channels, raw_ref, w_ref):
    block = 8 * channels
    per_part = channels // 8
    same = lax.broadcasted_iota(jnp.int32, (block, block), 0) == lax.broadcasted_iota(jnp.int32, (block, block), 1)
    unit = jnp.where(same, 1.0, 0.0).astype(BF16)

    def body(i, carry):
        for part in range(2):
            first = (part * per_part + i) * (block // 128)
            modes = raw_ref.shape[1] * raw_ref.shape[2]
            raw = jnp.concatenate([raw_ref[first + n].reshape(modes, 128) for n in range(block // 128)], axis=1)
            value = lax.dot_general(unit, raw, (((1,), (1,)), ((), ())), preferred_element_type=F32)
            w_ref[part, pl.ds(i * 8, 8)] = value.astype(BF16).reshape(8, channels, value.shape[1])
        return carry

    lax.fori_loop(0, per_part, body, 0)


def sample_picks(channels, columns, lane, samples, e_ref):
    size = 2 * channels
    row = lax.broadcasted_iota(jnp.int32, (size, columns), 0)
    column = lax.broadcasted_iota(jnp.int32, (size, columns), 1) + lane * columns
    part = lane * columns // (channels * channels)
    c = column // channels % channels
    sign = jnp.where(part == 0, 1.0, -1.0) / samples
    e_ref[...] = jnp.zeros_like(e_ref)
    e_ref[:size, :columns] = jnp.where(row == c, 1.0 / samples, 0.0).astype(BF16)
    e_ref[:size, columns : 2 * columns] = jnp.where(row == channels + c, sign, 0.0).astype(BF16)
    row = lax.broadcasted_iota(jnp.int32, (size, 128), 0)
    o = lax.broadcasted_iota(jnp.int32, (size, 128), 1) % channels
    e_ref[size:, 2 * columns : 2 * columns + 128] = jnp.where(row == part * channels + o, 1.0, 0.0).astype(BF16)
    e_ref[size:, 2 * columns + 128 :] = jnp.where(row == (1 - part) * channels + o, 1.0, 0.0).astype(BF16)


def sample_grads(columns, samples, both_ref, e_ref, out_ref):
    modes = both_ref.shape[1]
    batch = 256

    def body(i, carry):
        rows = pl.ds(pl.multiple_of(i * batch, batch), batch)
        totals = [None] * (columns // 128)
        for n in range(samples):
            wide = dot(both_ref[n, rows, :], e_ref[...])
            same = wide[:, 2 * columns : 2 * columns + 128]
            other = wide[:, 2 * columns + 128 :]
            for q in range(len(totals)):
                first = wide[:, q * 128 : (q + 1) * 128]
                second = wide[:, columns + q * 128 : columns + (q + 1) * 128]
                term = first * same + second * other
                totals[q] = term if totals[q] is None else totals[q] + term
        for q, total in enumerate(totals):
            out_ref[rows, q * 128 : (q + 1) * 128] = total
        return carry

    lax.fori_loop(0, modes // batch, body, 0)


def gate_pair(plan, channels, z, g_ref, sm_ref, cot_ref, wave_ref, tyi_ref, kp_ref, kt_ref, bias_ref, move_ref):
    mobility(g_ref, z, move_ref)
    height = channels * 16
    bias = bias_ref[:, 0:1, :]
    for k in range(NX // 16):
        rows = pl.ds(k * 16, 16)

        def tile(ref, n):
            return ref[:, z + n, rows, :].reshape(height, NY)

        mixed = dot(kp_ref[...], jnp.concatenate([tile(sm_ref, 0), tile(sm_ref, 1)], axis=1))
        wave = wave_ref[:, rows, :].reshape(height, 2 * plan.width)
        spectral = dot(wave, tyi_ref[z // 2])
        deltas = []
        for n in range(2):
            cols = slice(n * NY, (n + 1) * NY)
            moving = move_ref[n, rows, :]
            local = mixed[:, cols].reshape(channels, 16, NY) * moving[None]
            pre = spectral[:, cols].reshape(channels, 16, NY) + local + bias
            half = 0.5 * jnp.tanh(0.5 * pre)
            delta = tile(cot_ref, n).astype(F32).reshape(channels, 16, NY) * (0.5 + half) * (1.0 + pre * (0.5 - half))
            delta = delta.astype(BF16)
            cot_ref[:, z + n, rows, :] = delta
            deltas.append(delta.reshape(height, NY))
        turned = dot(kt_ref[...], jnp.concatenate(deltas, axis=1))
        for n in range(2):
            cols = slice(n * NY, (n + 1) * NY)
            value = turned[:, cols].reshape(channels, 16, NY) * move_ref[n, rows, :][None]
            sm_ref[:, z + n, rows, :] = value.astype(BF16)


def pair_waves(plan, read, tx_ref):
    width = plan.width
    pair = jnp.concatenate([
        jnp.concatenate([read(g, k).astype(F32) for g in range(plan.lead)], axis=0) for k in range(2)
    ], axis=1).astype(BF16)
    wave = dot(tx_ref[...], pair).astype(BF16)
    found = []
    for k in range(2):
        cols = slice(k * width, (k + 1) * width)
        found.append(jnp.concatenate([wave[:NX, cols], wave[NX:, cols]], axis=1))
    return found


def layer_kernel(plan, channels, peers, cell_scale, mode_scale,
                 taps_ref, bias_in, x_hbm, cot_hbm, w_hbm, g_ref, pw_ref,
                 ty_ref, tx_ref, tyi_ref, txi_ref, zf_ref, zi_ref,
                 out_hbm, grad_hbm,
                 x_ref, y_ref, cot_ref, w_ref, before_ref, after_ref, before2_ref, after2_ref,
                 send1, recv1, send2, recv2, send3, recv3, send4, recv4,
                 wave_ref, kp_ref, kt_ref, move_ref, bias_ref, spec_ref, dual_ref, both_ref, gather_ref, e_ref, grad_ref,
                 band_ref, wide_ref, lower_ref, upper_ref, z_scr, s_scr, m_scr, o_scr,
                 load_sem, cot_sem, w_sem, store_sem, grad_sem, halo_send, halo_recv, send_sem, recv_sem, both_send, both_recv):
    planes, slabs = plan.planes, plan.slabs
    columns = grad_ref.shape[1]
    me = lax.axis_index("slab")
    lane = lax.axis_index("dp")
    chunk = 8
    chunks = channels // chunk
    step = 2 * KX // plan.lead
    pairs = planes // 2
    inner, outer = list(range(1, pairs - 1)), [0, pairs - 1]

    def load(i):
        rows = pl.ds(i * chunk, chunk)
        return pltpu.make_async_copy(x_hbm.at[rows], x_ref.at[rows], load_sem.at[i])

    for i in range(chunks):
        load(i).start()
    enter({"slab": slabs, "dp": peers})
    halos = [halo_copies(me, slabs, x_hbm, before_ref, after_ref, planes, chunk, i, halo_send.at[0], halo_recv.at[0])
             for i in range(chunks)]
    halo_start(me, slabs, halos[0])
    loads_w = [
        pltpu.make_async_copy(w_hbm.at[:, :, pl.ds(128 * i, 128)], cot_ref.at[i], w_sem.at[i])
        for i in range(w_hbm.shape[2] // 128)
    ]
    for copy in loads_w:
        copy.start()

    @pl.when(me == 0)
    def _():
        before_ref[...] = jnp.zeros_like(before_ref)
        before2_ref[...] = jnp.zeros_like(before2_ref)

    @pl.when(me == slabs - 1)
    def _():
        after_ref[...] = jnp.zeros_like(after_ref)
        after2_ref[...] = jnp.zeros_like(after2_ref)

    band_ref[...] = jnp.zeros_like(band_ref)
    for u in range(4):
        for n in range(wide_ref.shape[1]):
            wide_ref[u, n, 0:8, :] = jnp.zeros((8, NY), F32)
            wide_ref[u, n, NX + 8 : NX + 16, :] = jnp.zeros((8, NY), F32)
    for c in range(channels):
        bias_ref[c] = jnp.full((8, NY), bias_in[c], F32)
    spread_weights(channels, pw_ref, kp_ref, True)
    spread_weights(channels, pw_ref, kt_ref, False)
    sample_picks(channels, columns, lane, peers, e_ref)

    def spectra(src_ref, out_ref):
        def body(i, carry):
            if src_ref is x_ref:
                load(i).wait()
            lines = [jnp.concatenate([src_ref[i * chunk + c, z] for z in range(planes)], axis=1) for c in range(chunk)]
            batch_modes(plan, out_ref, pl.multiple_of(i * chunk * step, chunk * step), lines, ty_ref, tx_ref)
            return carry
        lax.fori_loop(0, chunks, body, 0)

    spectra(x_ref, send1)
    first = exchange(me, slabs, send1, recv1, send_sem.at[0], recv_sem.at[0])
    for copy in first:
        copy.start()
    halo_start(me, slabs, halos[1])

    masks = band_masks()

    def stencil(groups, adjoint):
        src, dst = (y_ref, x_ref) if adjoint else (x_ref, y_ref)
        low, high = (before2_ref, after2_ref) if adjoint else (before_ref, after_ref)

        def body(i, carry):
            for u in range(4):
                stencil_part(plan, taps_ref, src, low, high, i * 4 + u, groups, adjoint, masks, dst,
                             band_ref.at[u], wide_ref.at[u], lower_ref.at[u], upper_ref.at[u])
            return carry
        return body

    def gates(start, stride):
        def body(i, carry):
            gate_pair(plan, channels, 2 * (start + stride * i), g_ref, y_ref, cot_ref, wave_ref, tyi_ref,
                      kp_ref, kt_ref, bias_ref, move_ref)
            return carry
        return body

    lax.fori_loop(0, channels // 4, stencil(inner, False), 0)
    for copy in loads_w:
        copy.wait()
    turn_weights(channels, cot_ref, w_ref)
    load_cot = pltpu.make_async_copy(cot_hbm, cot_ref, cot_sem)
    load_cot.start()
    for copy in first:
        copy.wait()
    mix_modes(plan, channels, me, False, cell_scale, mode_scale, send1, recv1, zf_ref, zi_ref, w_ref,
              send2, spec_ref, z_scr, s_scr, m_scr, o_scr)
    second = exchange(me, slabs, send2, recv2, send_sem.at[1], recv_sem.at[1])
    for copy in second:
        copy.start()
    for copies in halos[2:]:
        halo_start(me, slabs, copies)
    recv2[me] = send2[me]
    edge = stencil(outer, False)
    for i in range(2):
        halo_wait_recv(me, slabs, halos[i])
        lax.fori_loop(2 * i, 2 * i + 2, edge, 0)
    load_cot.wait()
    for copy in second:
        copy.wait()

    def unfold(src_ref):
        def body(i, carry):
            for k in range(0, 8, 2):
                c = i * 8 + k
                found = pl.ds(pl.multiple_of(c * step, 2 * step), 2 * step)
                for n, wave in enumerate(pair_waves(
                        plan, lambda g, j: src_ref[g, found, :][j * step : (j + 1) * step], txi_ref)):
                    wave_ref[c + n] = wave
            return carry
        lax.fori_loop(0, channels // 8, body, 0)

    unfold(recv2)
    lax.fori_loop(0, pairs - 2, gates(1, 1), 0)
    for i in range(2, chunks):
        halo_wait_recv(me, slabs, halos[i])
        lax.fori_loop(2 * i, 2 * i + 2, edge, 0)
    lax.fori_loop(0, 2, gates(0, pairs - 1), 0)

    turns = [halo_copies(me, slabs, y_ref, before2_ref, after2_ref, planes, chunk, i, halo_send.at[1], halo_recv.at[1])
             for i in range(chunks)]
    halo_start(me, slabs, turns[0])
    spectra(cot_ref, send3)
    third = exchange(me, slabs, send3, recv3, send_sem.at[2], recv_sem.at[2])
    for copy in third:
        copy.start()
    halo_start(me, slabs, turns[1])
    lax.fori_loop(0, channels // 4, stencil(inner, True), 0)
    for copy in third:
        copy.wait()
    mix_modes(plan, channels, me, True, mode_scale, cell_scale, send3, recv3, zf_ref, zi_ref, w_ref,
              send4, dual_ref, z_scr, s_scr, m_scr, o_scr)
    fourth = exchange(me, slabs, send4, recv4, send_sem.at[3], recv_sem.at[3])
    for copy in fourth:
        copy.start()
    for copies in turns[2:]:
        halo_start(me, slabs, copies)
    recv4[me] = send4[me]
    both_ref[...] = jnp.concatenate([spec_ref[...], dual_ref[...]], axis=1)
    shares = []
    for d in range(1, peers):
        shares.append(pltpu.make_async_remote_copy(
            src_ref=both_ref,
            dst_ref=gather_ref.at[lane],
            send_sem=both_send.at[d - 1],
            recv_sem=both_recv.at[d - 1],
            device_id={"dp": slab_peer(lane, d, peers)},
            device_id_type=pl.DeviceIdType.MESH,
        ))
    for copy in shares:
        copy.start()
    gather_ref[lane] = both_ref[...]

    def store(i):
        rows = pl.ds(i * chunk, chunk)
        return pltpu.make_async_copy(x_ref.at[rows], out_hbm.at[rows], store_sem.at[i])

    def close(i):
        waves_of = wave_ref[pl.ds(i * chunk, chunk)].reshape(chunk * NX, 2 * plan.width)
        for g in range(pairs):
            full = dot(waves_of, tyi_ref[g])
            for c in range(chunk):
                for n in range(2):
                    total = full[c * NX : (c + 1) * NX, n * NY : (n + 1) * NY]
                    spot = (i * chunk + c, 2 * g + n)
                    x_ref[spot] = (total + x_ref[spot].astype(F32)).astype(BF16)

    edge = stencil(outer, True)
    for i in range(2):
        halo_wait_recv(me, slabs, turns[i])
        lax.fori_loop(2 * i, 2 * i + 2, edge, 0)
    for copy in fourth:
        copy.wait()
    unfold(recv4)
    for i in range(2):
        close(i)
        store(i).start()
    for copy in shares:
        copy.wait()
    sample_grads(columns, peers, gather_ref, e_ref, grad_ref)
    store_grad = pltpu.make_async_copy(grad_ref, grad_hbm, grad_sem)
    store_grad.start()
    for i in range(2, chunks):
        halo_wait_recv(me, slabs, turns[i])
        lax.fori_loop(2 * i, 2 * i + 2, edge, 0)
        close(i)
        store(i).start()
    for copies in halos + turns:
        halo_wait_send(me, slabs, copies)
    store_grad.wait()
    for i in range(chunks):
        store(i).wait()


def layer_call(plan, taps, field, cotangent, weights, grains, bias, point, ty, tx, tyi, txi, zf, zi,
               cell_scale, mode_scale, peers):
    channels, planes = field.shape[:2]
    slabs = plan.slabs
    rows = channels * 2 * plan.jl
    modes = plan.jl * plan.lanes
    columns = 2 * channels * channels // peers
    whole_vmem = pl.BlockSpec(memory_space=pltpu.VMEM)
    anywhere = pl.BlockSpec(memory_space=pl.ANY)
    chunks = channels // 8
    block = pltpu.VMEM((slabs, rows, plan.pk), BF16)
    rim = pltpu.VMEM((channels, NX, NY), BF16)
    wide = pltpu.VMEM((16 * channels, 16 * channels), BF16)
    dma = pltpu.SemaphoreType.DMA
    tyi = tyi.reshape(2 * plan.width, planes // 2, 2 * NY).transpose(1, 0, 2)
    return pl.pallas_call(
        functools.partial(layer_kernel, plan, channels, peers, cell_scale, mode_scale),
        in_specs=[pl.BlockSpec(memory_space=pltpu.SMEM)] * 2 + [anywhere] * 3 + [whole_vmem] * 8,
        out_specs=[anywhere, anywhere],
        out_shape=[
            jax.ShapeDtypeStruct(field.shape, BF16),
            jax.ShapeDtypeStruct((modes, columns), F32),
        ],
        scratch_shapes=[
            pltpu.VMEM(field.shape, BF16),
            pltpu.VMEM(field.shape, BF16),
            pltpu.VMEM(field.shape, BF16),
            pltpu.VMEM((2, channels, channels, modes), BF16),
            rim, rim, rim, rim,
            block, block, block, block, block, block, block, block,
            pltpu.VMEM((channels, NX, 2 * plan.width), BF16),
            wide, wide,
            pltpu.VMEM((2, NX, NY), F32),
            pltpu.VMEM((channels, 8, NY), F32),
            pltpu.VMEM((modes, 2 * channels), BF16),
            pltpu.VMEM((modes, 2 * channels), BF16),
            pltpu.VMEM((modes, 4 * channels), BF16),
            pltpu.VMEM((peers, modes, 4 * channels), BF16),
            pltpu.VMEM((4 * channels, 2 * columns + 256), BF16),
            pltpu.VMEM((modes, columns), F32),
            pltpu.VMEM((4, 12 * NY, 2 * NY), BF16),
            pltpu.VMEM((4, 8, NX + 16, NY), F32),
            pltpu.VMEM((4, 8, NX, NY), BF16),
            pltpu.VMEM((4, 8, NX, NY), BF16),
            pltpu.VMEM((2 * plan.lanes // 128, rows, 128), F32),
            pltpu.VMEM((plan.jl, 2, channels, plan.lanes), F32),
            pltpu.VMEM((plan.jl * channels, 2 * plan.lanes), F32),
            pltpu.VMEM((rows, plan.pw), F32),
            dma((chunks,)), dma, dma((weights.shape[2] // 128,)), dma((chunks,)), dma,
            dma((2, 2, chunks)), dma((2, 2, chunks)),
            dma((4, slabs - 1)), dma((4, slabs - 1)),
            dma((peers - 1,)), dma((peers - 1,)),
        ],
        compiler_params=pltpu.CompilerParams(
            vmem_limit_bytes=55 * MIB, collective_id=0, has_side_effects=True),
        name="layer",
    )(taps, bias, field, cotangent, weights, grains, point, ty, tx, tyi, txi, zf, zi)


def hand_on_kernel(chunks, x_hbm, grad_hbm, out_hbm, out_grad_hbm, x_ref, grad_ref, in_sem, out_sem):
    arrays = [(grad_hbm, grad_ref, out_grad_hbm, chunks)]
    size = x_hbm.shape[0] // chunks
    for i in range(chunks):
        rows = pl.ds(i * size, size)
        arrays.append((x_hbm.at[rows], x_ref.at[rows], out_hbm.at[rows], i))
    ins = [pltpu.make_async_copy(src, mid, in_sem.at[n]) for src, mid, _, n in arrays]
    outs = [pltpu.make_async_copy(mid, dst, out_sem.at[n]) for _, mid, dst, n in arrays]
    for copy in ins:
        copy.start()
    for came, goes in zip(ins, outs):
        came.wait()
        goes.start()
    for copy in outs:
        copy.wait()


def hand_on_call(value, grad, chunks=8):
    anywhere = pl.BlockSpec(memory_space=pl.ANY)
    return pl.pallas_call(
        functools.partial(hand_on_kernel, chunks),
        in_specs=[anywhere] * 2,
        out_specs=[anywhere] * 2,
        out_shape=[jax.ShapeDtypeStruct(value.shape, value.dtype), jax.ShapeDtypeStruct(grad.shape, grad.dtype)],
        scratch_shapes=[
            pltpu.VMEM(value.shape, value.dtype),
            pltpu.VMEM(grad.shape, grad.dtype),
            pltpu.SemaphoreType.DMA((chunks + 1,)),
            pltpu.SemaphoreType.DMA((chunks + 1,)),
        ],
        compiler_params=params(62),
        name="hand_on",
    )(value, grad)


def column_picks(channels, columns):
    column = lax.axis_index("dp") * columns + jnp.arange(columns)
    part = column // (channels * channels)
    c = column // channels % channels
    o = column % channels
    index = jnp.arange(2 * channels)[:, None]
    spec_real = (index == c).astype(F32)
    spec_imag = (index == channels + c).astype(F32) * jnp.where(part == 0, 1.0, -1.0)
    dual_same = (index == part * channels + o).astype(F32)
    dual_other = (index == (1 - part) * channels + o).astype(F32)
    return jnp.stack([spec_real, dual_same, spec_imag, dual_other]).astype(BF16)


def local(feats, grains, spec_weight, taps, point_weight, bias, cotangent):
    samples_here, channels, planes = feats.shape[:3]
    assert samples_here == 1
    slabs = lax.axis_size("slab")
    dp = lax.axis_size("dp")
    plan = Plan(planes, slabs)
    mode_rows = spec_weight.shape[0]
    half = lambda t: jnp.asarray(t.astype(jnp.bfloat16))
    ty, tx = half(plan.y_forward), half(plan.x_forward)
    tyi, txi = half(plan.y_inverse), half(plan.x_inverse)
    zf = jnp.asarray(plan.z_forward.astype(np.float32))
    zi = jnp.asarray(plan.z_inverse.astype(np.float32))
    cell_scale = 1.0 / math.sqrt(NX * NY * NZ)
    mode_scale = 1.0 / math.sqrt(KX * KY * KZ)
    jl, kq, kk, groups = plan.jl, plan.kq, plan.kk, plan.groups

    def swap(value):
        return lax.all_to_all(value, "slab", split_axis=0, concat_axis=0, tiled=True)

    def scatter_modes(modes):
        if plan.lead == 1 or kq > 1 or plan.used < plan.width:
            modes = modes[..., : plan.used].reshape(plan.lead, channels, -1, 2 * jl, planes, kq, kk)
            modes = modes.transpose(0, 2, 5, 1, 3, 4, 6)
        return swap(modes.reshape(slabs, channels * 2 * jl, plan.pk))

    def gather_planes(planar):
        planar = swap(planar)
        if plan.lead == 1 or kq > 1 or plan.used < plan.width:
            planar = planar.reshape(plan.lead, groups // plan.lead, kq, channels, 2 * jl, planes, kk)
            planar = planar.transpose(0, 3, 1, 4, 5, 2, 6).reshape(
                plan.lead, channels, 2 * KX // plan.lead, plan.used)
            return jnp.pad(planar, ((0, 0), (0, 0), (0, 0), (0, plan.width - plan.used)))
        return planar.reshape(plan.lead, channels, 2 * KX // plan.lead, plan.width)

    up = [(i, i + 1) for i in range(slabs - 1)]
    down = [(j, i) for i, j in up]
    field = feats[0]
    columns = 2 * channels * channels // dp
    weights = spec_weight.reshape(mode_rows * KZ, 2 * channels * channels)
    fused = (
        mode_rows * KZ == planes * NX and 2 * channels * channels == 128 * channels // 2 and
        plan.lead == slabs and kq == 1 and plan.used == plan.width and planes % 2 == 0 and planes > 4
        and dp > 1 and channels * channels % columns == 0 and columns % 128 == 0
    )
    if fused:
        zfb = half(plan.z_forward.reshape(slabs * plan.pk, 2 * plan.lanes))
        zib = half(plan.z_inverse)
        grad_feats, grad_spec = layer_call(
            plan, taps, field, cotangent[0], weights.reshape(planes, NX, -1), grains[0], bias, point_weight, ty, tx, tyi, txi, zfb, zib,
            cell_scale, mode_scale, dp)
        grad_feats, grad_spec = hand_on_call(grad_feats, grad_spec)
        return grad_feats[None], grad_spec.reshape(mode_rows, KZ, columns)
    weights = weights.T.reshape(2, channels, channels, mode_rows * KZ)
    kp, kt = point_weight, point_weight.T
    pick = column_picks(channels, columns)
    scale = 1.0 / (samples_here * dp)
    pick = pick * jnp.array([scale, 1, scale, 1], BF16)[:, None, None]
    low, high = rims_call(field)
    before = lax.ppermute(high, "slab", up)
    after = lax.ppermute(low, "slab", down)
    received = scatter_modes(planes_call(plan, field, ty, tx))
    smooth = stencil_call(plan, taps, field, (before, after), False)
    received, smooth = lax.optimization_barrier((received, smooth))
    mixed, spec = mix_call(plan, received, weights, zf, zi, False, cell_scale, mode_scale)
    mixed, smooth = lax.optimization_barrier((mixed, smooth))
    modes = gather_planes(mixed)
    smooth = stencil_call(plan, taps, field, (before, after), False, smooth)
    spread, first, last, dual_modes = middle_call(
        plan, grains[0], smooth, cotangent[0], modes, bias, kp, kt, txi, tyi, ty, tx)
    spread_before = lax.ppermute(last, "slab", up)
    spread_after = lax.ppermute(first, "slab", down)
    received = scatter_modes(dual_modes)
    partial = stencil_call(plan, taps, spread, (), True)
    received, partial = lax.optimization_barrier((received, partial))
    back, dual = mix_call(plan, received, weights, zf, zi, True, mode_scale, cell_scale)
    back, partial = lax.optimization_barrier((back, partial))
    back_modes = gather_planes(back)
    partial = stencil_call(plan, taps, spread, (), True, partial)
    both = jnp.concatenate([spec, dual], axis=1)
    both = lax.all_to_all(
        jnp.broadcast_to(both[None], (dp,) + both.shape), "dp", split_axis=0, concat_axis=0, tiled=True)
    grad_spec = grad_call(both, pick)
    grad_feats = final_call(plan, taps, partial, spread_before, spread_after, back_modes, txi, tyi)
    return grad_feats[None], grad_spec.reshape(mode_rows, KZ, columns)


def solution(mesh):
    in_specs = (
        P(("grp", "dp"), None, "slab", None, None),
        P(("grp", "dp"), "slab", None, None),
        P("slab", None, None),
        P(),
        P(),
        P(),
        P(("grp", "dp"), None, "slab", None, None),
    )
    out_specs = (P(("grp", "dp"), None, "slab", None, None), P("slab", "grp", "dp"))
    return jax.shard_map(local, mesh=mesh, in_specs=in_specs, out_specs=out_specs, check_vma=False)
```

```python
import functools
import math

import jax
import jax.numpy as jnp
import numpy as np
from jax import lax
from jax.experimental import pallas as pl
from jax.experimental.pallas import tpu as pltpu
from jax.sharding import PartitionSpec as P

NX = 128
NY = 128
NZ = 32
KX = 16
KY = 16
KZ = 16
F32 = jnp.float32
BF16 = jnp.bfloat16
HIGHEST = lax.Precision.HIGHEST
MIB = 1 << 20


def waves(count, length):
    index = np.arange(count)
    frequency = np.where(index < count // 2, index, length - count + index)
    phases = frequency[:, None] * np.arange(length)[None, :] % length
    angles = phases * (2.0 * math.pi / length)
    return np.cos(angles), np.sin(angles)


class Plan:
    def __init__(self, planes, slabs):
        self.planes = planes
        self.slabs = slabs
        rows = KX * KY // slabs
        self.rows = rows
        self.groups = slabs if rows >= KY else KX
        self.jl = KX // self.groups
        self.kq = slabs // self.groups
        self.kk = KY // self.kq
        self.width = max(128, planes * KY)
        self.used = planes * KY
        self.pk = planes * self.kk
        self.lanes = self.kk * KZ
        self.lead = self.groups if (2 * self.jl) % 8 == 0 else 1
        width, jl = self.width, self.jl
        cos_x, sin_x = waves(KX, NX)
        cos_y, sin_y = waves(KY, NY)
        cos_z, sin_z = waves(KZ, NZ)
        forward = np.zeros((planes, NY, 2, width))
        for z in range(planes):
            forward[z, :, 0, z * KY : (z + 1) * KY] = cos_y.T
            forward[z, :, 1, z * KY : (z + 1) * KY] = -sin_y.T
        forward = forward.reshape(planes * NY, 2 * width)
        self.y_forward = forward
        self.y_inverse = forward.T
        table = np.zeros((self.groups, 2, jl, 2, NX))
        back = np.zeros((2, NX, self.groups, 2, jl))
        for j in range(KX):
            g, i = divmod(j, jl)
            table[g, 0, i, 0], table[g, 0, i, 1] = cos_x[j], sin_x[j]
            table[g, 1, i, 1], table[g, 1, i, 0] = cos_x[j], -sin_x[j]
            back[0, :, g, 0, i], back[0, :, g, 1, i] = cos_x[j], -sin_x[j]
            back[1, :, g, 1, i], back[1, :, g, 0, i] = cos_x[j], sin_x[j]
        self.x_forward = table.reshape(2 * KX, 2 * NX)
        self.x_inverse = back.reshape(2 * NX, 2 * KX)
        kk, pk, lanes = self.kk, self.pk, self.lanes
        zf = np.zeros((slabs, planes, kk, 2, kk, KZ))
        self.pw = max(128, pk)
        zi = np.zeros((slabs, 2, kk, KZ, 2, planes, kk))
        for s in range(slabs):
            for z in range(planes):
                c, n = cos_z[:, s * planes + z], sin_z[:, s * planes + z]
                for k in range(kk):
                    zf[s, z, k, 0, k], zf[s, z, k, 1, k] = c, n
                    zi[s, 0, k, :, 0, z, k], zi[s, 1, k, :, 0, z, k] = c, -n
                    zi[s, 1, k, :, 1, z, k], zi[s, 0, k, :, 1, z, k] = c, n
        self.z_forward = zf.reshape(slabs, pk, 2 * lanes)
        zi = zi.reshape(slabs, 2 * lanes, 2, pk)
        zi = np.pad(zi, ((0, 0), (0, 0), (0, 0), (0, self.pw - pk)))
        self.z_inverse = zi.reshape(slabs, 2 * lanes, 2 * self.pw)


def whole(shape):
    zeros = (0,) * len(shape)
    return pl.BlockSpec(shape, lambda *_: zeros)


def params(mib):
    return pltpu.CompilerParams(vmem_limit_bytes=mib * MIB)


def dot(a, b, **kw):
    return jnp.dot(a, b, preferred_element_type=F32, **kw)


def channel_modes(plan, planes_of, ty, tx):
    field = jnp.concatenate([planes_of(z) for z in range(plan.planes)], axis=1)
    along = dot(field, ty).astype(BF16)
    stacked = jnp.concatenate([along[:, : plan.width], along[:, plan.width :]], axis=0)
    return dot(tx, stacked)


def put_modes(plan, out_ref, c, value):
    if plan.lead == 1:
        out_ref[0, c] = value.astype(BF16)
    else:
        step = 2 * KX // plan.lead
        for g in range(plan.lead):
            out_ref[g, c] = value[g * step : (g + 1) * step].astype(BF16)


def get_modes(plan, ref, c):
    if plan.lead == 1:
        return ref[0, c]
    parts = [ref[g, c].astype(F32) for g in range(plan.lead)]
    return jnp.concatenate(parts, axis=0).astype(BF16)


def planes_kernel(plan, batch, x_ref, ty_ref, tx_ref, out_ref):
    for c in range(batch):
        value = channel_modes(plan, lambda z: x_ref[c, z], ty_ref[...], tx_ref[...])
        put_modes(plan, out_ref, c, value)


def planes_call(plan, field, ty, tx):
    channels, planes = field.shape[:2]
    batch = 4
    step = 2 * KX // plan.lead
    return pl.pallas_call(
        functools.partial(planes_kernel, plan, batch),
        grid=(channels // batch,),
        in_specs=[
            pl.BlockSpec((batch, planes, NX, NY), lambda i: (i, 0, 0, 0)),
            whole(ty.shape),
            whole(tx.shape),
        ],
        out_specs=pl.BlockSpec((plan.lead, batch, step, plan.width), lambda i: (0, i, 0, 0)),
        out_shape=jax.ShapeDtypeStruct((plan.lead, channels, step, plan.width), BF16),
        compiler_params=params(60),
        cost_estimate=pl.CostEstimate(
            flops=2 * channels * NX * planes * NY * 256, bytes_accessed=field.size * 2, transcendentals=0
        ),
        name="plane_modes",
    )(field, ty, tx)


def rims_kernel(low_ref, high_ref, first_ref, last_ref):
    first_ref[...] = low_ref[:, 0]
    last_ref[...] = high_ref[:, 0]


def rims_call(field):
    channels, planes = field.shape[:2]
    batch = 8
    rim = pl.BlockSpec((batch, NX, NY), lambda i: (i, 0, 0))
    shape = jax.ShapeDtypeStruct((channels, NX, NY), field.dtype)
    return pl.pallas_call(
        rims_kernel,
        grid=(channels // batch,),
        in_specs=[
            pl.BlockSpec((batch, 1, NX, NY), lambda i: (i, 0, 0, 0)),
            pl.BlockSpec((batch, 1, NX, NY), lambda i: (i, planes - 1, 0, 0)),
        ],
        out_specs=[rim, rim],
        out_shape=[shape, shape],
        compiler_params=params(60),
        name="rims",
    )(field, field)


def bands(taps_ref, c, adjoint, group, band_ref):
    row = lax.broadcasted_iota(jnp.int32, (NY, NY), 0)
    col = lax.broadcasted_iota(jnp.int32, (NY, NY), 1)
    diff = row - col
    for dz in range(3):
        for dx in range(3):
            base = 9 * dz + 3 * dx
            t = [taps_ref[base + i, c] for i in range(3)]
            if adjoint:
                t = t[::-1]
            band = jnp.where(
                diff == 0,
                t[1],
                jnp.where(diff == 1, t[2], jnp.where(diff == -1, t[0], 0.0)),
            ).astype(BF16)
            zi, xi = (2 - dz, 2 - dx) if adjoint else (dz, dx)
            for z in range(group):
                top = (xi * (group + 2) + z + zi) * NY
                band_ref[top : top + NY, z * NY : (z + 1) * NY] = band


def shifted(plan, x_ref, before_ref, after_ref, c, rows_ref):
    edge = lax.broadcasted_iota(jnp.int32, (NX, NY), 0)
    for i in range(plan.planes + 2):
        if before_ref is None and i in (0, plan.planes + 1):
            continue
        if i == 0:
            plane = before_ref[c]
        elif i == plan.planes + 1:
            plane = after_ref[c]
        else:
            plane = x_ref[c, i - 1]
        wide = plane.astype(F32)
        lower = jnp.where(edge == 0, 0.0, pltpu.roll(wide, 1, 0))
        upper = jnp.where(edge == NX - 1, 0.0, pltpu.roll(wide, NX - 1, 0))
        cols = slice(i * NY, (i + 1) * NY)
        rows_ref[0, :, cols] = lower.astype(BF16)
        rows_ref[1, :, cols] = plane
        rows_ref[2, :, cols] = upper.astype(BF16)


def stencil_kernel(plan, batch, adjoint, group, offset, *refs):
    if offset:
        refs = refs[1:]
    if adjoint:
        taps_ref, x_ref, out_ref, band_ref, rows_ref = refs
        before_ref = after_ref = None
    else:
        taps_ref, x_ref, before_ref, after_ref, out_ref, band_ref, rows_ref = refs

    @pl.when(pl.program_id(0) == 0)
    def _():
        band_ref[...] = jnp.zeros_like(band_ref)
        rows_ref[...] = jnp.zeros_like(rows_ref)

    first = pl.program_id(0) * batch + offset
    for c in range(batch):
        half = c % 2
        band, rows = band_ref.at[half], rows_ref.at[half]
        bands(taps_ref, first + c, adjoint, group, band)
        shifted(plan, x_ref, before_ref, after_ref, c, rows)
        for z in range(0, plan.planes, group):
            cols = slice(z * NY, (z + group + 2) * NY)
            near = jnp.concatenate([rows[d, :, cols] for d in range(3)], axis=1)
            total = dot(near, band[...])
            for i in range(group):
                out_ref[c, z + i] = total[:, i * NY : (i + 1) * NY].astype(BF16)


def stencil_call(plan, taps, field, rims, adjoint, done=None):
    channels, planes = field.shape[:2]
    batch = 4
    group = 2 if planes % 2 == 0 else 1
    offset = 0 if done is None else channels // 2
    skip = offset // batch
    block = pl.BlockSpec((batch, planes, NX, NY), lambda i: (i + skip, 0, 0, 0))
    specs = [pl.BlockSpec(memory_space=pltpu.SMEM), block]
    specs += [pl.BlockSpec((batch, NX, NY), lambda i: (i + skip, 0, 0))] * len(rims)
    operands = (taps, field, *rims)
    if done is not None:
        specs = [pl.BlockSpec(memory_space=pl.ANY)] + specs
        operands = (done,) + operands
    return pl.pallas_call(
        functools.partial(stencil_kernel, plan, batch, adjoint, group, offset),
        grid=(channels // 2 // batch,),
        in_specs=specs,
        out_specs=block,
        out_shape=jax.ShapeDtypeStruct(field.shape, BF16),
        input_output_aliases={} if done is None else {0: 0},
        scratch_shapes=[
            pltpu.VMEM((2, 3 * (group + 2) * NY, group * NY), BF16),
            pltpu.VMEM((2, 3, NX, (planes + 2) * NY), BF16),
        ],
        compiler_params=params(60),
        cost_estimate=pl.CostEstimate(
            flops=field.size * 3 * (group + 2) * NY, bytes_accessed=field.size * 2, transcendentals=0
        ),
        name="stencil_back" if adjoint else "stencil",
    )(*operands)


def final_kernel(plan, batch, taps_ref, x_ref, before_ref, after_ref, m_ref, tx_ref, ty_ref, out_ref):
    first = pl.program_id(0) * batch
    edge = lax.broadcasted_iota(jnp.int32, (NX, NY), 0)
    diff = lax.broadcasted_iota(jnp.int32, (NY, NY), 0) - lax.broadcasted_iota(jnp.int32, (NY, NY), 1)

    def rim(c, plane, dz):
        wide = plane.astype(F32)
        lower = jnp.where(edge == 0, 0.0, pltpu.roll(wide, 1, 0)).astype(BF16)
        upper = jnp.where(edge == NX - 1, 0.0, pltpu.roll(wide, NX - 1, 0)).astype(BF16)
        band = []
        for dx in (2, 1, 0):
            t = [taps_ref[9 * dz + 3 * dx + i, first + c] for i in range(3)]
            band.append(jnp.where(
                diff == 0,
                t[1],
                jnp.where(diff == 1, t[0], jnp.where(diff == -1, t[2], 0.0)),
            ).astype(BF16))
        return dot(jnp.concatenate([lower, plane, upper], axis=1), jnp.concatenate(band, axis=0))

    for c in range(batch):
        wave = dot(tx_ref[...], get_modes(plan, m_ref, c)).astype(BF16)
        wave = jnp.concatenate([wave[:NX], wave[NX:]], axis=1)
        full = dot(wave, ty_ref[...])
        for z in range(plan.planes):
            total = full[:, z * NY : (z + 1) * NY] + x_ref[c, z].astype(F32)
            if z == 0:
                total = total + rim(c, before_ref[c], 2)
            if z == plan.planes - 1:
                total = total + rim(c, after_ref[c], 0)
            out_ref[c, z] = total.astype(BF16)


def final_call(plan, taps, partial, before, after, modes, tx, ty):
    channels, planes = partial.shape[:2]
    batch = 4
    block = pl.BlockSpec((batch, planes, NX, NY), lambda i: (i, 0, 0, 0))
    rim = pl.BlockSpec((batch, NX, NY), lambda i: (i, 0, 0))
    return pl.pallas_call(
        functools.partial(final_kernel, plan, batch),
        grid=(channels // batch,),
        in_specs=[
            pl.BlockSpec(memory_space=pltpu.SMEM),
            block,
            rim,
            rim,
            pl.BlockSpec((modes.shape[0], batch) + modes.shape[2:], lambda i: (0, i, 0, 0)),
            whole(tx.shape),
            whole(ty.shape),
        ],
        out_specs=block,
        out_shape=jax.ShapeDtypeStruct(partial.shape, BF16),
        compiler_params=params(60),
        cost_estimate=pl.CostEstimate(
            flops=2 * partial.size * 512, bytes_accessed=partial.size * 4, transcendentals=0
        ),
        name="final",
    )(taps, partial, before, after, modes, tx, ty)


def mix_kernel(plan, channels, adjoint, scale_in, scale_out, r_ref, zf_ref, zi_ref, w_ref,
               out_ref, turned_ref, z_scr, s_scr, m_scr, o_scr):
    jl, lanes, pk, pw = plan.jl, plan.lanes, plan.pk, plan.pw
    chunks = 2 * lanes // 128
    total = None
    for s in range(plan.slabs):
        part = dot(r_ref[s].astype(F32), zf_ref[s], precision=HIGHEST)
        total = part if total is None else total + part
    total = total * scale_in
    for q in range(chunks):
        z_scr[q] = total[:, q * 128 : (q + 1) * 128]

    def rows_of(start):
        return jnp.concatenate(
            [z_scr[q, pl.ds(start, channels, stride=2 * jl), :] for q in range(chunks)], axis=1)

    for j in range(jl):
        re, im = rows_of(j), rows_of(jl + j)
        real = re[:, :lanes] + im[:, lanes:]
        imag = im[:, :lanes] - re[:, lanes:]
        s_scr[j, 0] = real
        s_scr[j, 1] = imag
        both = jnp.concatenate([real, imag], axis=0)
        turned_ref[j * lanes : (j + 1) * lanes, :] = both.T.astype(BF16)
        cols = slice(j * lanes, (j + 1) * lanes)
        rows = slice(j * channels, (j + 1) * channels)
        if adjoint:
            for c in range(channels):
                wr = w_ref[0, c, :, cols].astype(F32)
                wi = w_ref[1, c, :, cols].astype(F32)
                br = jnp.sum(wr * real + wi * imag, axis=0, keepdims=True)
                bi = jnp.sum(wr * imag - wi * real, axis=0, keepdims=True)
                m_scr[j * channels + c : j * channels + c + 1, :lanes] = br
                m_scr[j * channels + c : j * channels + c + 1, lanes:] = bi
        else:
            mr = jnp.zeros((channels, lanes), F32)
            mi = jnp.zeros((channels, lanes), F32)
            for c in range(channels):
                wr = w_ref[0, c, :, cols].astype(F32)
                wi = w_ref[1, c, :, cols].astype(F32)
                sr = s_scr[j, 0, c : c + 1, :]
                si = s_scr[j, 1, c : c + 1, :]
                mr = mr + (sr * wr - si * wi)
                mi = mi + (sr * wi + si * wr)
            m_scr[rows, :lanes] = mr
            m_scr[rows, lanes:] = mi
    mixed = m_scr[...] * scale_out
    for s in range(plan.slabs):
        planar = dot(mixed, zi_ref[s], precision=HIGHEST)
        for j in range(jl):
            for part in range(2):
                o_scr[pl.ds(part * jl + j, channels, stride=2 * jl), :] = planar[
                    j * channels : (j + 1) * channels, part * pw : (part + 1) * pw
                ]
        out_ref[s] = o_scr[:, :pk].astype(BF16)


def mix_call(plan, received, weights, zf, zi, adjoint, scale_in, scale_out):
    channels = weights.shape[1]
    rows = channels * 2 * plan.jl
    modes = plan.jl * plan.lanes
    return pl.pallas_call(
        functools.partial(mix_kernel, plan, channels, adjoint, scale_in, scale_out),
        out_shape=(
            jax.ShapeDtypeStruct((plan.slabs, rows, plan.pk), BF16),
            jax.ShapeDtypeStruct((modes, 2 * channels), BF16),
        ),
        scratch_shapes=[
            pltpu.VMEM((2 * plan.lanes // 128, rows, 128), F32),
            pltpu.VMEM((plan.jl, 2, channels, plan.lanes), F32),
            pltpu.VMEM((plan.jl * channels, 2 * plan.lanes), F32),
            pltpu.VMEM((rows, plan.pw), F32),
        ],
        compiler_params=params(60),
        name="mix_back" if adjoint else "mix",
    )(received, zf, zi, weights)


def middle_kernel(plan, channels, g_ref, sm_ref, cot_ref, m_ref, bias_ref, pw_ref, pt_ref,
                  txi_ref, tyi_ref, ty_ref, tx_ref,
                  spread_ref, first_ref, last_ref, modes_ref, wave_scr, delta_scr, move_scr, kp_ref, kt_ref):
    z = pl.program_id(0)
    planes = plan.planes
    width = plan.width

    @pl.when(z == 0)
    def _():
        def body(c, carry):
            wave = dot(txi_ref[...], get_modes(plan, m_ref, c)).astype(BF16)
            wave_scr[c, :, :width] = wave[:NX]
            wave_scr[c, :, width:] = wave[NX:]
            return carry
        lax.fori_loop(0, channels, body, 0, unroll=4)
        rows = channels * 16
        pick = lax.broadcasted_iota(jnp.int32, (rows, channels), 0) >> 4
        pick = pick == lax.broadcasted_iota(jnp.int32, (rows, channels), 1)
        pick = jnp.where(pick, 1.0, 0.0).astype(BF16)
        same = lax.broadcasted_iota(jnp.int32, (rows, rows), 0) & 15
        same = same == (lax.broadcasted_iota(jnp.int32, (rows, rows), 1) & 15)
        for src, dst in ((pt_ref, kp_ref), (pw_ref, kt_ref)):
            tall = dot(pick, src[...]).astype(BF16)
            full = lax.dot_general(tall, pick, (((1,), (1,)), ((), ())), preferred_element_type=F32)
            dst[...] = jnp.where(same, full, 0.0).astype(BF16)

    g = g_ref[0]
    row = lax.broadcasted_iota(jnp.int32, (NX, NY), 0)
    col = lax.broadcasted_iota(jnp.int32, (NX, NY), 1)

    def differs(shift, axis, inside):
        return jnp.where((g != pltpu.roll(g, shift, axis)) & inside, 0.25, 0.0)

    move_scr[...] = (
        0.25
        + differs(1, 0, row > 0)
        + differs(NX - 1, 0, row < NX - 1)
        + differs(1, 1, col > 0)
        + differs(NY - 1, 1, col < NY - 1)
    )
    height = channels * 16
    bias = bias_ref[...]

    def body(pair, carry):
        starts = [pair * 32 + 16 * i for i in range(2)]

        def tile(ref):
            return [ref[:, 0, pl.ds(x, 16), :].reshape(height, NY) for x in starts]

        mixed = dot(kp_ref[...], jnp.concatenate(tile(sm_ref), axis=1))
        cot = tile(cot_ref)
        deltas = []
        for i, x in enumerate(starts):
            moving = move_scr[pl.ds(x, 16), :]
            wave = wave_scr[:, pl.ds(x, 16), :].reshape(height, 2 * width)
            spectral = dot(wave, tyi_ref[...])
            local = mixed[:, i * NY : (i + 1) * NY].reshape(channels, 16, NY) * moving[None]
            pre = spectral.reshape(channels, 16, NY) + local + bias
            gate = 0.5 + 0.5 * jnp.tanh(0.5 * pre)
            delta = cot[i].astype(F32).reshape(channels, 16, NY) * gate * (1.0 + pre * (1.0 - gate))
            delta = delta.astype(BF16)
            delta_scr[:, z, pl.ds(x, 16), :] = delta
            deltas.append(delta.reshape(height, NY))
        turned = dot(kt_ref[...], jnp.concatenate(deltas, axis=1))
        for i, x in enumerate(starts):
            moving = move_scr[pl.ds(x, 16), :]
            value = turned[:, i * NY : (i + 1) * NY].reshape(channels, 16, NY) * moving[None]
            spread_ref[:, 0, pl.ds(x, 16), :] = value.astype(BF16)
        return carry

    for pair in range(NX // 32):
        body(pair, 0)

    @pl.when(z == 0)
    def _():
        first_ref[...] = spread_ref[:, 0]

    @pl.when(z == planes - 1)
    def _():
        last_ref[...] = spread_ref[:, 0]

        def body(i, carry):
            for c in (2 * i, 2 * i + 1):
                value = channel_modes(plan, lambda p: delta_scr[c, p], ty_ref[...], tx_ref[...])
                put_modes(plan, modes_ref, c, value)
            return carry

        lax.fori_loop(0, channels // 2, body, 0)


def middle_call(plan, grains, smooth, cotangent, modes, bias, kp, kt, txi, tyi, ty, tx):
    channels, planes = smooth.shape[:2]
    width = plan.width
    block = pl.BlockSpec((channels, 1, NX, NY), lambda z: (0, z, 0, 0))
    rim = jax.ShapeDtypeStruct((channels, NX, NY), BF16)
    return pl.pallas_call(
        functools.partial(middle_kernel, plan, channels),
        grid=(planes,),
        in_specs=[
            pl.BlockSpec((1, NX, NY), lambda z: (z, 0, 0)),
            block,
            block,
            whole(modes.shape),
            whole((channels, 1, 1)),
            whole(kp.shape),
            whole(kt.shape),
            whole(txi.shape),
            pl.BlockSpec((2 * width, NY), lambda z: (0, z)),
            whole(ty.shape),
            whole(tx.shape),
        ],
        out_specs=[block, whole(rim.shape), whole(rim.shape), whole(modes.shape)],
        out_shape=[jax.ShapeDtypeStruct(smooth.shape, BF16), rim, rim,
                   jax.ShapeDtypeStruct(modes.shape, BF16)],
        scratch_shapes=[
            pltpu.VMEM((channels, NX, 2 * width), BF16),
            pltpu.VMEM((channels, planes, NX, NY), BF16),
            pltpu.VMEM((NX, NY), F32),
            pltpu.VMEM((16 * channels, 16 * channels), BF16),
            pltpu.VMEM((16 * channels, 16 * channels), BF16),
        ],
        compiler_params=params(60),
        name="middle",
    )(grains, smooth, cotangent, modes, bias.reshape(channels, 1, 1), kp, kt, txi, tyi, ty, tx)


def grad_kernel(samples, both_ref, e_ref, out_ref):
    total = None
    for i in range(samples):
        half = both_ref.shape[-1] // 2
        spec, dual = both_ref[i, :, :half], both_ref[i, :, half:]
        term = dot(spec, e_ref[0]) * dot(dual, e_ref[1]) + dot(spec, e_ref[2]) * dot(dual, e_ref[3])
        total = term if total is None else total + term
    out_ref[...] = total


def grad_call(both, pick):
    samples, modes, width = both.shape
    columns = pick.shape[-1]
    batch = min(256, modes)
    return pl.pallas_call(
        functools.partial(grad_kernel, samples),
        grid=(modes // batch,),
        in_specs=[
            pl.BlockSpec((samples, batch, width), lambda i: (0, i, 0)),
            whole(pick.shape),
        ],
        out_specs=pl.BlockSpec((batch, columns), lambda i: (i, 0)),
        out_shape=jax.ShapeDtypeStruct((modes, columns), F32),
        compiler_params=params(60),
        cost_estimate=pl.CostEstimate(
            flops=8 * samples * modes * width * columns, bytes_accessed=modes * columns * 4, transcendentals=0
        ),
        name="grad_modes",
    )(both, pick)


def slab_peer(me, d, slabs):
    return lax.rem(me + d, slabs)


def enter(sizes):
    barrier = pltpu.get_barrier_semaphore()
    total = 0
    for axis, size in sizes.items():
        me = lax.axis_index(axis)
        for d in range(1, size):
            pl.semaphore_signal(
                barrier, inc=1, device_id={axis: slab_peer(me, d, size)}, device_id_type=pl.DeviceIdType.MESH)
        total += size - 1
    pl.semaphore_wait(barrier, total)


def exchange(me, slabs, send_ref, recv_ref, send_sem, recv_sem):
    copies = []
    for d in range(1, slabs):
        peer = slab_peer(me, d, slabs)
        copies.append(pltpu.make_async_remote_copy(
            src_ref=send_ref.at[peer],
            dst_ref=recv_ref.at[me],
            send_sem=send_sem.at[d - 1],
            recv_sem=recv_sem.at[d - 1],
            device_id={"slab": peer},
            device_id_type=pl.DeviceIdType.MESH,
        ))
    return copies


def halo_copies(me, slabs, field_ref, before_ref, after_ref, planes, rows, across, index, send_sem, recv_sem):
    up = pltpu.make_async_remote_copy(
        src_ref=field_ref.at[rows, planes - 1, across],
        dst_ref=before_ref.at[rows, across],
        send_sem=send_sem.at[0, index],
        recv_sem=recv_sem.at[0, index],
        device_id={"slab": lax.rem(me + 1, slabs)},
        device_id_type=pl.DeviceIdType.MESH,
    )
    down = pltpu.make_async_remote_copy(
        src_ref=field_ref.at[rows, 0, across],
        dst_ref=after_ref.at[rows, across],
        send_sem=send_sem.at[1, index],
        recv_sem=recv_sem.at[1, index],
        device_id={"slab": lax.rem(me + slabs - 1, slabs)},
        device_id_type=pl.DeviceIdType.MESH,
    )
    return up, down


def halo_start(me, slabs, copies):
    up, down = copies

    @pl.when(me < slabs - 1)
    def _():
        up.start()

    @pl.when(me > 0)
    def _():
        down.start()


def halo_wait_recv(me, slabs, copies):
    up, down = copies

    @pl.when(me > 0)
    def _():
        up.wait_recv()

    @pl.when(me < slabs - 1)
    def _():
        down.wait_recv()


def halo_wait_send(me, slabs, copies):
    up, down = copies

    @pl.when(me < slabs - 1)
    def _():
        up.wait_send()

    @pl.when(me > 0)
    def _():
        down.wait_send()


def batch_modes(plan, out_ref, row, lines, ty_ref, tx_ref):
    count = len(lines)
    along = dot(jnp.concatenate(lines, axis=0), ty_ref[...]).astype(BF16)
    width = plan.width
    values = []
    for c in range(0, count, 2):
        top = along[c * NX : (c + 1) * NX]
        low = along[(c + 1) * NX : (c + 2) * NX]
        pair = jnp.concatenate([
            jnp.concatenate([top[:, :width], low[:, :width]], axis=1),
            jnp.concatenate([top[:, width:], low[:, width:]], axis=1),
        ], axis=0)
        both = dot(tx_ref[...], pair)
        values += [both[:, :width], both[:, width:]]
    step = 2 * KX // plan.lead
    for g in range(plan.lead):
        part = jnp.concatenate([v[g * step : (g + 1) * step] for v in values], axis=0)
        out_ref[g, pl.ds(row, count * step), :] = part.astype(BF16)


def band_masks():
    diff = lax.broadcasted_iota(jnp.int32, (NY, NY), 0) - lax.broadcasted_iota(jnp.int32, (NY, NY), 1)
    return diff == 1, diff == 0, diff == -1


def fill_band(taps_ref, c, adjoint, masks, band_ref):
    low, mid, upp = masks
    for dz in range(3):
        for dx in range(3):
            base = 9 * dz + 3 * dx
            t = [taps_ref[base + i, c] for i in range(3)]
            if adjoint:
                t = t[::-1]
            band = jnp.where(mid, t[1], jnp.where(low, t[2], jnp.where(upp, t[0], 0.0))).astype(BF16)
            zi, xi = (2 - dz, 2 - dx) if adjoint else (dz, dx)
            for z in range(2):
                top = (xi * 4 + z + zi) * NY
                band_ref[top : top + NY, z * NY : (z + 1) * NY] = band


def stencil_part(plan, taps_ref, x_ref, before_ref, after_ref, c, groups, adjoint, masks, out_ref,
                 band_ref, wide_ref, lower_ref, upper_ref):
    fill_band(taps_ref, c, adjoint, masks, band_ref)
    planes = plan.planes

    def plane(i):
        if i == 0:
            return before_ref[c]
        if i == planes + 1:
            return after_ref[c]
        return x_ref[c, i - 1]

    needed = sorted({2 * g + i for g in groups for i in range(4)})
    slot = {i: n for n, i in enumerate(needed)}
    for i in needed:
        n = slot[i]
        wide_ref[n, 8 : NX + 8, :] = plane(i).astype(F32)
        lower_ref[n] = wide_ref[n, 7 : NX + 7, :].astype(BF16)
        upper_ref[n] = wide_ref[n, 9 : NX + 9, :].astype(BF16)

    def moved(dx, i):
        if dx == 1:
            return plane(i)
        return (lower_ref if dx == 0 else upper_ref)[slot[i]]

    near = jnp.concatenate([
        jnp.concatenate([moved(dx, 2 * g + i) for dx in range(3) for i in range(4)], axis=1)
        for g in groups
    ], axis=0)
    total = dot(near, band_ref[...])
    for n, g in enumerate(groups):
        for i in range(2):
            out_ref[c, 2 * g + i] = total[n * NX : (n + 1) * NX, i * NY : (i + 1) * NY].astype(BF16)


def mix_modes(plan, channels, me, adjoint, scale_in, scale_out, own_ref, r_ref, zf_ref, zi_ref, w_ref,
              out_ref, turned_ref, z_scr, s_scr, m_scr, o_scr):
    jl, lanes, pk, pw = plan.jl, plan.lanes, plan.pk, plan.pw
    chunks = 2 * lanes // 128
    r_ref[me] = own_ref[me]
    total = dot(jnp.concatenate([r_ref[s] for s in range(plan.slabs)], axis=1), zf_ref[...])
    total = total * scale_in
    for q in range(chunks):
        z_scr[q] = total[:, q * 128 : (q + 1) * 128]

    def rows_of(start):
        return jnp.concatenate(
            [z_scr[q, pl.ds(start, channels, stride=2 * jl), :] for q in range(chunks)], axis=1)

    for j in range(jl):
        re, im = rows_of(j), rows_of(jl + j)
        real = re[:, :lanes] + im[:, lanes:]
        imag = im[:, :lanes] - re[:, lanes:]
        s_scr[j, 0] = real
        s_scr[j, 1] = imag
        both = jnp.concatenate([real, imag], axis=0)
        turned_ref[j * lanes : (j + 1) * lanes, :] = both.T.astype(BF16)
        cols = slice(j * lanes, (j + 1) * lanes)
        rows = slice(j * channels, (j + 1) * channels)
        if adjoint:
            def body(i, carry):
                parts = []
                for k in range(8):
                    c = 8 * i + k
                    wr = w_ref[0, c, :, cols].astype(F32)
                    wi = w_ref[1, c, :, cols].astype(F32)
                    real, imag = s_scr[j, 0], s_scr[j, 1]
                    br = jnp.sum(wr * real + wi * imag, axis=0, keepdims=True)
                    bi = jnp.sum(wr * imag - wi * real, axis=0, keepdims=True)
                    parts.append(jnp.concatenate([br, bi], axis=1))
                m_scr[pl.ds(pl.multiple_of(j * channels + 8 * i, 8), 8), :] = jnp.concatenate(parts, axis=0)
                return carry
            lax.fori_loop(0, channels // 8, body, 0)
        else:
            def body(i, carry):
                mr, mi = carry
                for k in range(8):
                    c = 8 * i + k
                    wr = w_ref[0, c, :, cols].astype(F32)
                    wi = w_ref[1, c, :, cols].astype(F32)
                    sr = s_scr[j, 0, pl.ds(c, 1), :]
                    si = s_scr[j, 1, pl.ds(c, 1), :]
                    mr = mr + (sr * wr - si * wi)
                    mi = mi + (sr * wi + si * wr)
                return mr, mi
            zero = jnp.zeros((channels, lanes), F32)
            mr, mi = lax.fori_loop(0, channels // 8, body, (zero, zero))
            m_scr[rows, :lanes] = mr
            m_scr[rows, lanes:] = mi
    mixed = (m_scr[...] * scale_out).astype(BF16)
    for s in range(plan.slabs):
        planar = dot(mixed, zi_ref[s])
        for j in range(jl):
            for part in range(2):
                o_scr[pl.ds(part * jl + j, channels, stride=2 * jl), :] = planar[
                    j * channels : (j + 1) * channels, part * pw : (part + 1) * pw
                ]
        out_ref[s] = o_scr[:, :pk].astype(BF16)


def mobility(g_ref, z, move_ref):
    row = lax.broadcasted_iota(jnp.int32, (NX, NY), 0)
    col = lax.broadcasted_iota(jnp.int32, (NX, NY), 1)
    for i in range(2):
        g = g_ref[z + i]

        def differs(shift, axis, inside):
            return jnp.where((g != pltpu.roll(g, shift, axis)) & inside, 0.25, 0.0)

        move_ref[i] = (
            0.25
            + differs(1, 0, row > 0)
            + differs(NX - 1, 0, row < NX - 1)
            + differs(1, 1, col > 0)
            + differs(NY - 1, 1, col < NY - 1)
        )


def spread_weights(channels, src_ref, dst_ref, turned):
    rows = channels * 16
    pick = lax.broadcasted_iota(jnp.int32, (rows, channels), 0) >> 4
    pick = pick == lax.broadcasted_iota(jnp.int32, (rows, channels), 1)
    pick = jnp.where(pick, 1.0, 0.0).astype(BF16)
    same = lax.broadcasted_iota(jnp.int32, (rows, rows), 0) & 15
    same = same == (lax.broadcasted_iota(jnp.int32, (rows, rows), 1) & 15)
    axes = (((1,), (1 if turned else 0,)), ((), ()))
    tall = lax.dot_general(pick, src_ref[...], axes, preferred_element_type=F32).astype(BF16)
    full = lax.dot_general(tall, pick, (((1,), (1,)), ((), ())), preferred_element_type=F32)
    dst_ref[...] = jnp.where(same, full, 0.0).astype(BF16)


def turn_weights(channels, raw_ref, w_ref):
    block = 8 * channels
    per_part = channels // 8
    same = lax.broadcasted_iota(jnp.int32, (block, block), 0) == lax.broadcasted_iota(jnp.int32, (block, block), 1)
    unit = jnp.where(same, 1.0, 0.0).astype(BF16)

    def body(i, carry):
        for part in range(2):
            first = (part * per_part + i) * (block // 128)
            modes = raw_ref.shape[1] * raw_ref.shape[2]
            raw = jnp.concatenate([raw_ref[first + n].reshape(modes, 128) for n in range(block // 128)], axis=1)
            value = lax.dot_general(unit, raw, (((1,), (1,)), ((), ())), preferred_element_type=F32)
            w_ref[part, pl.ds(i * 8, 8)] = value.astype(BF16).reshape(8, channels, value.shape[1])
        return carry

    lax.fori_loop(0, per_part, body, 0)


def sample_picks(channels, columns, lane, samples, e_ref):
    size = 2 * channels
    row = lax.broadcasted_iota(jnp.int32, (size, columns), 0)
    column = lax.broadcasted_iota(jnp.int32, (size, columns), 1) + lane * columns
    part = lane * columns // (channels * channels)
    c = column // channels % channels
    sign = jnp.where(part == 0, 1.0, -1.0) / samples
    e_ref[...] = jnp.zeros_like(e_ref)
    e_ref[:size, :columns] = jnp.where(row == c, 1.0 / samples, 0.0).astype(BF16)
    e_ref[:size, columns : 2 * columns] = jnp.where(row == channels + c, sign, 0.0).astype(BF16)
    row = lax.broadcasted_iota(jnp.int32, (size, 128), 0)
    o = lax.broadcasted_iota(jnp.int32, (size, 128), 1) % channels
    e_ref[size:, 2 * columns : 2 * columns + 128] = jnp.where(row == part * channels + o, 1.0, 0.0).astype(BF16)
    e_ref[size:, 2 * columns + 128 :] = jnp.where(row == (1 - part) * channels + o, 1.0, 0.0).astype(BF16)


def sample_grads(columns, samples, both_ref, e_ref, out_ref):
    modes = both_ref.shape[1]
    batch = 256

    def body(i, carry):
        rows = pl.ds(pl.multiple_of(i * batch, batch), batch)
        totals = [None] * (columns // 128)
        for n in range(samples):
            wide = dot(both_ref[n, rows, :], e_ref[...])
            same = wide[:, 2 * columns : 2 * columns + 128]
            other = wide[:, 2 * columns + 128 :]
            for q in range(len(totals)):
                first = wide[:, q * 128 : (q + 1) * 128]
                second = wide[:, columns + q * 128 : columns + (q + 1) * 128]
                term = first * same + second * other
                totals[q] = term if totals[q] is None else totals[q] + term
        for q, total in enumerate(totals):
            out_ref[rows, q * 128 : (q + 1) * 128] = total
        return carry

    lax.fori_loop(0, modes // batch, body, 0)


def gate_pair(plan, channels, z, blocks, g_ref, sm_ref, cot_ref, wave_ref, tyi_ref, kp_ref, kt_ref, bias_ref, move_ref):
    mobility(g_ref, z, move_ref)
    height = channels * 16
    bias = bias_ref[:, 0:1, :]
    for k in blocks:
        rows = pl.ds(k * 16, 16)

        def tile(ref, n):
            return ref[:, z + n, rows, :].reshape(height, NY)

        mixed = dot(kp_ref[...], jnp.concatenate([tile(sm_ref, 0), tile(sm_ref, 1)], axis=1))
        wave = wave_ref[:, rows, :].reshape(height, 2 * plan.width)
        spectral = dot(wave, tyi_ref[z // 2])
        deltas = []
        for n in range(2):
            cols = slice(n * NY, (n + 1) * NY)
            moving = move_ref[n, rows, :]
            local = mixed[:, cols].reshape(channels, 16, NY) * moving[None]
            pre = spectral[:, cols].reshape(channels, 16, NY) + local + bias
            half = 0.5 * jnp.tanh(0.5 * pre)
            delta = tile(cot_ref, n).astype(F32).reshape(channels, 16, NY) * (0.5 + half) * (1.0 + pre * (0.5 - half))
            delta = delta.astype(BF16)
            cot_ref[:, z + n, rows, :] = delta
            deltas.append(delta.reshape(height, NY))
        turned = dot(kt_ref[...], jnp.concatenate(deltas, axis=1))
        for n in range(2):
            cols = slice(n * NY, (n + 1) * NY)
            value = turned[:, cols].reshape(channels, 16, NY) * move_ref[n, rows, :][None]
            sm_ref[:, z + n, rows, :] = value.astype(BF16)


def pair_waves(plan, read, tx_ref):
    width = plan.width
    pair = jnp.concatenate([
        jnp.concatenate([read(g, k).astype(F32) for g in range(plan.lead)], axis=0) for k in range(2)
    ], axis=1).astype(BF16)
    wave = dot(tx_ref[...], pair).astype(BF16)
    found = []
    for k in range(2):
        cols = slice(k * width, (k + 1) * width)
        found.append(jnp.concatenate([wave[:NX, cols], wave[NX:, cols]], axis=1))
    return found


def layer_kernel(plan, channels, peers, cell_scale, mode_scale,
                 taps_ref, bias_in, x_hbm, cot_hbm, w_hbm, g_ref, pw_ref,
                 ty_ref, tx_ref, tyi_ref, txi_ref, zf_ref, zi_ref,
                 out_hbm, grad_hbm,
                 x_ref, y_ref, cot_ref, w_ref, before_ref, after_ref, before2_ref, after2_ref,
                 send1, recv1, send2, recv2, send3, recv3, send4, recv4,
                 wave_ref, kp_ref, kt_ref, move_ref, bias_ref, spec_ref, dual_ref, both_ref, gather_ref, e_ref, grad_ref,
                 band_ref, wide_ref, lower_ref, upper_ref, z_scr, s_scr, m_scr, o_scr,
                 load_sem, cot_sem, w_sem, store_sem, grad_sem, halo_send, halo_recv, send_sem, recv_sem, both_send, both_recv):
    planes, slabs = plan.planes, plan.slabs
    columns = grad_ref.shape[1]
    me = lax.axis_index("slab")
    lane = lax.axis_index("dp")
    chunk = 8
    chunks = channels // chunk
    step = 2 * KX // plan.lead
    pairs = planes // 2
    inner, outer = list(range(1, pairs - 1)), [0, pairs - 1]

    def load(i):
        rows = pl.ds(i * chunk, chunk)
        return pltpu.make_async_copy(x_hbm.at[rows], x_ref.at[rows], load_sem.at[i])

    for i in range(chunks):
        load(i).start()
    enter({"slab": slabs, "dp": peers})
    part = 4
    pieces = channels // part
    quarter = pieces // 4

    def ahead(i):
        return halo_copies(me, slabs, x_hbm, before_ref, after_ref, planes, pl.ds(i * part, part), pl.ds(0, NX), i,
                           halo_send.at[0], halo_recv.at[0])

    def back(i, channel, count, start):
        return halo_copies(me, slabs, y_ref, before2_ref, after2_ref, planes, pl.ds(channel, count),
                           pl.ds(start, NX // 2), i, halo_send.at[1], halo_recv.at[1])

    def early():
        return back(pieces, 0, channels, 0)

    def late(i):
        return back(i, i * part, part, NX // 2)

    for i in range(quarter):
        halo_start(me, slabs, ahead(i))
    loads_w = [
        pltpu.make_async_copy(w_hbm.at[:, :, pl.ds(128 * i, 128)], cot_ref.at[i], w_sem.at[i])
        for i in range(w_hbm.shape[2] // 128)
    ]
    for copy in loads_w:
        copy.start()

    @pl.when(me == 0)
    def _():
        before_ref[...] = jnp.zeros_like(before_ref)
        before2_ref[...] = jnp.zeros_like(before2_ref)

    @pl.when(me == slabs - 1)
    def _():
        after_ref[...] = jnp.zeros_like(after_ref)
        after2_ref[...] = jnp.zeros_like(after2_ref)

    band_ref[...] = jnp.zeros_like(band_ref)
    for u in range(4):
        for n in range(wide_ref.shape[1]):
            wide_ref[u, n, 0:8, :] = jnp.zeros((8, NY), F32)
            wide_ref[u, n, NX + 8 : NX + 16, :] = jnp.zeros((8, NY), F32)
    for c in range(channels):
        bias_ref[c] = jnp.full((8, NY), bias_in[c], F32)
    spread_weights(channels, pw_ref, kp_ref, True)
    spread_weights(channels, pw_ref, kt_ref, False)
    sample_picks(channels, columns, lane, peers, e_ref)

    def spectra(src_ref, out_ref):
        def body(i, carry):
            if src_ref is x_ref:
                load(i).wait()
            lines = [jnp.concatenate([src_ref[i * chunk + c, z] for z in range(planes)], axis=1) for c in range(chunk)]
            batch_modes(plan, out_ref, pl.multiple_of(i * chunk * step, chunk * step), lines, ty_ref, tx_ref)
            return carry
        lax.fori_loop(0, chunks, body, 0)

    spectra(x_ref, send1)
    first = exchange(me, slabs, send1, recv1, send_sem.at[0], recv_sem.at[0])
    for copy in first:
        copy.start()
    for i in range(quarter, 2 * quarter):
        halo_start(me, slabs, ahead(i))

    masks = band_masks()

    def stencil(groups, adjoint):
        src, dst = (y_ref, x_ref) if adjoint else (x_ref, y_ref)
        low, high = (before2_ref, after2_ref) if adjoint else (before_ref, after_ref)

        def body(i, carry):
            for u in range(4):
                stencil_part(plan, taps_ref, src, low, high, i * 4 + u, groups, adjoint, masks, dst,
                             band_ref.at[u], wide_ref.at[u], lower_ref.at[u], upper_ref.at[u])
            return carry
        return body

    def gates(start, stride, blocks):
        def body(i, carry):
            gate_pair(plan, channels, 2 * (start + stride * i), blocks, g_ref, y_ref, cot_ref, wave_ref, tyi_ref,
                      kp_ref, kt_ref, bias_ref, move_ref)
            return carry
        return body

    for copy in loads_w:
        copy.wait()
    turn_weights(channels, cot_ref, w_ref)
    load_cot = pltpu.make_async_copy(cot_hbm, cot_ref, cot_sem)
    load_cot.start()
    lax.fori_loop(0, channels // 8, stencil(inner, False), 0)
    for copy in first:
        copy.wait()
    mix_modes(plan, channels, me, False, cell_scale, mode_scale, send1, recv1, zf_ref, zi_ref, w_ref,
              send2, spec_ref, z_scr, s_scr, m_scr, o_scr)
    second = exchange(me, slabs, send2, recv2, send_sem.at[1], recv_sem.at[1])
    for copy in second:
        copy.start()
    for i in range(2 * quarter, pieces):
        halo_start(me, slabs, ahead(i))
    recv2[me] = send2[me]
    lax.fori_loop(channels // 8, channels // 4, stencil(inner, False), 0)
    edge = stencil(outer, False)

    def smooth_edge(i, carry):
        halo_wait_recv(me, slabs, ahead(i))
        return edge(i, carry)

    lax.fori_loop(0, 2 * quarter, smooth_edge, 0)
    load_cot.wait()
    for copy in second:
        copy.wait()

    def unfold(src_ref):
        def body(i, carry):
            for k in range(0, 8, 2):
                c = i * 8 + k
                found = pl.ds(pl.multiple_of(c * step, 2 * step), 2 * step)
                for n, wave in enumerate(pair_waves(
                        plan, lambda g, j: src_ref[g, found, :][j * step : (j + 1) * step], txi_ref)):
                    wave_ref[c + n] = wave
            return carry
        lax.fori_loop(0, channels // 8, body, 0)

    unfold(recv2)
    lax.fori_loop(0, pairs - 2, gates(1, 1, range(NX // 16)), 0)
    lax.fori_loop(2 * quarter, pieces, smooth_edge, 0)
    lax.fori_loop(0, 2, gates(0, pairs - 1, range(NX // 32)), 0)
    halo_start(me, slabs, early())
    lax.fori_loop(0, 2, gates(0, pairs - 1, range(NX // 32, NX // 16)), 0)
    spectra(cot_ref, send3)
    third = exchange(me, slabs, send3, recv3, send_sem.at[2], recv_sem.at[2])
    for copy in third:
        copy.start()
    for i in range(2 * quarter):
        halo_start(me, slabs, late(i))
    lax.fori_loop(0, channels // 4, stencil(inner, True), 0)
    for copy in third:
        copy.wait()
    mix_modes(plan, channels, me, True, mode_scale, cell_scale, send3, recv3, zf_ref, zi_ref, w_ref,
              send4, dual_ref, z_scr, s_scr, m_scr, o_scr)
    fourth = exchange(me, slabs, send4, recv4, send_sem.at[3], recv_sem.at[3])
    for copy in fourth:
        copy.start()
    for i in range(2 * quarter, pieces):
        halo_start(me, slabs, late(i))
    recv4[me] = send4[me]
    both_ref[...] = jnp.concatenate([spec_ref[...], dual_ref[...]], axis=1)
    shares = []
    for d in range(1, peers):
        shares.append(pltpu.make_async_remote_copy(
            src_ref=both_ref,
            dst_ref=gather_ref.at[lane],
            send_sem=both_send.at[d - 1],
            recv_sem=both_recv.at[d - 1],
            device_id={"dp": slab_peer(lane, d, peers)},
            device_id_type=pl.DeviceIdType.MESH,
        ))
    for copy in shares:
        copy.start()
    gather_ref[lane] = both_ref[...]

    def store(i):
        rows = pl.ds(i * part, part)
        return pltpu.make_async_copy(x_ref.at[rows], out_hbm.at[rows], store_sem.at[i])

    def close(i, carry):
        waves_of = wave_ref[pl.ds(i * part, part)].reshape(part * NX, 2 * plan.width)
        for g in range(pairs):
            full = dot(waves_of, tyi_ref[g])
            for c in range(part):
                for n in range(2):
                    total = full[c * NX : (c + 1) * NX, n * NY : (n + 1) * NY]
                    spot = (i * part + c, 2 * g + n)
                    x_ref[spot] = (total + x_ref[spot].astype(F32)).astype(BF16)
        store(i).start()
        return carry

    edge = stencil(outer, True)

    def spread_edge(i, carry):
        halo_wait_recv(me, slabs, late(i))
        return edge(i, carry)

    def last(i, carry):
        return close(i, spread_edge(i, carry))

    halo_wait_recv(me, slabs, early())
    lax.fori_loop(0, 2 * quarter, spread_edge, 0)
    for copy in fourth:
        copy.wait()
    unfold(recv4)
    lax.fori_loop(0, 2 * quarter, close, 0)
    for copy in shares:
        copy.wait()
    sample_grads(columns, peers, gather_ref, e_ref, grad_ref)
    store_grad = pltpu.make_async_copy(grad_ref, grad_hbm, grad_sem)
    store_grad.start()
    lax.fori_loop(2 * quarter, pieces, last, 0)
    halo_wait_send(me, slabs, early())
    for i in range(pieces):
        halo_wait_send(me, slabs, ahead(i))
        halo_wait_send(me, slabs, late(i))
    store_grad.wait()
    for i in range(pieces):
        store(i).wait()


def layer_call(plan, taps, field, cotangent, weights, grains, bias, point, ty, tx, tyi, txi, zf, zi,
               cell_scale, mode_scale, peers):
    channels, planes = field.shape[:2]
    slabs = plan.slabs
    rows = channels * 2 * plan.jl
    modes = plan.jl * plan.lanes
    columns = 2 * channels * channels // peers
    whole_vmem = pl.BlockSpec(memory_space=pltpu.VMEM)
    anywhere = pl.BlockSpec(memory_space=pl.ANY)
    chunks = channels // 8
    block = pltpu.VMEM((slabs, rows, plan.pk), BF16)
    rim = pltpu.VMEM((channels, NX, NY), BF16)
    wide = pltpu.VMEM((16 * channels, 16 * channels), BF16)
    dma = pltpu.SemaphoreType.DMA
    tyi = tyi.reshape(2 * plan.width, planes // 2, 2 * NY).transpose(1, 0, 2)
    return pl.pallas_call(
        functools.partial(layer_kernel, plan, channels, peers, cell_scale, mode_scale),
        in_specs=[pl.BlockSpec(memory_space=pltpu.SMEM)] * 2 + [anywhere] * 3 + [whole_vmem] * 8,
        out_specs=[anywhere, anywhere],
        out_shape=[
            jax.ShapeDtypeStruct(field.shape, BF16),
            jax.ShapeDtypeStruct((modes, columns), F32),
        ],
        scratch_shapes=[
            pltpu.VMEM(field.shape, BF16),
            pltpu.VMEM(field.shape, BF16),
            pltpu.VMEM(field.shape, BF16),
            pltpu.VMEM((2, channels, channels, modes), BF16),
            rim, rim, rim, rim,
            block, block, block, block, block, block, block, block,
            pltpu.VMEM((channels, NX, 2 * plan.width), BF16),
            wide, wide,
            pltpu.VMEM((2, NX, NY), F32),
            pltpu.VMEM((channels, 8, NY), F32),
            pltpu.VMEM((modes, 2 * channels), BF16),
            pltpu.VMEM((modes, 2 * channels), BF16),
            pltpu.VMEM((modes, 4 * channels), BF16),
            pltpu.VMEM((peers, modes, 4 * channels), BF16),
            pltpu.VMEM((4 * channels, 2 * columns + 256), BF16),
            pltpu.VMEM((modes, columns), F32),
            pltpu.VMEM((4, 12 * NY, 2 * NY), BF16),
            pltpu.VMEM((4, 8, NX + 16, NY), F32),
            pltpu.VMEM((4, 8, NX, NY), BF16),
            pltpu.VMEM((4, 8, NX, NY), BF16),
            pltpu.VMEM((2 * plan.lanes // 128, rows, 128), F32),
            pltpu.VMEM((plan.jl, 2, channels, plan.lanes), F32),
            pltpu.VMEM((plan.jl * channels, 2 * plan.lanes), F32),
            pltpu.VMEM((rows, plan.pw), F32),
            dma((chunks,)), dma, dma((weights.shape[2] // 128,)), dma((channels // 4,)), dma,
            dma((2, 2, channels // 4 + 1)), dma((2, 2, channels // 4 + 1)),
            dma((4, slabs - 1)), dma((4, slabs - 1)),
            dma((peers - 1,)), dma((peers - 1,)),
        ],
        compiler_params=pltpu.CompilerParams(
            vmem_limit_bytes=55 * MIB, collective_id=0, has_side_effects=True),
        name="layer",
    )(taps, bias, field, cotangent, weights, grains, point, ty, tx, tyi, txi, zf, zi)


def hand_on_kernel(chunks, x_hbm, grad_hbm, out_hbm, out_grad_hbm, x_ref, grad_ref, in_sem, out_sem):
    arrays = [(grad_hbm, grad_ref, out_grad_hbm, chunks)]
    size = x_hbm.shape[0] // chunks
    for i in range(chunks):
        rows = pl.ds(i * size, size)
        arrays.append((x_hbm.at[rows], x_ref.at[rows], out_hbm.at[rows], i))
    ins = [pltpu.make_async_copy(src, mid, in_sem.at[n]) for src, mid, _, n in arrays]
    outs = [pltpu.make_async_copy(mid, dst, out_sem.at[n]) for _, mid, dst, n in arrays]
    for copy in ins:
        copy.start()
    for came, goes in zip(ins, outs):
        came.wait()
        goes.start()
    for copy in outs:
        copy.wait()


def hand_on_call(value, grad, chunks=8):
    anywhere = pl.BlockSpec(memory_space=pl.ANY)
    return pl.pallas_call(
        functools.partial(hand_on_kernel, chunks),
        in_specs=[anywhere] * 2,
        out_specs=[anywhere] * 2,
        out_shape=[jax.ShapeDtypeStruct(value.shape, value.dtype), jax.ShapeDtypeStruct(grad.shape, grad.dtype)],
        scratch_shapes=[
            pltpu.VMEM(value.shape, value.dtype),
            pltpu.VMEM(grad.shape, grad.dtype),
            pltpu.SemaphoreType.DMA((chunks + 1,)),
            pltpu.SemaphoreType.DMA((chunks + 1,)),
        ],
        compiler_params=params(62),
        name="hand_on",
    )(value, grad)


def column_picks(channels, columns):
    column = lax.axis_index("dp") * columns + jnp.arange(columns)
    part = column // (channels * channels)
    c = column // channels % channels
    o = column % channels
    index = jnp.arange(2 * channels)[:, None]
    spec_real = (index == c).astype(F32)
    spec_imag = (index == channels + c).astype(F32) * jnp.where(part == 0, 1.0, -1.0)
    dual_same = (index == part * channels + o).astype(F32)
    dual_other = (index == (1 - part) * channels + o).astype(F32)
    return jnp.stack([spec_real, dual_same, spec_imag, dual_other]).astype(BF16)


def local(feats, grains, spec_weight, taps, point_weight, bias, cotangent):
    samples_here, channels, planes = feats.shape[:3]
    assert samples_here == 1
    slabs = lax.axis_size("slab")
    dp = lax.axis_size("dp")
    plan = Plan(planes, slabs)
    mode_rows = spec_weight.shape[0]
    half = lambda t: jnp.asarray(t.astype(jnp.bfloat16))
    ty, tx = half(plan.y_forward), half(plan.x_forward)
    tyi, txi = half(plan.y_inverse), half(plan.x_inverse)
    zf = jnp.asarray(plan.z_forward.astype(np.float32))
    zi = jnp.asarray(plan.z_inverse.astype(np.float32))
    cell_scale = 1.0 / math.sqrt(NX * NY * NZ)
    mode_scale = 1.0 / math.sqrt(KX * KY * KZ)
    jl, kq, kk, groups = plan.jl, plan.kq, plan.kk, plan.groups

    def swap(value):
        return lax.all_to_all(value, "slab", split_axis=0, concat_axis=0, tiled=True)

    def scatter_modes(modes):
        if plan.lead == 1 or kq > 1 or plan.used < plan.width:
            modes = modes[..., : plan.used].reshape(plan.lead, channels, -1, 2 * jl, planes, kq, kk)
            modes = modes.transpose(0, 2, 5, 1, 3, 4, 6)
        return swap(modes.reshape(slabs, channels * 2 * jl, plan.pk))

    def gather_planes(planar):
        planar = swap(planar)
        if plan.lead == 1 or kq > 1 or plan.used < plan.width:
            planar = planar.reshape(plan.lead, groups // plan.lead, kq, channels, 2 * jl, planes, kk)
            planar = planar.transpose(0, 3, 1, 4, 5, 2, 6).reshape(
                plan.lead, channels, 2 * KX // plan.lead, plan.used)
            return jnp.pad(planar, ((0, 0), (0, 0), (0, 0), (0, plan.width - plan.used)))
        return planar.reshape(plan.lead, channels, 2 * KX // plan.lead, plan.width)

    up = [(i, i + 1) for i in range(slabs - 1)]
    down = [(j, i) for i, j in up]
    field = feats[0]
    columns = 2 * channels * channels // dp
    weights = spec_weight.reshape(mode_rows * KZ, 2 * channels * channels)
    fused = (
        mode_rows * KZ == planes * NX and 2 * channels * channels == 128 * channels // 2 and
        plan.lead == slabs and kq == 1 and plan.used == plan.width and planes % 2 == 0 and planes > 4
        and dp > 1 and channels * channels % columns == 0 and columns % 128 == 0
    )
    if fused:
        zfb = half(plan.z_forward.reshape(slabs * plan.pk, 2 * plan.lanes))
        zib = half(plan.z_inverse)
        grad_feats, grad_spec = layer_call(
            plan, taps, field, cotangent[0], weights.reshape(planes, NX, -1), grains[0], bias, point_weight, ty, tx, tyi, txi, zfb, zib,
            cell_scale, mode_scale, dp)
        grad_feats, grad_spec = hand_on_call(grad_feats, grad_spec)
        return grad_feats[None], grad_spec.reshape(mode_rows, KZ, columns)
    weights = weights.T.reshape(2, channels, channels, mode_rows * KZ)
    kp, kt = point_weight, point_weight.T
    pick = column_picks(channels, columns)
    scale = 1.0 / (samples_here * dp)
    pick = pick * jnp.array([scale, 1, scale, 1], BF16)[:, None, None]
    low, high = rims_call(field)
    before = lax.ppermute(high, "slab", up)
    after = lax.ppermute(low, "slab", down)
    received = scatter_modes(planes_call(plan, field, ty, tx))
    smooth = stencil_call(plan, taps, field, (before, after), False)
    received, smooth = lax.optimization_barrier((received, smooth))
    mixed, spec = mix_call(plan, received, weights, zf, zi, False, cell_scale, mode_scale)
    mixed, smooth = lax.optimization_barrier((mixed, smooth))
    modes = gather_planes(mixed)
    smooth = stencil_call(plan, taps, field, (before, after), False, smooth)
    spread, first, last, dual_modes = middle_call(
        plan, grains[0], smooth, cotangent[0], modes, bias, kp, kt, txi, tyi, ty, tx)
    spread_before = lax.ppermute(last, "slab", up)
    spread_after = lax.ppermute(first, "slab", down)
    received = scatter_modes(dual_modes)
    partial = stencil_call(plan, taps, spread, (), True)
    received, partial = lax.optimization_barrier((received, partial))
    back, dual = mix_call(plan, received, weights, zf, zi, True, mode_scale, cell_scale)
    back, partial = lax.optimization_barrier((back, partial))
    back_modes = gather_planes(back)
    partial = stencil_call(plan, taps, spread, (), True, partial)
    both = jnp.concatenate([spec, dual], axis=1)
    both = lax.all_to_all(
        jnp.broadcast_to(both[None], (dp,) + both.shape), "dp", split_axis=0, concat_axis=0, tiled=True)
    grad_spec = grad_call(both, pick)
    grad_feats = final_call(plan, taps, partial, spread_before, spread_after, back_modes, txi, tyi)
    return grad_feats[None], grad_spec.reshape(mode_rows, KZ, columns)


def solution(mesh):
    in_specs = (
        P(("grp", "dp"), None, "slab", None, None),
        P(("grp", "dp"), "slab", None, None),
        P("slab", None, None),
        P(),
        P(),
        P(),
        P(("grp", "dp"), None, "slab", None, None),
    )
    out_specs = (P(("grp", "dp"), None, "slab", None, None), P("slab", "grp", "dp"))
    return jax.shard_map(local, mesh=mesh, in_specs=in_specs, out_specs=out_specs, check_vma=False)
```

```python
import functools
import math

import jax
import jax.numpy as jnp
import numpy as np
from jax import lax
from jax.experimental import pallas as pl
from jax.experimental.pallas import tpu as pltpu
from jax.sharding import PartitionSpec as P

NX = 128
NY = 128
NZ = 32
KX = 16
KY = 16
KZ = 16
F32 = jnp.float32
BF16 = jnp.bfloat16
HIGHEST = lax.Precision.HIGHEST
MIB = 1 << 20


def waves(count, length):
    index = np.arange(count)
    frequency = np.where(index < count // 2, index, length - count + index)
    phases = frequency[:, None] * np.arange(length)[None, :] % length
    angles = phases * (2.0 * math.pi / length)
    return np.cos(angles), np.sin(angles)


class Plan:
    def __init__(self, planes, slabs):
        self.planes = planes
        self.slabs = slabs
        rows = KX * KY // slabs
        self.rows = rows
        self.groups = slabs if rows >= KY else KX
        self.jl = KX // self.groups
        self.kq = slabs // self.groups
        self.kk = KY // self.kq
        self.width = max(128, planes * KY)
        self.used = planes * KY
        self.pk = planes * self.kk
        self.lanes = self.kk * KZ
        self.lead = self.groups if (2 * self.jl) % 8 == 0 else 1
        width, jl = self.width, self.jl
        cos_x, sin_x = waves(KX, NX)
        cos_y, sin_y = waves(KY, NY)
        cos_z, sin_z = waves(KZ, NZ)
        forward = np.zeros((planes, NY, 2, width))
        for z in range(planes):
            forward[z, :, 0, z * KY : (z + 1) * KY] = cos_y.T
            forward[z, :, 1, z * KY : (z + 1) * KY] = -sin_y.T
        forward = forward.reshape(planes * NY, 2 * width)
        self.y_forward = forward
        self.y_inverse = forward.T
        table = np.zeros((self.groups, 2, jl, 2, NX))
        back = np.zeros((2, NX, self.groups, 2, jl))
        for j in range(KX):
            g, i = divmod(j, jl)
            table[g, 0, i, 0], table[g, 0, i, 1] = cos_x[j], sin_x[j]
            table[g, 1, i, 1], table[g, 1, i, 0] = cos_x[j], -sin_x[j]
            back[0, :, g, 0, i], back[0, :, g, 1, i] = cos_x[j], -sin_x[j]
            back[1, :, g, 1, i], back[1, :, g, 0, i] = cos_x[j], sin_x[j]
        self.x_forward = table.reshape(2 * KX, 2 * NX)
        self.x_inverse = back.reshape(2 * NX, 2 * KX)
        kk, pk, lanes = self.kk, self.pk, self.lanes
        zf = np.zeros((slabs, planes, kk, 2, kk, KZ))
        self.pw = max(128, pk)
        zi = np.zeros((slabs, 2, kk, KZ, 2, planes, kk))
        for s in range(slabs):
            for z in range(planes):
                c, n = cos_z[:, s * planes + z], sin_z[:, s * planes + z]
                for k in range(kk):
                    zf[s, z, k, 0, k], zf[s, z, k, 1, k] = c, n
                    zi[s, 0, k, :, 0, z, k], zi[s, 1, k, :, 0, z, k] = c, -n
                    zi[s, 1, k, :, 1, z, k], zi[s, 0, k, :, 1, z, k] = c, n
        self.z_forward = zf.reshape(slabs, pk, 2 * lanes)
        zi = zi.reshape(slabs, 2 * lanes, 2, pk)
        zi = np.pad(zi, ((0, 0), (0, 0), (0, 0), (0, self.pw - pk)))
        self.z_inverse = zi.reshape(slabs, 2 * lanes, 2 * self.pw)


def whole(shape):
    zeros = (0,) * len(shape)
    return pl.BlockSpec(shape, lambda *_: zeros)


def params(mib):
    return pltpu.CompilerParams(vmem_limit_bytes=mib * MIB)


def dot(a, b, **kw):
    return jnp.dot(a, b, preferred_element_type=F32, **kw)


def channel_modes(plan, planes_of, ty, tx):
    field = jnp.concatenate([planes_of(z) for z in range(plan.planes)], axis=1)
    along = dot(field, ty).astype(BF16)
    stacked = jnp.concatenate([along[:, : plan.width], along[:, plan.width :]], axis=0)
    return dot(tx, stacked)


def put_modes(plan, out_ref, c, value):
    if plan.lead == 1:
        out_ref[0, c] = value.astype(BF16)
    else:
        step = 2 * KX // plan.lead
        for g in range(plan.lead):
            out_ref[g, c] = value[g * step : (g + 1) * step].astype(BF16)


def get_modes(plan, ref, c):
    if plan.lead == 1:
        return ref[0, c]
    parts = [ref[g, c].astype(F32) for g in range(plan.lead)]
    return jnp.concatenate(parts, axis=0).astype(BF16)


def planes_kernel(plan, batch, x_ref, ty_ref, tx_ref, out_ref):
    for c in range(batch):
        value = channel_modes(plan, lambda z: x_ref[c, z], ty_ref[...], tx_ref[...])
        put_modes(plan, out_ref, c, value)


def planes_call(plan, field, ty, tx):
    channels, planes = field.shape[:2]
    batch = 4
    step = 2 * KX // plan.lead
    return pl.pallas_call(
        functools.partial(planes_kernel, plan, batch),
        grid=(channels // batch,),
        in_specs=[
            pl.BlockSpec((batch, planes, NX, NY), lambda i: (i, 0, 0, 0)),
            whole(ty.shape),
            whole(tx.shape),
        ],
        out_specs=pl.BlockSpec((plan.lead, batch, step, plan.width), lambda i: (0, i, 0, 0)),
        out_shape=jax.ShapeDtypeStruct((plan.lead, channels, step, plan.width), BF16),
        compiler_params=params(60),
        cost_estimate=pl.CostEstimate(
            flops=2 * channels * NX * planes * NY * 256, bytes_accessed=field.size * 2, transcendentals=0
        ),
        name="plane_modes",
    )(field, ty, tx)


def rims_kernel(low_ref, high_ref, first_ref, last_ref):
    first_ref[...] = low_ref[:, 0]
    last_ref[...] = high_ref[:, 0]


def rims_call(field):
    channels, planes = field.shape[:2]
    batch = 8
    rim = pl.BlockSpec((batch, NX, NY), lambda i: (i, 0, 0))
    shape = jax.ShapeDtypeStruct((channels, NX, NY), field.dtype)
    return pl.pallas_call(
        rims_kernel,
        grid=(channels // batch,),
        in_specs=[
            pl.BlockSpec((batch, 1, NX, NY), lambda i: (i, 0, 0, 0)),
            pl.BlockSpec((batch, 1, NX, NY), lambda i: (i, planes - 1, 0, 0)),
        ],
        out_specs=[rim, rim],
        out_shape=[shape, shape],
        compiler_params=params(60),
        name="rims",
    )(field, field)


def bands(taps_ref, c, adjoint, group, band_ref):
    row = lax.broadcasted_iota(jnp.int32, (NY, NY), 0)
    col = lax.broadcasted_iota(jnp.int32, (NY, NY), 1)
    diff = row - col
    for dz in range(3):
        for dx in range(3):
            base = 9 * dz + 3 * dx
            t = [taps_ref[base + i, c] for i in range(3)]
            if adjoint:
                t = t[::-1]
            band = jnp.where(
                diff == 0,
                t[1],
                jnp.where(diff == 1, t[2], jnp.where(diff == -1, t[0], 0.0)),
            ).astype(BF16)
            zi, xi = (2 - dz, 2 - dx) if adjoint else (dz, dx)
            for z in range(group):
                top = (xi * (group + 2) + z + zi) * NY
                band_ref[top : top + NY, z * NY : (z + 1) * NY] = band


def shifted(plan, x_ref, before_ref, after_ref, c, rows_ref):
    edge = lax.broadcasted_iota(jnp.int32, (NX, NY), 0)
    for i in range(plan.planes + 2):
        if before_ref is None and i in (0, plan.planes + 1):
            continue
        if i == 0:
            plane = before_ref[c]
        elif i == plan.planes + 1:
            plane = after_ref[c]
        else:
            plane = x_ref[c, i - 1]
        wide = plane.astype(F32)
        lower = jnp.where(edge == 0, 0.0, pltpu.roll(wide, 1, 0))
        upper = jnp.where(edge == NX - 1, 0.0, pltpu.roll(wide, NX - 1, 0))
        cols = slice(i * NY, (i + 1) * NY)
        rows_ref[0, :, cols] = lower.astype(BF16)
        rows_ref[1, :, cols] = plane
        rows_ref[2, :, cols] = upper.astype(BF16)


def stencil_kernel(plan, batch, adjoint, group, offset, *refs):
    if offset:
        refs = refs[1:]
    if adjoint:
        taps_ref, x_ref, out_ref, band_ref, rows_ref = refs
        before_ref = after_ref = None
    else:
        taps_ref, x_ref, before_ref, after_ref, out_ref, band_ref, rows_ref = refs

    @pl.when(pl.program_id(0) == 0)
    def _():
        band_ref[...] = jnp.zeros_like(band_ref)
        rows_ref[...] = jnp.zeros_like(rows_ref)

    first = pl.program_id(0) * batch + offset
    for c in range(batch):
        half = c % 2
        band, rows = band_ref.at[half], rows_ref.at[half]
        bands(taps_ref, first + c, adjoint, group, band)
        shifted(plan, x_ref, before_ref, after_ref, c, rows)
        for z in range(0, plan.planes, group):
            cols = slice(z * NY, (z + group + 2) * NY)
            near = jnp.concatenate([rows[d, :, cols] for d in range(3)], axis=1)
            total = dot(near, band[...])
            for i in range(group):
                out_ref[c, z + i] = total[:, i * NY : (i + 1) * NY].astype(BF16)


def stencil_call(plan, taps, field, rims, adjoint, done=None):
    channels, planes = field.shape[:2]
    batch = 4
    group = 2 if planes % 2 == 0 else 1
    offset = 0 if done is None else channels // 2
    skip = offset // batch
    block = pl.BlockSpec((batch, planes, NX, NY), lambda i: (i + skip, 0, 0, 0))
    specs = [pl.BlockSpec(memory_space=pltpu.SMEM), block]
    specs += [pl.BlockSpec((batch, NX, NY), lambda i: (i + skip, 0, 0))] * len(rims)
    operands = (taps, field, *rims)
    if done is not None:
        specs = [pl.BlockSpec(memory_space=pl.ANY)] + specs
        operands = (done,) + operands
    return pl.pallas_call(
        functools.partial(stencil_kernel, plan, batch, adjoint, group, offset),
        grid=(channels // 2 // batch,),
        in_specs=specs,
        out_specs=block,
        out_shape=jax.ShapeDtypeStruct(field.shape, BF16),
        input_output_aliases={} if done is None else {0: 0},
        scratch_shapes=[
            pltpu.VMEM((2, 3 * (group + 2) * NY, group * NY), BF16),
            pltpu.VMEM((2, 3, NX, (planes + 2) * NY), BF16),
        ],
        compiler_params=params(60),
        cost_estimate=pl.CostEstimate(
            flops=field.size * 3 * (group + 2) * NY, bytes_accessed=field.size * 2, transcendentals=0
        ),
        name="stencil_back" if adjoint else "stencil",
    )(*operands)


def final_kernel(plan, batch, taps_ref, x_ref, before_ref, after_ref, m_ref, tx_ref, ty_ref, out_ref):
    first = pl.program_id(0) * batch
    edge = lax.broadcasted_iota(jnp.int32, (NX, NY), 0)
    diff = lax.broadcasted_iota(jnp.int32, (NY, NY), 0) - lax.broadcasted_iota(jnp.int32, (NY, NY), 1)

    def rim(c, plane, dz):
        wide = plane.astype(F32)
        lower = jnp.where(edge == 0, 0.0, pltpu.roll(wide, 1, 0)).astype(BF16)
        upper = jnp.where(edge == NX - 1, 0.0, pltpu.roll(wide, NX - 1, 0)).astype(BF16)
        band = []
        for dx in (2, 1, 0):
            t = [taps_ref[9 * dz + 3 * dx + i, first + c] for i in range(3)]
            band.append(jnp.where(
                diff == 0,
                t[1],
                jnp.where(diff == 1, t[0], jnp.where(diff == -1, t[2], 0.0)),
            ).astype(BF16))
        return dot(jnp.concatenate([lower, plane, upper], axis=1), jnp.concatenate(band, axis=0))

    for c in range(batch):
        wave = dot(tx_ref[...], get_modes(plan, m_ref, c)).astype(BF16)
        wave = jnp.concatenate([wave[:NX], wave[NX:]], axis=1)
        full = dot(wave, ty_ref[...])
        for z in range(plan.planes):
            total = full[:, z * NY : (z + 1) * NY] + x_ref[c, z].astype(F32)
            if z == 0:
                total = total + rim(c, before_ref[c], 2)
            if z == plan.planes - 1:
                total = total + rim(c, after_ref[c], 0)
            out_ref[c, z] = total.astype(BF16)


def final_call(plan, taps, partial, before, after, modes, tx, ty):
    channels, planes = partial.shape[:2]
    batch = 4
    block = pl.BlockSpec((batch, planes, NX, NY), lambda i: (i, 0, 0, 0))
    rim = pl.BlockSpec((batch, NX, NY), lambda i: (i, 0, 0))
    return pl.pallas_call(
        functools.partial(final_kernel, plan, batch),
        grid=(channels // batch,),
        in_specs=[
            pl.BlockSpec(memory_space=pltpu.SMEM),
            block,
            rim,
            rim,
            pl.BlockSpec((modes.shape[0], batch) + modes.shape[2:], lambda i: (0, i, 0, 0)),
            whole(tx.shape),
            whole(ty.shape),
        ],
        out_specs=block,
        out_shape=jax.ShapeDtypeStruct(partial.shape, BF16),
        compiler_params=params(60),
        cost_estimate=pl.CostEstimate(
            flops=2 * partial.size * 512, bytes_accessed=partial.size * 4, transcendentals=0
        ),
        name="final",
    )(taps, partial, before, after, modes, tx, ty)


def mix_kernel(plan, channels, adjoint, scale_in, scale_out, r_ref, zf_ref, zi_ref, w_ref,
               out_ref, turned_ref, z_scr, s_scr, m_scr, o_scr):
    jl, lanes, pk, pw = plan.jl, plan.lanes, plan.pk, plan.pw
    chunks = 2 * lanes // 128
    total = None
    for s in range(plan.slabs):
        part = dot(r_ref[s].astype(F32), zf_ref[s], precision=HIGHEST)
        total = part if total is None else total + part
    total = total * scale_in
    for q in range(chunks):
        z_scr[q] = total[:, q * 128 : (q + 1) * 128]

    def rows_of(start):
        return jnp.concatenate(
            [z_scr[q, pl.ds(start, channels, stride=2 * jl), :] for q in range(chunks)], axis=1)

    for j in range(jl):
        re, im = rows_of(j), rows_of(jl + j)
        real = re[:, :lanes] + im[:, lanes:]
        imag = im[:, :lanes] - re[:, lanes:]
        s_scr[j, 0] = real
        s_scr[j, 1] = imag
        both = jnp.concatenate([real, imag], axis=0)
        turned_ref[j * lanes : (j + 1) * lanes, :] = both.T.astype(BF16)
        cols = slice(j * lanes, (j + 1) * lanes)
        rows = slice(j * channels, (j + 1) * channels)
        if adjoint:
            for c in range(channels):
                wr = w_ref[0, c, :, cols].astype(F32)
                wi = w_ref[1, c, :, cols].astype(F32)
                br = jnp.sum(wr * real + wi * imag, axis=0, keepdims=True)
                bi = jnp.sum(wr * imag - wi * real, axis=0, keepdims=True)
                m_scr[j * channels + c : j * channels + c + 1, :lanes] = br
                m_scr[j * channels + c : j * channels + c + 1, lanes:] = bi
        else:
            mr = jnp.zeros((channels, lanes), F32)
            mi = jnp.zeros((channels, lanes), F32)
            for c in range(channels):
                wr = w_ref[0, c, :, cols].astype(F32)
                wi = w_ref[1, c, :, cols].astype(F32)
                sr = s_scr[j, 0, c : c + 1, :]
                si = s_scr[j, 1, c : c + 1, :]
                mr = mr + (sr * wr - si * wi)
                mi = mi + (sr * wi + si * wr)
            m_scr[rows, :lanes] = mr
            m_scr[rows, lanes:] = mi
    mixed = m_scr[...] * scale_out
    for s in range(plan.slabs):
        planar = dot(mixed, zi_ref[s], precision=HIGHEST)
        for j in range(jl):
            for part in range(2):
                o_scr[pl.ds(part * jl + j, channels, stride=2 * jl), :] = planar[
                    j * channels : (j + 1) * channels, part * pw : (part + 1) * pw
                ]
        out_ref[s] = o_scr[:, :pk].astype(BF16)


def mix_call(plan, received, weights, zf, zi, adjoint, scale_in, scale_out):
    channels = weights.shape[1]
    rows = channels * 2 * plan.jl
    modes = plan.jl * plan.lanes
    return pl.pallas_call(
        functools.partial(mix_kernel, plan, channels, adjoint, scale_in, scale_out),
        out_shape=(
            jax.ShapeDtypeStruct((plan.slabs, rows, plan.pk), BF16),
            jax.ShapeDtypeStruct((modes, 2 * channels), BF16),
        ),
        scratch_shapes=[
            pltpu.VMEM((2 * plan.lanes // 128, rows, 128), F32),
            pltpu.VMEM((plan.jl, 2, channels, plan.lanes), F32),
            pltpu.VMEM((plan.jl * channels, 2 * plan.lanes), F32),
            pltpu.VMEM((rows, plan.pw), F32),
        ],
        compiler_params=params(60),
        name="mix_back" if adjoint else "mix",
    )(received, zf, zi, weights)


def middle_kernel(plan, channels, g_ref, sm_ref, cot_ref, m_ref, bias_ref, pw_ref, pt_ref,
                  txi_ref, tyi_ref, ty_ref, tx_ref,
                  spread_ref, first_ref, last_ref, modes_ref, wave_scr, delta_scr, move_scr, kp_ref, kt_ref):
    z = pl.program_id(0)
    planes = plan.planes
    width = plan.width

    @pl.when(z == 0)
    def _():
        def body(c, carry):
            wave = dot(txi_ref[...], get_modes(plan, m_ref, c)).astype(BF16)
            wave_scr[c, :, :width] = wave[:NX]
            wave_scr[c, :, width:] = wave[NX:]
            return carry
        lax.fori_loop(0, channels, body, 0, unroll=4)
        rows = channels * 16
        pick = lax.broadcasted_iota(jnp.int32, (rows, channels), 0) >> 4
        pick = pick == lax.broadcasted_iota(jnp.int32, (rows, channels), 1)
        pick = jnp.where(pick, 1.0, 0.0).astype(BF16)
        same = lax.broadcasted_iota(jnp.int32, (rows, rows), 0) & 15
        same = same == (lax.broadcasted_iota(jnp.int32, (rows, rows), 1) & 15)
        for src, dst in ((pt_ref, kp_ref), (pw_ref, kt_ref)):
            tall = dot(pick, src[...]).astype(BF16)
            full = lax.dot_general(tall, pick, (((1,), (1,)), ((), ())), preferred_element_type=F32)
            dst[...] = jnp.where(same, full, 0.0).astype(BF16)

    g = g_ref[0]
    row = lax.broadcasted_iota(jnp.int32, (NX, NY), 0)
    col = lax.broadcasted_iota(jnp.int32, (NX, NY), 1)

    def differs(shift, axis, inside):
        return jnp.where((g != pltpu.roll(g, shift, axis)) & inside, 0.25, 0.0)

    move_scr[...] = (
        0.25
        + differs(1, 0, row > 0)
        + differs(NX - 1, 0, row < NX - 1)
        + differs(1, 1, col > 0)
        + differs(NY - 1, 1, col < NY - 1)
    )
    height = channels * 16
    bias = bias_ref[...]

    def body(pair, carry):
        starts = [pair * 32 + 16 * i for i in range(2)]

        def tile(ref):
            return [ref[:, 0, pl.ds(x, 16), :].reshape(height, NY) for x in starts]

        mixed = dot(kp_ref[...], jnp.concatenate(tile(sm_ref), axis=1))
        cot = tile(cot_ref)
        deltas = []
        for i, x in enumerate(starts):
            moving = move_scr[pl.ds(x, 16), :]
            wave = wave_scr[:, pl.ds(x, 16), :].reshape(height, 2 * width)
            spectral = dot(wave, tyi_ref[...])
            local = mixed[:, i * NY : (i + 1) * NY].reshape(channels, 16, NY) * moving[None]
            pre = spectral.reshape(channels, 16, NY) + local + bias
            gate = 0.5 + 0.5 * jnp.tanh(0.5 * pre)
            delta = cot[i].astype(F32).reshape(channels, 16, NY) * gate * (1.0 + pre * (1.0 - gate))
            delta = delta.astype(BF16)
            delta_scr[:, z, pl.ds(x, 16), :] = delta
            deltas.append(delta.reshape(height, NY))
        turned = dot(kt_ref[...], jnp.concatenate(deltas, axis=1))
        for i, x in enumerate(starts):
            moving = move_scr[pl.ds(x, 16), :]
            value = turned[:, i * NY : (i + 1) * NY].reshape(channels, 16, NY) * moving[None]
            spread_ref[:, 0, pl.ds(x, 16), :] = value.astype(BF16)
        return carry

    for pair in range(NX // 32):
        body(pair, 0)

    @pl.when(z == 0)
    def _():
        first_ref[...] = spread_ref[:, 0]

    @pl.when(z == planes - 1)
    def _():
        last_ref[...] = spread_ref[:, 0]

        def body(i, carry):
            for c in (2 * i, 2 * i + 1):
                value = channel_modes(plan, lambda p: delta_scr[c, p], ty_ref[...], tx_ref[...])
                put_modes(plan, modes_ref, c, value)
            return carry

        lax.fori_loop(0, channels // 2, body, 0)


def middle_call(plan, grains, smooth, cotangent, modes, bias, kp, kt, txi, tyi, ty, tx):
    channels, planes = smooth.shape[:2]
    width = plan.width
    block = pl.BlockSpec((channels, 1, NX, NY), lambda z: (0, z, 0, 0))
    rim = jax.ShapeDtypeStruct((channels, NX, NY), BF16)
    return pl.pallas_call(
        functools.partial(middle_kernel, plan, channels),
        grid=(planes,),
        in_specs=[
            pl.BlockSpec((1, NX, NY), lambda z: (z, 0, 0)),
            block,
            block,
            whole(modes.shape),
            whole((channels, 1, 1)),
            whole(kp.shape),
            whole(kt.shape),
            whole(txi.shape),
            pl.BlockSpec((2 * width, NY), lambda z: (0, z)),
            whole(ty.shape),
            whole(tx.shape),
        ],
        out_specs=[block, whole(rim.shape), whole(rim.shape), whole(modes.shape)],
        out_shape=[jax.ShapeDtypeStruct(smooth.shape, BF16), rim, rim,
                   jax.ShapeDtypeStruct(modes.shape, BF16)],
        scratch_shapes=[
            pltpu.VMEM((channels, NX, 2 * width), BF16),
            pltpu.VMEM((channels, planes, NX, NY), BF16),
            pltpu.VMEM((NX, NY), F32),
            pltpu.VMEM((16 * channels, 16 * channels), BF16),
            pltpu.VMEM((16 * channels, 16 * channels), BF16),
        ],
        compiler_params=params(60),
        name="middle",
    )(grains, smooth, cotangent, modes, bias.reshape(channels, 1, 1), kp, kt, txi, tyi, ty, tx)


def grad_kernel(samples, both_ref, e_ref, out_ref):
    total = None
    for i in range(samples):
        half = both_ref.shape[-1] // 2
        spec, dual = both_ref[i, :, :half], both_ref[i, :, half:]
        term = dot(spec, e_ref[0]) * dot(dual, e_ref[1]) + dot(spec, e_ref[2]) * dot(dual, e_ref[3])
        total = term if total is None else total + term
    out_ref[...] = total


def grad_call(both, pick):
    samples, modes, width = both.shape
    columns = pick.shape[-1]
    batch = min(256, modes)
    return pl.pallas_call(
        functools.partial(grad_kernel, samples),
        grid=(modes // batch,),
        in_specs=[
            pl.BlockSpec((samples, batch, width), lambda i: (0, i, 0)),
            whole(pick.shape),
        ],
        out_specs=pl.BlockSpec((batch, columns), lambda i: (i, 0)),
        out_shape=jax.ShapeDtypeStruct((modes, columns), F32),
        compiler_params=params(60),
        cost_estimate=pl.CostEstimate(
            flops=8 * samples * modes * width * columns, bytes_accessed=modes * columns * 4, transcendentals=0
        ),
        name="grad_modes",
    )(both, pick)


def slab_peer(me, d, slabs):
    return lax.rem(me + d, slabs)


def enter(sizes):
    barrier = pltpu.get_barrier_semaphore()
    total = 0
    for axis, size in sizes.items():
        me = lax.axis_index(axis)
        for d in range(1, size):
            pl.semaphore_signal(
                barrier, inc=1, device_id={axis: slab_peer(me, d, size)}, device_id_type=pl.DeviceIdType.MESH)
        total += size - 1
    pl.semaphore_wait(barrier, total)


def exchange(me, slabs, send_ref, recv_ref, send_sem, recv_sem):
    copies = []
    for d in range(1, slabs):
        peer = slab_peer(me, d, slabs)
        copies.append(pltpu.make_async_remote_copy(
            src_ref=send_ref.at[peer],
            dst_ref=recv_ref.at[me],
            send_sem=send_sem.at[d - 1],
            recv_sem=recv_sem.at[d - 1],
            device_id={"slab": peer},
            device_id_type=pl.DeviceIdType.MESH,
        ))
    return copies


def halo_copies(me, slabs, field_ref, before_ref, after_ref, planes, chunk, index, send_sem, recv_sem):
    rows = pl.ds(index * chunk, chunk)
    up = pltpu.make_async_remote_copy(
        src_ref=field_ref.at[rows, planes - 1],
        dst_ref=before_ref.at[rows],
        send_sem=send_sem.at[0, index],
        recv_sem=recv_sem.at[0, index],
        device_id={"slab": lax.rem(me + 1, slabs)},
        device_id_type=pl.DeviceIdType.MESH,
    )
    down = pltpu.make_async_remote_copy(
        src_ref=field_ref.at[rows, 0],
        dst_ref=after_ref.at[rows],
        send_sem=send_sem.at[1, index],
        recv_sem=recv_sem.at[1, index],
        device_id={"slab": lax.rem(me + slabs - 1, slabs)},
        device_id_type=pl.DeviceIdType.MESH,
    )
    return up, down


def halo_start(me, slabs, copies):
    up, down = copies

    @pl.when(me < slabs - 1)
    def _():
        up.start()

    @pl.when(me > 0)
    def _():
        down.start()


def halo_wait_recv(me, slabs, copies):
    up, down = copies

    @pl.when(me > 0)
    def _():
        up.wait_recv()

    @pl.when(me < slabs - 1)
    def _():
        down.wait_recv()


def halo_wait_send(me, slabs, copies):
    up, down = copies

    @pl.when(me < slabs - 1)
    def _():
        up.wait_send()

    @pl.when(me > 0)
    def _():
        down.wait_send()


def batch_modes(plan, out_ref, row, lines, ty_ref, tx_ref):
    count = len(lines)
    along = dot(jnp.concatenate(lines, axis=0), ty_ref[...]).astype(BF16)
    width = plan.width
    values = []
    for c in range(0, count, 2):
        top = along[c * NX : (c + 1) * NX]
        low = along[(c + 1) * NX : (c + 2) * NX]
        pair = jnp.concatenate([
            jnp.concatenate([top[:, :width], low[:, :width]], axis=1),
            jnp.concatenate([top[:, width:], low[:, width:]], axis=1),
        ], axis=0)
        both = dot(tx_ref[...], pair)
        values += [both[:, :width], both[:, width:]]
    step = 2 * KX // plan.lead
    for g in range(plan.lead):
        part = jnp.concatenate([v[g * step : (g + 1) * step] for v in values], axis=0)
        out_ref[g, pl.ds(row, count * step), :] = part.astype(BF16)


def band_masks():
    diff = lax.broadcasted_iota(jnp.int32, (NY, NY), 0) - lax.broadcasted_iota(jnp.int32, (NY, NY), 1)
    return diff == 1, diff == 0, diff == -1


def fill_band(taps_ref, c, adjoint, masks, band_ref):
    low, mid, upp = masks
    for dz in range(3):
        for dx in range(3):
            base = 9 * dz + 3 * dx
            t = [taps_ref[base + i, c] for i in range(3)]
            if adjoint:
                t = t[::-1]
            band = jnp.where(mid, t[1], jnp.where(low, t[2], jnp.where(upp, t[0], 0.0))).astype(BF16)
            zi, xi = (2 - dz, 2 - dx) if adjoint else (dz, dx)
            for z in range(2):
                top = (xi * 4 + z + zi) * NY
                band_ref[top : top + NY, z * NY : (z + 1) * NY] = band


def stencil_part(plan, taps_ref, x_ref, before_ref, after_ref, c, groups, adjoint, masks, out_ref,
                 band_ref, wide_ref, lower_ref, upper_ref):
    fill_band(taps_ref, c, adjoint, masks, band_ref)
    planes = plan.planes

    def plane(i):
        if i == 0:
            return before_ref[c]
        if i == planes + 1:
            return after_ref[c]
        return x_ref[c, i - 1]

    needed = sorted({2 * g + i for g in groups for i in range(4)})
    slot = {i: n for n, i in enumerate(needed)}
    for i in needed:
        n = slot[i]
        wide_ref[n, 8 : NX + 8, :] = plane(i).astype(F32)
        lower_ref[n] = wide_ref[n, 7 : NX + 7, :].astype(BF16)
        upper_ref[n] = wide_ref[n, 9 : NX + 9, :].astype(BF16)

    def moved(dx, i):
        if dx == 1:
            return plane(i)
        return (lower_ref if dx == 0 else upper_ref)[slot[i]]

    near = jnp.concatenate([
        jnp.concatenate([moved(dx, 2 * g + i) for dx in range(3) for i in range(4)], axis=1)
        for g in groups
    ], axis=0)
    total = dot(near, band_ref[...])
    for n, g in enumerate(groups):
        for i in range(2):
            out_ref[c, 2 * g + i] = total[n * NX : (n + 1) * NX, i * NY : (i + 1) * NY].astype(BF16)


def mix_modes(plan, channels, me, adjoint, scale_in, scale_out, own_ref, r_ref, zf_ref, zi_ref, w_ref,
              out_ref, turned_ref, z_scr, s_scr, m_scr, o_scr):
    jl, lanes, pk, pw = plan.jl, plan.lanes, plan.pk, plan.pw
    chunks = 2 * lanes // 128
    r_ref[me] = own_ref[me]
    total = dot(jnp.concatenate([r_ref[s] for s in range(plan.slabs)], axis=1), zf_ref[...])
    total = total * scale_in
    for q in range(chunks):
        z_scr[q] = total[:, q * 128 : (q + 1) * 128]

    def rows_of(start):
        return jnp.concatenate(
            [z_scr[q, pl.ds(start, channels, stride=2 * jl), :] for q in range(chunks)], axis=1)

    for j in range(jl):
        re, im = rows_of(j), rows_of(jl + j)
        real = re[:, :lanes] + im[:, lanes:]
        imag = im[:, :lanes] - re[:, lanes:]
        s_scr[j, 0] = real
        s_scr[j, 1] = imag
        both = jnp.concatenate([real, imag], axis=0)
        turned_ref[j * lanes : (j + 1) * lanes, :] = both.T.astype(BF16)
        cols = slice(j * lanes, (j + 1) * lanes)
        rows = slice(j * channels, (j + 1) * channels)
        if adjoint:
            def body(i, carry):
                parts = []
                for k in range(8):
                    c = 8 * i + k
                    wr = w_ref[0, c, :, cols].astype(F32)
                    wi = w_ref[1, c, :, cols].astype(F32)
                    real, imag = s_scr[j, 0], s_scr[j, 1]
                    br = jnp.sum(wr * real + wi * imag, axis=0, keepdims=True)
                    bi = jnp.sum(wr * imag - wi * real, axis=0, keepdims=True)
                    parts.append(jnp.concatenate([br, bi], axis=1))
                m_scr[pl.ds(pl.multiple_of(j * channels + 8 * i, 8), 8), :] = jnp.concatenate(parts, axis=0)
                return carry
            lax.fori_loop(0, channels // 8, body, 0)
        else:
            def body(i, carry):
                mr, mi = carry
                for k in range(8):
                    c = 8 * i + k
                    wr = w_ref[0, c, :, cols].astype(F32)
                    wi = w_ref[1, c, :, cols].astype(F32)
                    sr = s_scr[j, 0, pl.ds(c, 1), :]
                    si = s_scr[j, 1, pl.ds(c, 1), :]
                    mr = mr + (sr * wr - si * wi)
                    mi = mi + (sr * wi + si * wr)
                return mr, mi
            zero = jnp.zeros((channels, lanes), F32)
            mr, mi = lax.fori_loop(0, channels // 8, body, (zero, zero))
            m_scr[rows, :lanes] = mr
            m_scr[rows, lanes:] = mi
    mixed = (m_scr[...] * scale_out).astype(BF16)
    for s in range(plan.slabs):
        planar = dot(mixed, zi_ref[s])
        for j in range(jl):
            for part in range(2):
                o_scr[pl.ds(part * jl + j, channels, stride=2 * jl), :] = planar[
                    j * channels : (j + 1) * channels, part * pw : (part + 1) * pw
                ]
        out_ref[s] = o_scr[:, :pk].astype(BF16)


def mobility(g_ref, z, move_ref):
    row = lax.broadcasted_iota(jnp.int32, (NX, NY), 0)
    col = lax.broadcasted_iota(jnp.int32, (NX, NY), 1)
    for i in range(2):
        g = g_ref[z + i]

        def differs(shift, axis, inside):
            return jnp.where((g != pltpu.roll(g, shift, axis)) & inside, 0.25, 0.0)

        move_ref[i] = (
            0.25
            + differs(1, 0, row > 0)
            + differs(NX - 1, 0, row < NX - 1)
            + differs(1, 1, col > 0)
            + differs(NY - 1, 1, col < NY - 1)
        )


def spread_weights(channels, src_ref, dst_ref, turned):
    rows = channels * 16
    pick = lax.broadcasted_iota(jnp.int32, (rows, channels), 0) >> 4
    pick = pick == lax.broadcasted_iota(jnp.int32, (rows, channels), 1)
    pick = jnp.where(pick, 1.0, 0.0).astype(BF16)
    same = lax.broadcasted_iota(jnp.int32, (rows, rows), 0) & 15
    same = same == (lax.broadcasted_iota(jnp.int32, (rows, rows), 1) & 15)
    axes = (((1,), (1 if turned else 0,)), ((), ()))
    tall = lax.dot_general(pick, src_ref[...], axes, preferred_element_type=F32).astype(BF16)
    full = lax.dot_general(tall, pick, (((1,), (1,)), ((), ())), preferred_element_type=F32)
    dst_ref[...] = jnp.where(same, full, 0.0).astype(BF16)


def turn_weights(channels, raw_ref, w_ref):
    block = 8 * channels
    per_part = channels // 8
    same = lax.broadcasted_iota(jnp.int32, (block, block), 0) == lax.broadcasted_iota(jnp.int32, (block, block), 1)
    unit = jnp.where(same, 1.0, 0.0).astype(BF16)

    def body(i, carry):
        for part in range(2):
            first = (part * per_part + i) * (block // 128)
            modes = raw_ref.shape[1] * raw_ref.shape[2]
            raw = jnp.concatenate([raw_ref[first + n].reshape(modes, 128) for n in range(block // 128)], axis=1)
            value = lax.dot_general(unit, raw, (((1,), (1,)), ((), ())), preferred_element_type=F32)
            w_ref[part, pl.ds(i * 8, 8)] = value.astype(BF16).reshape(8, channels, value.shape[1])
        return carry

    lax.fori_loop(0, per_part, body, 0)


def sample_picks(channels, columns, lane, samples, e_ref):
    size = 2 * channels
    row = lax.broadcasted_iota(jnp.int32, (size, columns), 0)
    column = lax.broadcasted_iota(jnp.int32, (size, columns), 1) + lane * columns
    part = lane * columns // (channels * channels)
    c = column // channels % channels
    sign = jnp.where(part == 0, 1.0, -1.0) / samples
    e_ref[...] = jnp.zeros_like(e_ref)
    e_ref[:size, :columns] = jnp.where(row == c, 1.0 / samples, 0.0).astype(BF16)
    e_ref[:size, columns : 2 * columns] = jnp.where(row == channels + c, sign, 0.0).astype(BF16)
    row = lax.broadcasted_iota(jnp.int32, (size, 128), 0)
    o = lax.broadcasted_iota(jnp.int32, (size, 128), 1) % channels
    e_ref[size:, 2 * columns : 2 * columns + 128] = jnp.where(row == part * channels + o, 1.0, 0.0).astype(BF16)
    e_ref[size:, 2 * columns + 128 :] = jnp.where(row == (1 - part) * channels + o, 1.0, 0.0).astype(BF16)


def sample_grads(columns, samples, both_ref, e_ref, out_ref):
    modes = both_ref.shape[1]
    batch = 256

    def body(i, carry):
        rows = pl.ds(pl.multiple_of(i * batch, batch), batch)
        totals = [None] * (columns // 128)
        for n in range(samples):
            wide = dot(both_ref[n, rows, :], e_ref[...])
            same = wide[:, 2 * columns : 2 * columns + 128]
            other = wide[:, 2 * columns + 128 :]
            for q in range(len(totals)):
                first = wide[:, q * 128 : (q + 1) * 128]
                second = wide[:, columns + q * 128 : columns + (q + 1) * 128]
                term = first * same + second * other
                totals[q] = term if totals[q] is None else totals[q] + term
        for q, total in enumerate(totals):
            out_ref[rows, q * 128 : (q + 1) * 128] = total
        return carry

    lax.fori_loop(0, modes // batch, body, 0)


def gate_pair(plan, channels, z, g_ref, sm_ref, cot_ref, wave_ref, tyi_ref, kp_ref, kt_ref, bias_ref, move_ref):
    mobility(g_ref, z, move_ref)
    height = channels * 16
    bias = bias_ref[:, 0:1, :]
    for k in range(NX // 16):
        rows = pl.ds(k * 16, 16)

        def tile(ref, n):
            return ref[:, z + n, rows, :].reshape(height, NY)

        mixed = dot(kp_ref[...], jnp.concatenate([tile(sm_ref, 0), tile(sm_ref, 1)], axis=1))
        wave = wave_ref[:, rows, :].reshape(height, 2 * plan.width)
        spectral = dot(wave, tyi_ref[z // 2])
        deltas = []
        for n in range(2):
            cols = slice(n * NY, (n + 1) * NY)
            moving = move_ref[n, rows, :]
            local = mixed[:, cols].reshape(channels, 16, NY) * moving[None]
            pre = spectral[:, cols].reshape(channels, 16, NY) + local + bias
            half = 0.5 * jnp.tanh(0.5 * pre)
            delta = tile(cot_ref, n).astype(F32).reshape(channels, 16, NY) * (0.5 + half) * (1.0 + pre * (0.5 - half))
            delta = delta.astype(BF16)
            cot_ref[:, z + n, rows, :] = delta
            deltas.append(delta.reshape(height, NY))
        turned = dot(kt_ref[...], jnp.concatenate(deltas, axis=1))
        for n in range(2):
            cols = slice(n * NY, (n + 1) * NY)
            value = turned[:, cols].reshape(channels, 16, NY) * move_ref[n, rows, :][None]
            sm_ref[:, z + n, rows, :] = value.astype(BF16)


def pair_waves(plan, read, tx_ref):
    width = plan.width
    pair = jnp.concatenate([
        jnp.concatenate([read(g, k).astype(F32) for g in range(plan.lead)], axis=0) for k in range(2)
    ], axis=1).astype(BF16)
    wave = dot(tx_ref[...], pair).astype(BF16)
    found = []
    for k in range(2):
        cols = slice(k * width, (k + 1) * width)
        found.append(jnp.concatenate([wave[:NX, cols], wave[NX:, cols]], axis=1))
    return found


def layer_kernel(plan, channels, peers, cell_scale, mode_scale,
                 taps_ref, bias_in, x_hbm, cot_hbm, w_hbm, g_ref, pw_ref,
                 ty_ref, tx_ref, tyi_ref, txi_ref, zf_ref, zi_ref,
                 out_hbm, grad_hbm,
                 x_ref, y_ref, cot_ref, w_ref, before_ref, after_ref, before2_ref, after2_ref,
                 send1, recv1, send2, recv2, send3, recv3, send4, recv4,
                 wave_ref, kp_ref, kt_ref, move_ref, bias_ref, spec_ref, dual_ref, both_ref, gather_ref, e_ref, grad_ref,
                 band_ref, wide_ref, lower_ref, upper_ref, z_scr, s_scr, m_scr, o_scr,
                 load_sem, cot_sem, w_sem, store_sem, grad_sem, halo_send, halo_recv, send_sem, recv_sem, both_send, both_recv):
    planes, slabs = plan.planes, plan.slabs
    columns = grad_ref.shape[1]
    me = lax.axis_index("slab")
    lane = lax.axis_index("dp")
    chunk = 8
    chunks = channels // chunk
    step = 2 * KX // plan.lead
    pairs = planes // 2
    inner, outer = list(range(1, pairs - 1)), [0, pairs - 1]

    def load(i):
        rows = pl.ds(i * chunk, chunk)
        return pltpu.make_async_copy(x_hbm.at[rows], x_ref.at[rows], load_sem.at[i])

    for i in range(chunks):
        load(i).start()
    enter({"slab": slabs, "dp": peers})
    halos = [halo_copies(me, slabs, x_hbm, before_ref, after_ref, planes, chunk, i, halo_send.at[0], halo_recv.at[0])
             for i in range(chunks)]
    halo_start(me, slabs, halos[0])
    loads_w = [
        pltpu.make_async_copy(w_hbm.at[:, :, pl.ds(128 * i, 128)], cot_ref.at[i], w_sem.at[i])
        for i in range(w_hbm.shape[2] // 128)
    ]
    for copy in loads_w:
        copy.start()

    @pl.when(me == 0)
    def _():
        before_ref[...] = jnp.zeros_like(before_ref)
        before2_ref[...] = jnp.zeros_like(before2_ref)

    @pl.when(me == slabs - 1)
    def _():
        after_ref[...] = jnp.zeros_like(after_ref)
        after2_ref[...] = jnp.zeros_like(after2_ref)

    band_ref[...] = jnp.zeros_like(band_ref)
    for u in range(chunk):
        for n in range(wide_ref.shape[1]):
            wide_ref[u, n, 0:8, :] = jnp.zeros((8, NY), F32)
            wide_ref[u, n, NX + 8 : NX + 16, :] = jnp.zeros((8, NY), F32)
    for c in range(channels):
        bias_ref[c] = jnp.full((8, NY), bias_in[c], F32)
    spread_weights(channels, pw_ref, kp_ref, True)
    spread_weights(channels, pw_ref, kt_ref, False)
    sample_picks(channels, columns, lane, peers, e_ref)

    def spectra(src_ref, out_ref):
        def body(i, carry):
            if src_ref is x_ref:
                load(i).wait()
            lines = [jnp.concatenate([src_ref[i * chunk + c, z] for z in range(planes)], axis=1) for c in range(chunk)]
            batch_modes(plan, out_ref, pl.multiple_of(i * chunk * step, chunk * step), lines, ty_ref, tx_ref)
            return carry
        lax.fori_loop(0, chunks, body, 0)

    spectra(x_ref, send1)
    first = exchange(me, slabs, send1, recv1, send_sem.at[0], recv_sem.at[0])
    for copy in first:
        copy.start()
    halo_start(me, slabs, halos[1])

    masks = band_masks()

    def stencil(groups, adjoint):
        src, dst = (y_ref, x_ref) if adjoint else (x_ref, y_ref)
        low, high = (before2_ref, after2_ref) if adjoint else (before_ref, after_ref)

        def body(i, carry):
            for u in range(chunk):
                stencil_part(plan, taps_ref, src, low, high, i * chunk + u, groups, adjoint, masks, dst,
                             band_ref.at[u], wide_ref.at[u], lower_ref.at[u], upper_ref.at[u])
            return carry
        return body

    def gates(start, stride):
        def body(i, carry):
            gate_pair(plan, channels, 2 * (start + stride * i), g_ref, y_ref, cot_ref, wave_ref, tyi_ref,
                      kp_ref, kt_ref, bias_ref, move_ref)
            return carry
        return body

    lax.fori_loop(0, chunks, stencil(inner, False), 0)
    for copy in loads_w:
        copy.wait()
    turn_weights(channels, cot_ref, w_ref)
    load_cot = pltpu.make_async_copy(cot_hbm, cot_ref, cot_sem)
    load_cot.start()
    for copy in first:
        copy.wait()
    mix_modes(plan, channels, me, False, cell_scale, mode_scale, send1, recv1, zf_ref, zi_ref, w_ref,
              send2, spec_ref, z_scr, s_scr, m_scr, o_scr)
    second = exchange(me, slabs, send2, recv2, send_sem.at[1], recv_sem.at[1])
    for copy in second:
        copy.start()
    for copies in halos[2:]:
        halo_start(me, slabs, copies)
    recv2[me] = send2[me]
    edge = stencil(outer, False)
    for i in range(2):
        halo_wait_recv(me, slabs, halos[i])
        lax.fori_loop(i, i + 1, edge, 0)
    load_cot.wait()
    for copy in second:
        copy.wait()

    def unfold(src_ref):
        def body(i, carry):
            for k in range(0, 8, 2):
                c = i * 8 + k
                found = pl.ds(pl.multiple_of(c * step, 2 * step), 2 * step)
                for n, wave in enumerate(pair_waves(
                        plan, lambda g, j: src_ref[g, found, :][j * step : (j + 1) * step], txi_ref)):
                    wave_ref[c + n] = wave
            return carry
        lax.fori_loop(0, channels // 8, body, 0)

    unfold(recv2)
    lax.fori_loop(0, pairs - 2, gates(1, 1), 0)
    for i in range(2, chunks):
        halo_wait_recv(me, slabs, halos[i])
        lax.fori_loop(i, i + 1, edge, 0)
    lax.fori_loop(0, 2, gates(0, pairs - 1), 0)

    turns = [halo_copies(me, slabs, y_ref, before2_ref, after2_ref, planes, chunk, i, halo_send.at[1], halo_recv.at[1])
             for i in range(chunks)]
    halo_start(me, slabs, turns[0])
    spectra(cot_ref, send3)
    third = exchange(me, slabs, send3, recv3, send_sem.at[2], recv_sem.at[2])
    for copy in third:
        copy.start()
    halo_start(me, slabs, turns[1])
    lax.fori_loop(0, chunks, stencil(inner, True), 0)
    for copy in third:
        copy.wait()
    mix_modes(plan, channels, me, True, mode_scale, cell_scale, send3, recv3, zf_ref, zi_ref, w_ref,
              send4, dual_ref, z_scr, s_scr, m_scr, o_scr)
    fourth = exchange(me, slabs, send4, recv4, send_sem.at[3], recv_sem.at[3])
    for copy in fourth:
        copy.start()
    for copies in turns[2:]:
        halo_start(me, slabs, copies)
    recv4[me] = send4[me]
    both_ref[...] = jnp.concatenate([spec_ref[...], dual_ref[...]], axis=1)
    shares = []
    for d in range(1, peers):
        shares.append(pltpu.make_async_remote_copy(
            src_ref=both_ref,
            dst_ref=gather_ref.at[lane],
            send_sem=both_send.at[d - 1],
            recv_sem=both_recv.at[d - 1],
            device_id={"dp": slab_peer(lane, d, peers)},
            device_id_type=pl.DeviceIdType.MESH,
        ))
    for copy in shares:
        copy.start()
    gather_ref[lane] = both_ref[...]

    def store(i):
        rows = pl.ds(i * chunk, chunk)
        return pltpu.make_async_copy(x_ref.at[rows], out_hbm.at[rows], store_sem.at[i])

    def close(i):
        waves_of = wave_ref[pl.ds(i * chunk, chunk)].reshape(chunk * NX, 2 * plan.width)
        for g in range(pairs):
            full = dot(waves_of, tyi_ref[g])
            for c in range(chunk):
                for n in range(2):
                    total = full[c * NX : (c + 1) * NX, n * NY : (n + 1) * NY]
                    spot = (i * chunk + c, 2 * g + n)
                    x_ref[spot] = (total + x_ref[spot].astype(F32)).astype(BF16)

    edge = stencil(outer, True)
    for i in range(2):
        halo_wait_recv(me, slabs, turns[i])
        lax.fori_loop(i, i + 1, edge, 0)
    for copy in fourth:
        copy.wait()
    unfold(recv4)
    for i in range(2):
        close(i)
        store(i).start()
    for copy in shares:
        copy.wait()
    sample_grads(columns, peers, gather_ref, e_ref, grad_ref)
    store_grad = pltpu.make_async_copy(grad_ref, grad_hbm, grad_sem)
    store_grad.start()
    for i in range(2, chunks):
        halo_wait_recv(me, slabs, turns[i])
        lax.fori_loop(i, i + 1, edge, 0)
        close(i)
        store(i).start()
    for copies in halos + turns:
        halo_wait_send(me, slabs, copies)
    store_grad.wait()
    for i in range(chunks):
        store(i).wait()


def layer_call(plan, taps, field, cotangent, weights, grains, bias, point, ty, tx, tyi, txi, zf, zi,
               cell_scale, mode_scale, peers):
    channels, planes = field.shape[:2]
    slabs = plan.slabs
    rows = channels * 2 * plan.jl
    modes = plan.jl * plan.lanes
    columns = 2 * channels * channels // peers
    whole_vmem = pl.BlockSpec(memory_space=pltpu.VMEM)
    anywhere = pl.BlockSpec(memory_space=pl.ANY)
    chunks = channels // 8
    block = pltpu.VMEM((slabs, rows, plan.pk), BF16)
    rim = pltpu.VMEM((channels, NX, NY), BF16)
    wide = pltpu.VMEM((16 * channels, 16 * channels), BF16)
    dma = pltpu.SemaphoreType.DMA
    tyi = tyi.reshape(2 * plan.width, planes // 2, 2 * NY).transpose(1, 0, 2)
    return pl.pallas_call(
        functools.partial(layer_kernel, plan, channels, peers, cell_scale, mode_scale),
        in_specs=[pl.BlockSpec(memory_space=pltpu.SMEM)] * 2 + [anywhere] * 3 + [whole_vmem] * 8,
        out_specs=[anywhere, anywhere],
        out_shape=[
            jax.ShapeDtypeStruct(field.shape, BF16),
            jax.ShapeDtypeStruct((modes, columns), F32),
        ],
        scratch_shapes=[
            pltpu.VMEM(field.shape, BF16),
            pltpu.VMEM(field.shape, BF16),
            pltpu.VMEM(field.shape, BF16),
            pltpu.VMEM((2, channels, channels, modes), BF16),
            rim, rim, rim, rim,
            block, block, block, block, block, block, block, block,
            pltpu.VMEM((channels, NX, 2 * plan.width), BF16),
            wide, wide,
            pltpu.VMEM((2, NX, NY), F32),
            pltpu.VMEM((channels, 8, NY), F32),
            pltpu.VMEM((modes, 2 * channels), BF16),
            pltpu.VMEM((modes, 2 * channels), BF16),
            pltpu.VMEM((modes, 4 * channels), BF16),
            pltpu.VMEM((peers, modes, 4 * channels), BF16),
            pltpu.VMEM((4 * channels, 2 * columns + 256), BF16),
            pltpu.VMEM((modes, columns), F32),
            pltpu.VMEM((8, 12 * NY, 2 * NY), BF16),
            pltpu.VMEM((8, 8, NX + 16, NY), F32),
            pltpu.VMEM((8, 8, NX, NY), BF16),
            pltpu.VMEM((8, 8, NX, NY), BF16),
            pltpu.VMEM((2 * plan.lanes // 128, rows, 128), F32),
            pltpu.VMEM((plan.jl, 2, channels, plan.lanes), F32),
            pltpu.VMEM((plan.jl * channels, 2 * plan.lanes), F32),
            pltpu.VMEM((rows, plan.pw), F32),
            dma((chunks,)), dma, dma((weights.shape[2] // 128,)), dma((chunks,)), dma,
            dma((2, 2, chunks)), dma((2, 2, chunks)),
            dma((4, slabs - 1)), dma((4, slabs - 1)),
            dma((peers - 1,)), dma((peers - 1,)),
        ],
        compiler_params=pltpu.CompilerParams(
            vmem_limit_bytes=63 * MIB, collective_id=0, has_side_effects=True),
        name="layer",
    )(taps, bias, field, cotangent, weights, grains, point, ty, tx, tyi, txi, zf, zi)


def hand_on_kernel(chunks, x_hbm, grad_hbm, out_hbm, out_grad_hbm, x_ref, grad_ref, in_sem, out_sem):
    arrays = [(grad_hbm, grad_ref, out_grad_hbm, chunks)]
    size = x_hbm.shape[0] // chunks
    for i in range(chunks):
        rows = pl.ds(i * size, size)
        arrays.append((x_hbm.at[rows], x_ref.at[rows], out_hbm.at[rows], i))
    ins = [pltpu.make_async_copy(src, mid, in_sem.at[n]) for src, mid, _, n in arrays]
    outs = [pltpu.make_async_copy(mid, dst, out_sem.at[n]) for _, mid, dst, n in arrays]
    for copy in ins:
        copy.start()
    for came, goes in zip(ins, outs):
        came.wait()
        goes.start()
    for copy in outs:
        copy.wait()


def hand_on_call(value, grad, chunks=8):
    anywhere = pl.BlockSpec(memory_space=pl.ANY)
    return pl.pallas_call(
        functools.partial(hand_on_kernel, chunks),
        in_specs=[anywhere] * 2,
        out_specs=[anywhere] * 2,
        out_shape=[jax.ShapeDtypeStruct(value.shape, value.dtype), jax.ShapeDtypeStruct(grad.shape, grad.dtype)],
        scratch_shapes=[
            pltpu.VMEM(value.shape, value.dtype),
            pltpu.VMEM(grad.shape, grad.dtype),
            pltpu.SemaphoreType.DMA((chunks + 1,)),
            pltpu.SemaphoreType.DMA((chunks + 1,)),
        ],
        compiler_params=params(62),
        name="hand_on",
    )(value, grad)


def column_picks(channels, columns):
    column = lax.axis_index("dp") * columns + jnp.arange(columns)
    part = column // (channels * channels)
    c = column // channels % channels
    o = column % channels
    index = jnp.arange(2 * channels)[:, None]
    spec_real = (index == c).astype(F32)
    spec_imag = (index == channels + c).astype(F32) * jnp.where(part == 0, 1.0, -1.0)
    dual_same = (index == part * channels + o).astype(F32)
    dual_other = (index == (1 - part) * channels + o).astype(F32)
    return jnp.stack([spec_real, dual_same, spec_imag, dual_other]).astype(BF16)


def local(feats, grains, spec_weight, taps, point_weight, bias, cotangent):
    samples_here, channels, planes = feats.shape[:3]
    assert samples_here == 1
    slabs = lax.axis_size("slab")
    dp = lax.axis_size("dp")
    plan = Plan(planes, slabs)
    mode_rows = spec_weight.shape[0]
    half = lambda t: jnp.asarray(t.astype(jnp.bfloat16))
    ty, tx = half(plan.y_forward), half(plan.x_forward)
    tyi, txi = half(plan.y_inverse), half(plan.x_inverse)
    zf = jnp.asarray(plan.z_forward.astype(np.float32))
    zi = jnp.asarray(plan.z_inverse.astype(np.float32))
    cell_scale = 1.0 / math.sqrt(NX * NY * NZ)
    mode_scale = 1.0 / math.sqrt(KX * KY * KZ)
    jl, kq, kk, groups = plan.jl, plan.kq, plan.kk, plan.groups

    def swap(value):
        return lax.all_to_all(value, "slab", split_axis=0, concat_axis=0, tiled=True)

    def scatter_modes(modes):
        if plan.lead == 1 or kq > 1 or plan.used < plan.width:
            modes = modes[..., : plan.used].reshape(plan.lead, channels, -1, 2 * jl, planes, kq, kk)
            modes = modes.transpose(0, 2, 5, 1, 3, 4, 6)
        return swap(modes.reshape(slabs, channels * 2 * jl, plan.pk))

    def gather_planes(planar):
        planar = swap(planar)
        if plan.lead == 1 or kq > 1 or plan.used < plan.width:
            planar = planar.reshape(plan.lead, groups // plan.lead, kq, channels, 2 * jl, planes, kk)
            planar = planar.transpose(0, 3, 1, 4, 5, 2, 6).reshape(
                plan.lead, channels, 2 * KX // plan.lead, plan.used)
            return jnp.pad(planar, ((0, 0), (0, 0), (0, 0), (0, plan.width - plan.used)))
        return planar.reshape(plan.lead, channels, 2 * KX // plan.lead, plan.width)

    up = [(i, i + 1) for i in range(slabs - 1)]
    down = [(j, i) for i, j in up]
    field = feats[0]
    columns = 2 * channels * channels // dp
    weights = spec_weight.reshape(mode_rows * KZ, 2 * channels * channels)
    fused = (
        mode_rows * KZ == planes * NX and 2 * channels * channels == 128 * channels // 2 and
        plan.lead == slabs and kq == 1 and plan.used == plan.width and planes % 2 == 0 and planes > 4
        and dp > 1 and channels * channels % columns == 0 and columns % 128 == 0
    )
    if fused:
        zfb = half(plan.z_forward.reshape(slabs * plan.pk, 2 * plan.lanes))
        zib = half(plan.z_inverse)
        grad_feats, grad_spec = layer_call(
            plan, taps, field, cotangent[0], weights.reshape(planes, NX, -1), grains[0], bias, point_weight, ty, tx, tyi, txi, zfb, zib,
            cell_scale, mode_scale, dp)
        grad_feats, grad_spec = hand_on_call(grad_feats, grad_spec)
        return grad_feats[None], grad_spec.reshape(mode_rows, KZ, columns)
    weights = weights.T.reshape(2, channels, channels, mode_rows * KZ)
    kp, kt = point_weight, point_weight.T
    pick = column_picks(channels, columns)
    scale = 1.0 / (samples_here * dp)
    pick = pick * jnp.array([scale, 1, scale, 1], BF16)[:, None, None]
    low, high = rims_call(field)
    before = lax.ppermute(high, "slab", up)
    after = lax.ppermute(low, "slab", down)
    received = scatter_modes(planes_call(plan, field, ty, tx))
    smooth = stencil_call(plan, taps, field, (before, after), False)
    received, smooth = lax.optimization_barrier((received, smooth))
    mixed, spec = mix_call(plan, received, weights, zf, zi, False, cell_scale, mode_scale)
    mixed, smooth = lax.optimization_barrier((mixed, smooth))
    modes = gather_planes(mixed)
    smooth = stencil_call(plan, taps, field, (before, after), False, smooth)
    spread, first, last, dual_modes = middle_call(
        plan, grains[0], smooth, cotangent[0], modes, bias, kp, kt, txi, tyi, ty, tx)
    spread_before = lax.ppermute(last, "slab", up)
    spread_after = lax.ppermute(first, "slab", down)
    received = scatter_modes(dual_modes)
    partial = stencil_call(plan, taps, spread, (), True)
    received, partial = lax.optimization_barrier((received, partial))
    back, dual = mix_call(plan, received, weights, zf, zi, True, mode_scale, cell_scale)
    back, partial = lax.optimization_barrier((back, partial))
    back_modes = gather_planes(back)
    partial = stencil_call(plan, taps, spread, (), True, partial)
    both = jnp.concatenate([spec, dual], axis=1)
    both = lax.all_to_all(
        jnp.broadcast_to(both[None], (dp,) + both.shape), "dp", split_axis=0, concat_axis=0, tiled=True)
    grad_spec = grad_call(both, pick)
    grad_feats = final_call(plan, taps, partial, spread_before, spread_after, back_modes, txi, tyi)
    return grad_feats[None], grad_spec.reshape(mode_rows, KZ, columns)


def solution(mesh):
    in_specs = (
        P(("grp", "dp"), None, "slab", None, None),
        P(("grp", "dp"), "slab", None, None),
        P("slab", None, None),
        P(),
        P(),
        P(),
        P(("grp", "dp"), None, "slab", None, None),
    )
    out_specs = (P(("grp", "dp"), None, "slab", None, None), P("slab", "grp", "dp"))
    return jax.shard_map(local, mesh=mesh, in_specs=in_specs, out_specs=out_specs, check_vma=False)
```
